32 devices in a mesh: outer: 4 (over y, x), inner: 2 (over core), mp: 4 (over z).
Axes of the slice: x: 2, y: 2, z: 4, core: 2. Of those that a mesh axis runs over, the one named last changes fastest.
Arguments:
- inputs: bfloat16 [16384, 4096], P(('outer', 'inner'), 'mp'), may hold values from -6 to 6
- log_decay: float32 [64, 16384], P('mp', ('outer', 'inner')), may hold values from -2.5 to 0, as said below
- write_keys: bfloat16 [16384, 128], P(('outer', 'inner')), may hold values from -6 to 6
- read_keys: bfloat16 [16384, 128], P(('outer', 'inner')), may hold values from -0.5 to 0.5
- skip_gain: float32 [64], P('mp'), may hold values from 0.5 to 1.5
- grad_out: bfloat16 [16384, 4096], P(('outer', 'inner'), 'mp'), may hold values from -0.75 to 0.75
Outputs:
- mixed_out: bfloat16 [16384, 4096], P(('outer', 'inner'), 'mp')
- grad_inputs: bfloat16 [16384, 4096], P(('outer', 'inner'), 'mp')
- grad_write: float32 [16384, 128], P(('outer', 'inner', 'mp'))
- grad_read: float32 [16384, 128], P(('outer', 'inner', 'mp'))
The draws below stay inside these ranges and needn't reach their ends.
Inputs may be any that keep to these rules, and one draw needn't show every extreme that they name: `log_decay`: strictly negative.
All inputs are finite; a program needn't handle non-finite values.
Results may differ from the reference program's by a relative error of at most 0.0055.
Values sent between devices are 32-bit elements; how exact they have to be, the bound alone decides.
No kernel may reach another device: no remote copies, remote signals or barrier semaphores. Data moves between devices by JAX's collectives and lax.ppermute only.
A program may use at most 192 MiB of HBM per device.

```python
import jax
import jax.numpy as jnp
from jax import lax

HEAD_COUNT = 64
P_SIZE = 64
N = 128
Q = 256
L_DEV = 2048
SEQUENCE_TOKENS = 16384


def draw_log_decay(key, part):
    sequence_flows = jax.random.split(key, 7)
    fast_share = 0.5
    is_fast = jax.random.bernoulli(sequence_flows[0], fast_share, (HEAD_COUNT, 1))
    fast_rate = 1.0 / jax.random.uniform(sequence_flows[1], (HEAD_COUNT, 1), minval=30.0, maxval=50.0)
    slow_rate = 0.5 / SEQUENCE_TOKENS * jax.random.uniform(sequence_flows[2], (HEAD_COUNT, 1), minval=0.3, maxval=1.0)
    decay_speed = jnp.where(is_fast, fast_rate, slow_rate)
    random_noise = jnp.exp(jax.random.uniform(sequence_flows[3], (HEAD_COUNT, SEQUENCE_TOKENS), minval=-0.7, maxval=0.7))
    device_count = SEQUENCE_TOKENS // L_DEV
    per_processor = jnp.exp(jax.random.uniform(sequence_flows[4], (HEAD_COUNT, device_count), minval=-0.7, maxval=0.7))
    per_processor = jnp.repeat(per_processor, L_DEV, axis=1)
    spike_position = jax.random.randint(sequence_flows[5], (3,), 0, SEQUENCE_TOKENS)
    spike_strength = jax.random.uniform(sequence_flows[6], (HEAD_COUNT, 3), minval=0.2, maxval=0.5)
    token_position = jnp.arange(SEQUENCE_TOKENS)[None, :]
    spike_events = jnp.zeros((HEAD_COUNT, SEQUENCE_TOKENS), jnp.float32)
    for spike_event in range(3):
        spike_events = spike_events + jnp.where(token_position == spike_position[spike_event], jnp.log1p(-spike_strength[:, spike_event:spike_event + 1]), 0.0)
    return (-decay_speed * random_noise * per_processor + spike_events).astype(jnp.float32)


def levels(key, shape, cuts, low, top_value):
    level = 1.0
    for dim, blocks in cuts:
        draws = jax.random.uniform(jax.random.fold_in(jax.random.fold_in(key, 6), dim), (blocks,), jnp.float32, low / len(cuts), top_value / len(cuts))
        level = level * jnp.repeat(jnp.exp(draws), shape[dim] // blocks).reshape((-1,) + (1,) * (len(shape) - 1 - dim))
    return level


def normal_values(stream_key, extent, scale, bound, cuts=(), held_as=jnp.bfloat16):
    level = levels(stream_key, extent, cuts, -0.22, 0.18) if cuts else 1.0
    drawn = jax.random.normal(stream_key, extent, jnp.float32) * scale * level
    return jnp.minimum(jnp.maximum(drawn, -bound), bound).astype(held_as)


def setup_inputs(seed: int = 0) -> dict:
    keys = jax.random.split(jax.random.key(seed), 7)
    inputs = normal_values(keys[0], (SEQUENCE_TOKENS, HEAD_COUNT * P_SIZE), 1.0, 6.0, ((0, 8), (1, 4)))
    log_decay = draw_log_decay(jax.random.fold_in(keys[6], 71), 0)
    write_keys = normal_values(keys[2], (SEQUENCE_TOKENS, N), 1.0, 6.0, ((0, 8),))
    read_keys = normal_values(keys[3], (SEQUENCE_TOKENS, N), N ** -0.5, 0.5, ((0, 8),))
    skip_gain = jnp.clip(0.5 + 1.0 * jax.random.uniform(keys[4], (HEAD_COUNT,), jnp.float32) ** levels(keys[4], (HEAD_COUNT,), ((0, 4),), -0.2, 0.2), 0.5, 1.5)
    grad_out = normal_values(keys[5], (SEQUENCE_TOKENS, HEAD_COUNT * P_SIZE), 0.125, 0.75, ((0, 8), (1, 4)))
    return dict(inputs=inputs, log_decay=log_decay, write_keys=write_keys, read_keys=read_keys, skip_gain=skip_gain, grad_out=grad_out)


def reference(inputs, log_decay, write_keys, read_keys, skip_gain, grad_out):
    hi = lax.Precision.HIGHEST
    count = SEQUENCE_TOKENS // Q
    cumulative = jnp.cumsum(log_decay.reshape(HEAD_COUNT, count, Q), axis=2).transpose(1, 0, 2)
    gain = jnp.sqrt(-jnp.expm1(2.0 * log_decay)).reshape(HEAD_COUNT, count, Q).transpose(1, 2, 0)
    input_blocks = inputs.reshape(count, Q, HEAD_COUNT, P_SIZE)
    grad_blocks = grad_out.reshape(count, Q, HEAD_COUNT, P_SIZE)
    scaled = (input_blocks.astype(jnp.float32) * gain[..., None]).astype(jnp.bfloat16)
    write_blocks = write_keys.reshape(count, Q, N)
    read_blocks = read_keys.reshape(count, Q, N)
    tails = jnp.exp(cumulative[:, :, -1:] - cumulative)
    leads = jnp.exp(cumulative)
    block_decay = jnp.exp(cumulative[:, :, -1])

    def weigh(factor_b, keys_b):
        return (factor_b[:, :, None] * keys_b.astype(jnp.float32)[None]).astype(jnp.bfloat16).astype(jnp.float32)

    def forward_step(state, item):
        decay_b, tail_b, write_b, scaled_b = item
        push = jnp.einsum('hjn,jhp->hnp', weigh(tail_b, write_b), scaled_b.astype(jnp.float32), precision=hi)
        return (decay_b[:, None, None] * state + push, state)

    def backward_step(state, item):
        decay_b, lead_b, read_b, grad_b = item
        pull = jnp.einsum('hkn,khp->hnp', weigh(lead_b, read_b), grad_b.astype(jnp.float32), precision=hi)
        return (decay_b[:, None, None] * state + pull, state)
    zero_state = jnp.zeros((HEAD_COUNT, N, P_SIZE), jnp.float32)
    final_state, entries = lax.scan(forward_step, zero_state, (block_decay, tails, write_blocks, scaled))
    first_state, afters = lax.scan(backward_step, zero_state, (block_decay, leads, read_blocks, grad_blocks), reverse=True)
    lower = jnp.arange(Q)[:, None] >= jnp.arange(Q)[None, :]
    skip_scale = skip_gain[None, :, None]

    def block_terms(item):
        scaled_b, grad_b, write_b, read_b, cum_b, tail_b, lead_b, entry_b, after_b, input_b, gain_b = item
        write_f = write_b.astype(jnp.float32)
        read_f = read_b.astype(jnp.float32)
        scaled_f = scaled_b.astype(jnp.float32)
        grad_f = grad_b.astype(jnp.float32)
        entry_h = entry_b.astype(jnp.bfloat16).astype(jnp.float32)
        after_h = after_b.astype(jnp.bfloat16).astype(jnp.float32)
        tail_write = weigh(tail_b, write_b)
        lead_read = weigh(lead_b, read_b)
        scores = jnp.dot(read_b, write_b.T, preferred_element_type=jnp.float32)
        gaps = jnp.where(lower[None], cum_b[:, :, None] - cum_b[:, None, :], -jnp.inf)
        decay = jnp.exp(gaps)
        mixing = (scores[None] * decay).astype(jnp.bfloat16).astype(jnp.float32)
        out_intra = jnp.einsum('hij,jhp->ihp', mixing, scaled_f, precision=hi)
        back_intra = jnp.einsum('hki,khp->ihp', mixing, grad_f, precision=hi)
        pairs = jnp.einsum('khp,ihp->hki', grad_f, scaled_f, precision=hi)
        paired = (pairs * decay).astype(jnp.bfloat16).astype(jnp.float32)
        write_intra = jnp.einsum('hki,kn->in', paired, read_f, precision=hi)
        read_intra = jnp.einsum('hij,jn->in', paired, write_f, precision=hi)
        out_carry = jnp.einsum('hin,hnp->ihp', lead_read, entry_h, precision=hi)
        back_carry = jnp.einsum('hin,hnp->ihp', tail_write, after_h, precision=hi)
        write_carry = jnp.einsum('hi,ihp,hnp->in', tail_b, scaled_f, after_h, precision=hi)
        read_carry = jnp.einsum('hi,ihp,hnp->in', lead_b, grad_f, entry_h, precision=hi)
        mixed = (out_intra + out_carry + skip_scale * input_b.astype(jnp.float32)).astype(jnp.bfloat16)
        grad_in = (gain_b[..., None] * (back_intra + back_carry) + skip_scale * grad_f).astype(jnp.bfloat16)
        return (mixed, grad_in, write_intra + write_carry, read_intra + read_carry)
    mixed, grad_in, grad_w, grad_r = lax.map(block_terms, (scaled, grad_blocks, write_blocks, read_blocks, cumulative, tails, leads, entries, afters, input_blocks, gain))
    return (mixed.reshape(SEQUENCE_TOKENS, HEAD_COUNT * P_SIZE), grad_in.reshape(SEQUENCE_TOKENS, HEAD_COUNT * P_SIZE), grad_w.reshape(SEQUENCE_TOKENS, N), grad_r.reshape(SEQUENCE_TOKENS, N))
```

```python
import functools

import jax
import jax.numpy as jnp
from jax import lax
from jax.experimental import pallas as pl
from jax.experimental.pallas import tpu as pltpu
from jax.sharding import PartitionSpec as P

WIDTH = 64
BLOCK = 128
TOTALS_BLOCK = 256
GRADS_BLOCK = 256
FAR = -1e30
VMEM_BYTES = 48 * 1024 * 1024
F32 = jnp.float32
BF16 = jnp.bfloat16


def dot(a, b, over_a, over_b):
    return lax.dot_general(a, b, (((over_a,), (over_b,)), ((), ())), preferred_element_type=F32)


def minus_expm1(y):
    series = 1.0 + y * (1.0 / 9.0)
    for k in (8.0, 7.0, 6.0, 5.0, 4.0, 3.0, 2.0):
        series = 1.0 + y * (1.0 / k) * series
    return jnp.where(y > -0.4, -y * series, 1.0 - jnp.exp(y))


def spread_matrix(heads):
    row = lax.broadcasted_iota(jnp.int32, (2 * heads, heads * WIDTH), 0)
    lane = lax.broadcasted_iota(jnp.int32, (2 * heads, heads * WIDTH), 1)
    return jnp.where(lax.rem(row, heads) == lane // WIDTH, 1.0, 0.0).astype(BF16)


def spread(factor, matrix):
    heads = factor.shape[0] // 2
    high = factor.astype(BF16).astype(F32)
    row = lax.broadcasted_iota(jnp.int32, factor.shape, 0)
    parts = jnp.where(row < heads, high, factor - high).astype(BF16)
    return dot(parts, matrix, 0, 0)


def sums(log_decay):
    rows, size = log_decay.shape
    high = log_decay.astype(BF16)
    rest = log_decay - high.astype(F32)
    middle = rest.astype(BF16)
    low = (rest - middle.astype(F32)).astype(BF16)
    source = lax.broadcasted_iota(jnp.int32, (size, 2 * size), 0)
    target = lax.broadcasted_iota(jnp.int32, (size, 2 * size), 1)
    within = jnp.where(
        target < size, jnp.where(source <= target, 1.0, 0.0), jnp.where(source > target - size, 1.0, 0.0)
    ).astype(BF16)
    both = dot(high, within, 1, 0) + dot(middle, within, 1, 0) + dot(low, within, 1, 0)
    return both[:, :size], both[:, size:]


def factors(ld_ref):
    ld = ld_ref[...]
    ld = jnp.concatenate([ld, ld], axis=0)
    gain = jnp.sqrt(minus_expm1(2.0 * ld))
    before, after = sums(ld)
    total = before[:, -1:]
    return gain, before, after, total


def totals_kernel(inputs_ref, grad_ref, ld_ref, write_ref, read_ref, out_ref, push, pull, base):
    step = pl.program_id(0)
    heads = ld_ref.shape[0]
    states = write_ref.shape[1]

    @pl.when(step == 0)
    def _():
        push[...] = jnp.zeros_like(push)
        pull[...] = jnp.zeros_like(pull)
        base[...] = jnp.zeros_like(base)

    matrix = spread_matrix(heads)
    gain, before, after, total = factors(ld_ref)
    start = base[:, :1]
    lead = spread(jnp.exp(start + before), matrix)
    tail = spread(gain * jnp.exp(after), matrix)
    decay = spread(jnp.broadcast_to(jnp.exp(total), (2 * heads, states)), matrix)
    weighted = (lead * grad_ref[...].astype(F32)).astype(BF16)
    pull[...] += dot(read_ref[...], weighted, 0, 0)
    weighted = (tail * inputs_ref[...].astype(F32)).astype(BF16)
    push[...] = push[...] * decay + dot(write_ref[...], weighted, 0, 0)
    base[...] += jnp.broadcast_to(total, base.shape)

    @pl.when(step == pl.num_programs(0) - 1)
    def _():
        out_ref[0:states] = push[...]
        out_ref[states : 2 * states] = pull[...]
        whole = jnp.broadcast_to(jnp.exp(base[:, :1]), (2 * heads, 128))
        out_ref[2 * states :] = spread(whole, matrix)[0:8]


def totals(inputs, grad_out, log_decay, write_keys, read_keys):
    length, lanes = inputs.shape
    heads = log_decay.shape[0]
    states = write_keys.shape[1]
    size = TOTALS_BLOCK
    return pl.pallas_call(
        totals_kernel,
        out_shape=jax.ShapeDtypeStruct((2 * states + 8, lanes), F32),
        grid=(length // size,),
        in_specs=[
            pl.BlockSpec((size, lanes), lambda c: (c, 0)),
            pl.BlockSpec((size, lanes), lambda c: (c, 0)),
            pl.BlockSpec((heads, size), lambda c: (0, c)),
            pl.BlockSpec((size, states), lambda c: (c, 0)),
            pl.BlockSpec((size, states), lambda c: (c, 0)),
        ],
        out_specs=pl.BlockSpec((2 * states + 8, lanes), lambda c: (0, 0)),
        scratch_shapes=[
            pltpu.VMEM((states, lanes), F32),
            pltpu.VMEM((states, lanes), F32),
            pltpu.VMEM((2 * heads, 128), F32),
        ],
        compiler_params=pltpu.CompilerParams(vmem_limit_bytes=VMEM_BYTES),
        cost_estimate=pl.CostEstimate(
            flops=6 * length * lanes * states, bytes_accessed=4 * length * lanes, transcendentals=0
        ),
        name="totals",
    )(inputs, grad_out, log_decay, write_keys, read_keys)


def halves(pair):
    first = lax.broadcasted_iota(jnp.int32, pair.shape, 1) < WIDTH
    zero = jnp.zeros_like(pair)
    return jnp.concatenate([jnp.where(first, pair, zero), jnp.where(first, zero, pair)], axis=0)


def local_kernel(
    inputs_ref,
    grad_ref,
    ld_ref,
    write_ref,
    read_ref,
    inputs_back_ref,
    grad_back_ref,
    ld_back_ref,
    write_back_ref,
    read_back_ref,
    read_terms_ref,
    write_terms_ref,
    lead_ref,
    tail_ref,
    entry,
    after,
    since,
    until,
):
    step = pl.program_id(0)
    count = pl.num_programs(0)
    heads = ld_ref.shape[0]
    states = write_ref.shape[1]

    @pl.when(step == 0)
    def _():
        entry[...] = jnp.zeros_like(entry)
        after[...] = jnp.zeros_like(after)
        since[...] = jnp.ones_like(since)
        until[...] = jnp.ones_like(until)
        write_terms_ref[...] = jnp.zeros_like(write_terms_ref)

    matrix = spread_matrix(heads)
    gain, before, behind, total = factors(ld_ref)
    grad = grad_ref[...]
    inputs = inputs_ref[...].astype(F32)
    led = spread(jnp.exp(before), matrix) * grad.astype(F32)
    lead_ref[...] = (led * since[0:1]).astype(BF16)
    read_terms = dot(led.astype(BF16), entry[...].astype(BF16), 1, 1)
    tailed = (spread(gain * jnp.exp(behind), matrix) * inputs).astype(BF16)
    scaled = (spread(gain, matrix) * inputs).astype(BF16)
    decay = spread(jnp.broadcast_to(jnp.exp(total), (2 * heads, states)), matrix)
    since[...] *= decay[0:8]
    entry[...] = entry[...] * decay + dot(write_ref[...], tailed, 0, 0)
    columns = before.T
    lower = lax.broadcasted_iota(jnp.int32, (BLOCK, BLOCK), 0) >= lax.broadcasted_iota(
        jnp.int32, (BLOCK, BLOCK), 1
    )
    gathered = jnp.zeros((BLOCK, BLOCK), F32)
    for pair in range(heads // 2):
        lanes = slice(pair * 128, pair * 128 + 128)
        products = dot(grad[:, lanes], halves(scaled[:, lanes]), 1, 1)
        for k in range(2):
            head = 2 * pair + k
            gap = columns[:, head : head + 1] - before[head : head + 1, :]
            gathered += products[:, k * BLOCK : k * BLOCK + BLOCK] * jnp.exp(jnp.where(lower, gap, FAR))
    high = gathered.astype(BF16)
    low = (gathered - high.astype(F32)).astype(BF16)
    read_terms_ref[...] = read_terms + dot(high, write_ref[...], 1, 0) + dot(low, write_ref[...], 1, 0)
    at = pl.ds(pl.multiple_of(step * BLOCK, BLOCK), BLOCK)
    write_terms_ref[at, :] += dot(high, read_ref[...], 0, 0) + dot(low, read_ref[...], 0, 0)

    gain, before, behind, total = factors(ld_back_ref)
    tailed = spread(gain * jnp.exp(behind), matrix) * inputs_back_ref[...].astype(F32)
    tail_ref[...] = (tailed * until[0:1]).astype(BF16)
    at = pl.ds(pl.multiple_of((count - 1 - step) * BLOCK, BLOCK), BLOCK)
    write_terms_ref[at, :] += dot(tailed.astype(BF16), after[...].astype(BF16), 1, 1)
    led = (spread(jnp.exp(before), matrix) * grad_back_ref[...].astype(F32)).astype(BF16)
    decay = spread(jnp.broadcast_to(jnp.exp(total), (2 * heads, states)), matrix)
    until[...] *= decay[0:8]
    after[...] = after[...] * decay + dot(read_back_ref[...], led, 0, 0)


def local(inputs, grad_out, log_decay, write_keys, read_keys):
    length, lanes = inputs.shape
    heads = log_decay.shape[0]
    states = write_keys.shape[1]
    count = length // BLOCK

    def specs(at):
        return [
            pl.BlockSpec((BLOCK, lanes), lambda c: (at(c), 0)),
            pl.BlockSpec((BLOCK, lanes), lambda c: (at(c), 0)),
            pl.BlockSpec((heads, BLOCK), lambda c: (0, at(c))),
            pl.BlockSpec((BLOCK, states), lambda c: (at(c), 0)),
            pl.BlockSpec((BLOCK, states), lambda c: (at(c), 0)),
        ]

    operands = (inputs, grad_out, log_decay, write_keys, read_keys)
    return pl.pallas_call(
        local_kernel,
        out_shape=(
            jax.ShapeDtypeStruct((length, states), F32),
            jax.ShapeDtypeStruct((length, states), F32),
            jax.ShapeDtypeStruct((length, lanes), BF16),
            jax.ShapeDtypeStruct((length, lanes), BF16),
        ),
        grid=(count,),
        in_specs=specs(lambda c: c) + specs(lambda c: count - 1 - c),
        out_specs=(
            pl.BlockSpec((BLOCK, states), lambda c: (c, 0)),
            pl.BlockSpec((length, states), lambda c: (0, 0)),
            pl.BlockSpec((BLOCK, lanes), lambda c: (c, 0)),
            pl.BlockSpec((BLOCK, lanes), lambda c: (count - 1 - c, 0)),
        ),
        scratch_shapes=[
            pltpu.VMEM((states, lanes), F32),
            pltpu.VMEM((states, lanes), F32),
            pltpu.VMEM((8, lanes), F32),
            pltpu.VMEM((8, lanes), F32),
        ],
        compiler_params=pltpu.CompilerParams(vmem_limit_bytes=VMEM_BYTES),
        cost_estimate=pl.CostEstimate(
            flops=24 * length * lanes * states, bytes_accessed=12 * length * lanes, transcendentals=0
        ),
        name="local",
    )(*operands, *operands)


def grads_kernel(
    lead_ref, tail_ref, read_terms_ref, write_terms_ref, entry_ref, after_ref, read_ref, write_ref
):
    entry = entry_ref[...].astype(BF16)
    after = after_ref[...].astype(BF16)
    read_ref[...] = read_terms_ref[...] + dot(lead_ref[...], entry, 1, 1)
    write_ref[...] = write_terms_ref[...] + dot(tail_ref[...], after, 1, 1)


def grads(lead, tail, read_terms, write_terms, entry, after):
    length, lanes = lead.shape
    states = entry.shape[0]
    size = GRADS_BLOCK
    wide = pl.BlockSpec((size, lanes), lambda c: (c, 0))
    thin = pl.BlockSpec((size, states), lambda c: (c, 0))
    state = pl.BlockSpec((states, lanes), lambda c: (0, 0))
    shape = jax.ShapeDtypeStruct((length, states), F32)
    return pl.pallas_call(
        grads_kernel,
        out_shape=(shape, shape),
        grid=(length // size,),
        in_specs=[wide, wide, thin, thin, state, state],
        out_specs=(thin, thin),
        compiler_params=pltpu.CompilerParams(vmem_limit_bytes=VMEM_BYTES),
        cost_estimate=pl.CostEstimate(
            flops=4 * length * lanes * states, bytes_accessed=4 * length * lanes, transcendentals=0
        ),
        name="grads",
    )(lead, tail, read_terms, write_terms, entry, after)


def forward_kernel(inputs_ref, ld_ref, write_ref, read_ref, entry_ref, skip_ref, out_ref, entry):
    step = pl.program_id(0)
    heads = ld_ref.shape[0]
    states = write_ref.shape[1]

    @pl.when(step == 0)
    def _():
        entry[...] = entry_ref[...]

    matrix = spread_matrix(heads)
    gain, before, behind, total = factors(ld_ref)
    inputs = inputs_ref[...].astype(F32)
    scaled = (spread(gain, matrix) * inputs).astype(BF16)
    tailed = (spread(gain * jnp.exp(behind), matrix) * inputs).astype(BF16)
    decay = spread(jnp.broadcast_to(jnp.exp(total), (2 * heads, states)), matrix)
    carried = dot(read_ref[...], entry[...].astype(BF16), 1, 0)
    rest = spread(jnp.exp(before), matrix) * carried + skip_ref[0:1] * inputs
    entry[...] = entry[...] * decay + dot(write_ref[...], tailed, 0, 0)
    scores = dot(read_ref[...], write_ref[...], 1, 1)
    columns = before.T
    lower = lax.broadcasted_iota(jnp.int32, (BLOCK, BLOCK), 0) >= lax.broadcasted_iota(
        jnp.int32, (BLOCK, BLOCK), 1
    )
    for pair in range(heads // 2):
        lanes = slice(pair * 128, pair * 128 + 128)
        mixing = []
        for k in range(2):
            head = 2 * pair + k
            gap = columns[:, head : head + 1] - before[head : head + 1, :]
            mixing.append((scores * jnp.exp(jnp.where(lower, gap, FAR))).astype(BF16))
        mixed = dot(jnp.concatenate(mixing, axis=1), halves(scaled[:, lanes]), 1, 0)
        out_ref[:, lanes] = (mixed + rest[:, lanes]).astype(BF16)


def backward_kernel(inputs_ref, ld_ref, write_ref, read_ref, after_ref, skip_ref, out_ref, after):
    step = pl.program_id(0)
    heads = ld_ref.shape[0]
    states = write_ref.shape[1]

    @pl.when(step == 0)
    def _():
        after[...] = after_ref[...]

    matrix = spread_matrix(heads)
    gain, before, behind, total = factors(ld_ref)
    grad = inputs_ref[...]
    grad_wide = grad.astype(F32)
    led = (spread(jnp.exp(before), matrix) * grad_wide).astype(BF16)
    decay = spread(jnp.broadcast_to(jnp.exp(total), (2 * heads, states)), matrix)
    gains = spread(gain, matrix)
    carried = dot(write_ref[...], after[...].astype(BF16), 1, 0)
    rest = spread(gain * jnp.exp(behind), matrix) * carried + skip_ref[0:1] * grad_wide
    after[...] = after[...] * decay + dot(read_ref[...], led, 0, 0)
    scores = dot(write_ref[...], read_ref[...], 1, 1)
    columns = before.T
    upper = lax.broadcasted_iota(jnp.int32, (BLOCK, BLOCK), 0) <= lax.broadcasted_iota(
        jnp.int32, (BLOCK, BLOCK), 1
    )
    for pair in range(heads // 2):
        lanes = slice(pair * 128, pair * 128 + 128)
        mixing = []
        for k in range(2):
            head = 2 * pair + k
            gap = before[head : head + 1, :] - columns[:, head : head + 1]
            mixing.append((scores * jnp.exp(jnp.where(upper, gap, FAR))).astype(BF16))
        mixed = dot(jnp.concatenate(mixing, axis=1), halves(grad[:, lanes]), 1, 0)
        out_ref[:, lanes] = (gains[:, lanes] * mixed + rest[:, lanes]).astype(BF16)


def sweep(kernel, name, reverse, values, log_decay, write_keys, read_keys, state, skip):
    length, lanes = values.shape
    heads = log_decay.shape[0]
    states = write_keys.shape[1]
    count = length // BLOCK

    def at(c):
        return count - 1 - c if reverse else c

    return pl.pallas_call(
        kernel,
        out_shape=jax.ShapeDtypeStruct((length, lanes), BF16),
        grid=(count,),
        in_specs=[
            pl.BlockSpec((BLOCK, lanes), lambda c: (at(c), 0)),
            pl.BlockSpec((heads, BLOCK), lambda c: (0, at(c))),
            pl.BlockSpec((BLOCK, states), lambda c: (at(c), 0)),
            pl.BlockSpec((BLOCK, states), lambda c: (at(c), 0)),
            pl.BlockSpec((states, lanes), lambda c: (0, 0)),
            pl.BlockSpec((8, lanes), lambda c: (0, 0)),
        ],
        out_specs=pl.BlockSpec((BLOCK, lanes), lambda c: (at(c), 0)),
        scratch_shapes=[pltpu.VMEM((states, lanes), F32)],
        compiler_params=pltpu.CompilerParams(vmem_limit_bytes=VMEM_BYTES),
        cost_estimate=pl.CostEstimate(
            flops=16 * length * lanes * states, bytes_accessed=4 * length * lanes, transcendentals=0
        ),
        name=name,
    )(values, log_decay, write_keys, read_keys, state, skip)


def carried_states(summed, states):
    axes = ("outer", "inner")
    devices = lax.axis_size(axes)
    here = lax.axis_index(axes)
    first = lax.rem(here, 2) == 0
    place = here // 2
    part = states // 2
    other = lax.ppermute(summed, axes, [(d, d ^ 1) for d in range(devices)])
    early = jnp.where(first, summed, other)
    late = jnp.where(first, other, summed)
    early_decay = early[2 * states : 2 * states + 1]
    late_decay = late[2 * states : 2 * states + 1]
    row = jnp.where(first, 0, part)

    def mine(x, start):
        return lax.dynamic_slice_in_dim(x, start + row, part, 0)

    push = mine(late, 0) + late_decay * mine(early, 0)
    pull = mine(early, states) + early_decay * mine(late, states)
    decay = jnp.broadcast_to(early_decay * late_decay, (8, summed.shape[1]))
    forth = jnp.concatenate([push, decay], axis=0)
    back = jnp.concatenate([pull, decay], axis=0)
    got = {}
    for m in range(1, devices // 2):
        sent = jnp.where(place < (place ^ m), forth, back)
        got[m] = lax.ppermute(sent, axes, [(d, d ^ (2 * m)) for d in range(devices)])
    entry = jnp.zeros((part, summed.shape[1]), F32)
    after = jnp.zeros((part, summed.shape[1]), F32)
    for m, value in got.items():
        source = place ^ m
        weight = jnp.ones((1, summed.shape[1]), F32)
        for k, between in got.items():
            middle = place ^ k
            inside = ((source < middle) & (middle < place)) | ((place < middle) & (middle < source))
            weight = weight * jnp.where(inside, between[part : part + 1], 1.0)
        term = weight * value[:part]
        entry = entry + jnp.where(source < place, term, 0.0)
        after = after + jnp.where(source > place, term, 0.0)
    own = jnp.concatenate([entry, after], axis=0)
    others = lax.ppermute(own, axes, [(d, d ^ 1) for d in range(devices)])
    top = jnp.where(first, own, others)
    bottom = jnp.where(first, others, own)
    entry = jnp.concatenate([top[:part], bottom[:part]], axis=0)
    after = jnp.concatenate([top[part:], bottom[part:]], axis=0)
    entry = jnp.where(first, entry, early[:states] + early_decay * entry)
    after = jnp.where(first, late[states : 2 * states] + late_decay * after, after)
    return entry, after


def on_device(inputs, log_decay, write_keys, read_keys, skip_gain, grad_out):
    states = write_keys.shape[1]
    skip = jnp.broadcast_to(jnp.repeat(skip_gain, WIDTH)[None], (8, inputs.shape[1]))
    summed = totals(inputs, grad_out, log_decay, write_keys, read_keys)
    read_terms, write_terms, lead, tail = local(inputs, grad_out, log_decay, write_keys, read_keys)
    entry, after = carried_states(summed, states)
    read_terms, write_terms = grads(lead, tail, read_terms, write_terms, entry, after)
    grad_write = lax.psum_scatter(write_terms, "mp", scatter_dimension=0, tiled=True)
    grad_read = lax.psum_scatter(read_terms, "mp", scatter_dimension=0, tiled=True)
    mixed = sweep(
        forward_kernel, "forward", False, inputs, log_decay, write_keys, read_keys, entry, skip
    )
    grad_in = sweep(
        backward_kernel, "backward", True, grad_out, log_decay, write_keys, read_keys, after, skip
    )
    return mixed, grad_in, grad_write, grad_read


def solution(mesh):
    tokens = ("outer", "inner")
    return jax.shard_map(
        on_device,
        mesh=mesh,
        in_specs=(
            P(tokens, "mp"),
            P("mp", tokens),
            P(tokens, None),
            P(tokens, None),
            P("mp"),
            P(tokens, "mp"),
        ),
        out_specs=(
            P(tokens, "mp"),
            P(tokens, "mp"),
            P(("outer", "inner", "mp"), None),
            P(("outer", "inner", "mp"), None),
        ),
        check_vma=False,
    )
```

```python
import functools

import jax
import jax.numpy as jnp
from jax import lax
from jax.experimental import pallas as pl
from jax.experimental.pallas import tpu as pltpu
from jax.sharding import PartitionSpec as P

WIDTH = 64
BLOCK = 128
STEP = 512
GRADS_STEP = 1024
FAR = -1e30
LOG2E = 1.4426950408889634
VMEM_BYTES = 60 * 1024 * 1024
F32 = jnp.float32
BF16 = jnp.bfloat16


def dot(a, b, over_a, over_b):
    return lax.dot_general(a, b, (((over_a,), (over_b,)), ((), ())), preferred_element_type=F32)


def minus_expm1(y):
    series = 1.0 + y * (1.0 / 9.0)
    for k in (8.0, 7.0, 6.0, 5.0, 4.0, 3.0, 2.0):
        series = 1.0 + y * (1.0 / k) * series
    return jnp.where(y > -0.4, -y * series, 1.0 - jnp.exp(y))


def iota(shape, dimension):
    return lax.broadcasted_iota(jnp.int32, shape, dimension)


def spread_matrix(heads, group):
    shape = (128, heads * WIDTH)
    row = iota(shape, 0) - 2 * heads * group
    gap = iota(shape, 1) - WIDTH * jnp.where(row < heads, row, row - heads)
    inside = (row >= 0) & (row < 2 * heads) & (gap >= 0) & (gap < WIDTH)
    return jnp.where(inside, 1.0, 0.0).astype(BF16)


def row_spread_matrix(heads):
    shape = (heads, heads * WIDTH)
    gap = iota(shape, 1) - WIDTH * iota(shape, 0)
    one = jnp.where((gap >= 0) & (gap < WIDTH), 1.0, 0.0)
    return jnp.concatenate([one, one, one], axis=0).astype(BF16)


def three(x):
    high = x.astype(BF16).astype(F32)
    middle = (x - high).astype(BF16).astype(F32)
    return high, middle, x - high - middle


def block_sums(rows):
    shape = (BLOCK, 2 * BLOCK)
    source, target = iota(shape, 0), iota(shape, 1)
    upto = jnp.where(source <= target, 1.0, 0.0)
    beyond = jnp.where(source > target - BLOCK, 1.0, 0.0)
    within = jnp.where(target < BLOCK, upto, beyond).astype(BF16)
    count = rows.shape[0]
    both = dot(jnp.concatenate(three(rows), axis=0).astype(BF16), within, 1, 0)
    both = both[:count] + both[count : 2 * count] + both[2 * count :]
    return both[:, :BLOCK], both[:, BLOCK:]


def stacked(x):
    return jnp.concatenate(
        [x[:, at : at + BLOCK] for at in range(0, x.shape[1], BLOCK)], axis=0
    )


def block_factors(ld_ref):
    ld = ld_ref[...]
    gain = stacked(jnp.sqrt(minus_expm1(2.0 * ld)))
    before, behind = block_sums(stacked(ld))
    return gain, before, behind


def in_columns(groups, heads, block):
    parts = []
    for factor in groups:
        rows = factor[block * heads : block * heads + heads]
        high = rows.astype(BF16).astype(F32)
        parts += [high, rows - high]
    parts.append(jnp.zeros((128 - 2 * heads * len(groups), BLOCK), F32))
    rows = jnp.concatenate(parts, axis=0).astype(BF16)
    eye = jnp.where(iota((BLOCK, BLOCK), 0) == iota((BLOCK, BLOCK), 1), 1.0, 0.0).astype(BF16)
    return dot(eye, rows, 1, 1).astype(BF16)


def totals_kernel(
    inputs_ref, grad_ref, ld_ref, write_ref, read_ref, out_ref, lead_ref, tail_ref, parts, lanes_of
):
    step = pl.program_id(0)
    heads = ld_ref.shape[0]
    states = write_ref.shape[1]
    count = ld_ref.shape[1] // BLOCK

    @pl.when(step == 0)
    def _():
        lanes_of[0] = spread_matrix(heads, 0)
        lanes_of[1] = spread_matrix(heads, 1)
        gain, before, behind = block_factors(ld_ref)
        totals = [before[c * heads : c * heads + heads, BLOCK - 1 :] for c in range(count)]
        start = [jnp.zeros((heads, 1), F32)]
        for total in totals:
            start.append(start[-1] + total)
        end = [jnp.zeros((heads, 1), F32)]
        for total in totals[::-1]:
            end.append(end[-1] + total)
        since = jnp.concatenate(start[:count], axis=0)
        until = jnp.concatenate(end[:count][::-1], axis=0)
        lead = jnp.exp(since + before)
        tail = gain * jnp.exp(until + behind)
        for c in range(count):
            parts[c * BLOCK : c * BLOCK + BLOCK] = in_columns((lead, tail), heads, c)
        out_ref[...] = jnp.zeros_like(out_ref)
        whole = jnp.concatenate(three(jnp.exp(start[count])), axis=0)
        whole = jnp.broadcast_to(whole, (3 * heads, 128)).astype(BF16)
        out_ref[2 * states :] = dot(whole, row_spread_matrix(heads), 0, 0)[0:8]

    at = pl.ds(pl.multiple_of(step * STEP, STEP), STEP)
    here = parts[at, :]
    lead = (dot(here, lanes_of[0], 1, 0) * grad_ref[...].astype(F32)).astype(BF16)
    lead_ref[...] = lead
    out_ref[states : 2 * states] += dot(read_ref[at, :], lead, 0, 0)
    tail = (dot(here, lanes_of[1], 1, 0) * inputs_ref[...].astype(F32)).astype(BF16)
    tail_ref[...] = tail
    out_ref[0:states] += dot(write_ref[at, :], tail, 0, 0)


def totals(inputs, grad_out, log_decay, write_keys, read_keys):
    length, lanes = inputs.shape
    heads = log_decay.shape[0]
    states = write_keys.shape[1]
    wide = pl.BlockSpec((STEP, lanes), lambda c: (c, 0))
    keys = pl.BlockSpec((length, states), lambda c: (0, 0))
    return pl.pallas_call(
        totals_kernel,
        out_shape=(
            jax.ShapeDtypeStruct((2 * states + 8, lanes), F32),
            jax.ShapeDtypeStruct((length, lanes), BF16),
            jax.ShapeDtypeStruct((length, lanes), BF16),
        ),
        grid=(length // STEP,),
        in_specs=[wide, wide, pl.BlockSpec((heads, length), lambda c: (0, 0)), keys, keys],
        out_specs=(pl.BlockSpec((2 * states + 8, lanes), lambda c: (0, 0)), wide, wide),
        scratch_shapes=[
            pltpu.VMEM((length, 128), BF16),
            pltpu.VMEM((2, 128, lanes), BF16),
        ],
        compiler_params=pltpu.CompilerParams(vmem_limit_bytes=VMEM_BYTES),
        cost_estimate=pl.CostEstimate(
            flops=6 * length * lanes * states, bytes_accessed=8 * length * lanes, transcendentals=0
        ),
        name="totals",
    )(inputs, grad_out, log_decay, write_keys, read_keys)


def halves(pair):
    first = iota(pair.shape, 1) < WIDTH
    zero = jnp.zeros_like(pair)
    return jnp.concatenate([jnp.where(first, pair, zero), jnp.where(first, zero, pair)], axis=0)


def lower_block():
    return iota((BLOCK, BLOCK), 0) >= iota((BLOCK, BLOCK), 1)


def local_kernel(
    inputs_ref,
    grad_ref,
    ld_ref,
    write_ref,
    read_ref,
    read_terms_ref,
    write_terms_ref,
    entries_ref,
    afters_ref,
    parts_ref,
    rows_ref,
    columns_ref,
    ranges_ref,
    entry,
    after,
    decays,
    leads,
    tails,
    lanes_of,
):
    step = pl.program_id(0)
    heads = ld_ref.shape[0]
    length = ld_ref.shape[1]
    states = write_ref.shape[1]
    count = length // BLOCK
    steps = length // STEP
    inner = STEP // BLOCK

    @pl.when(step == 0)
    def _():
        for k in range(3):
            lanes_of[k] = spread_matrix(heads, k)
        gain, before, behind = block_factors(ld_ref)
        lead = jnp.exp(before)
        tail = gain * jnp.exp(behind)
        matrix = row_spread_matrix(heads)
        powers = before * LOG2E
        rows_ref[...] = powers
        lasts = []
        for c in range(count):
            at = slice(c * BLOCK, c * BLOCK + BLOCK)
            mine = slice(c * heads, c * heads + heads)
            parts_ref[at] = in_columns((lead, tail, gain), heads, c)
            columns_ref[at] = powers[mine].T
            lasts.append(lead[mine, BLOCK - 1 :])
        last = jnp.concatenate(lasts, axis=1)
        decays[...] = dot(jnp.concatenate(three(last), axis=0).astype(BF16), matrix, 0, 0)
        ones = jnp.ones((1, heads * WIDTH), F32)
        since, until = [ones], [ones]
        for c in range(count - 1):
            since.append(since[-1] * decays[c : c + 1])
            until.append(until[-1] * decays[count - 1 - c : count - c])
        ranges_ref[:count] = jnp.concatenate(since, axis=0)
        ranges_ref[count:] = jnp.concatenate(until[::-1], axis=0)
        entry[...] = jnp.zeros_like(entry)
        after[...] = jnp.zeros_like(after)

    @pl.when(step < steps)
    def _():
        for k in range(inner):
            inside = slice(k * BLOCK, k * BLOCK + BLOCK)
            block = step * inner + k
            at = pl.ds(pl.multiple_of(block * BLOCK, BLOCK), BLOCK)
            here = parts_ref[at, :]
            write, read = write_ref[at, :], read_ref[at, :]
            grad = grad_ref[inside]
            inputs = inputs_ref[inside].astype(F32)
            lead = (dot(here, lanes_of[0], 1, 0) * grad.astype(F32)).astype(BF16)
            tail = (dot(here, lanes_of[1], 1, 0) * inputs).astype(BF16)
            scaled = (dot(here, lanes_of[2], 1, 0) * inputs).astype(BF16)
            leads[at, :] = lead
            tails[at, :] = tail
            state = entry[...]
            held = state.astype(BF16)
            entries_ref[inside] = held
            entry[...] = state * decays[pl.ds(block, 1), :] + dot(write, tail, 0, 0)
            rows = rows_ref[pl.ds(pl.multiple_of(block * heads, heads), heads), :]
            columns = columns_ref[at, :]
            lower = lower_block()
            gathered = jnp.zeros((BLOCK, BLOCK), F32)
            for pair in range(heads // 2):
                lanes = slice(pair * 128, pair * 128 + 128)
                products = dot(grad[:, lanes], halves(scaled[:, lanes]), 1, 1)
                for j in range(2):
                    head = 2 * pair + j
                    gap = columns[:, head : head + 1] - rows[head : head + 1, :]
                    gathered += products[:, j * BLOCK : j * BLOCK + BLOCK] * jnp.exp2(
                        jnp.where(lower, gap, FAR)
                    )
            high = gathered.astype(BF16)
            low = (gathered - high.astype(F32)).astype(BF16)
            read_terms_ref[inside] = dot(lead, held, 1, 1) + dot(high, write, 1, 0) + dot(low, write, 1, 0)
            write_terms_ref[at, :] = dot(high, read, 0, 0) + dot(low, read, 0, 0)

    @pl.when(step >= steps)
    def _():
        for k in reversed(range(inner)):
            inside = slice(k * BLOCK, k * BLOCK + BLOCK)
            block = (2 * steps - 1 - step) * inner + k
            at = pl.ds(pl.multiple_of(block * BLOCK, BLOCK), BLOCK)
            state = after[...]
            held = state.astype(BF16)
            afters_ref[inside] = held
            after[...] = state * decays[pl.ds(block, 1), :] + dot(read_ref[at, :], leads[at, :], 0, 0)
            write_terms_ref[at, :] += dot(tails[at, :], held, 1, 1)


def local(inputs, grad_out, log_decay, write_keys, read_keys):
    length, lanes = inputs.shape
    heads = log_decay.shape[0]
    states = write_keys.shape[1]
    assert states == BLOCK and 6 * heads <= 128
    count = length // BLOCK
    steps = length // STEP

    def forth(c):
        return jnp.minimum(c, steps - 1)

    def back(c):
        return jnp.minimum(2 * steps - 1 - c, steps - 1)

    def whole(*shape):
        return pl.BlockSpec(shape, lambda c: (0, 0))

    return pl.pallas_call(
        local_kernel,
        out_shape=(
            jax.ShapeDtypeStruct((length, states), F32),
            jax.ShapeDtypeStruct((length, states), F32),
            jax.ShapeDtypeStruct((length, lanes), BF16),
            jax.ShapeDtypeStruct((length, lanes), BF16),
            jax.ShapeDtypeStruct((length, 128), BF16),
            jax.ShapeDtypeStruct((count * heads, BLOCK), F32),
            jax.ShapeDtypeStruct((length, heads), F32),
            jax.ShapeDtypeStruct((2 * count, lanes), F32),
        ),
        grid=(2 * steps,),
        in_specs=[
            pl.BlockSpec((STEP, lanes), lambda c: (forth(c), 0)),
            pl.BlockSpec((STEP, lanes), lambda c: (forth(c), 0)),
            whole(heads, length),
            whole(length, states),
            whole(length, states),
        ],
        out_specs=(
            pl.BlockSpec((STEP, states), lambda c: (forth(c), 0)),
            whole(length, states),
            pl.BlockSpec((STEP, lanes), lambda c: (forth(c), 0)),
            pl.BlockSpec((STEP, lanes), lambda c: (back(c), 0)),
            whole(length, 128),
            whole(count * heads, BLOCK),
            whole(length, heads),
            whole(2 * count, lanes),
        ),
        scratch_shapes=[
            pltpu.VMEM((states, lanes), F32),
            pltpu.VMEM((states, lanes), F32),
            pltpu.VMEM((count, lanes), F32),
            pltpu.VMEM((length, lanes), BF16),
            pltpu.VMEM((length, lanes), BF16),
            pltpu.VMEM((3, 128, lanes), BF16),
        ],
        compiler_params=pltpu.CompilerParams(vmem_limit_bytes=VMEM_BYTES),
        cost_estimate=pl.CostEstimate(
            flops=24 * length * lanes * states, bytes_accessed=8 * length * lanes, transcendentals=0
        ),
        name="local",
    )(inputs, grad_out, log_decay, write_keys, read_keys)


def grads_kernel(
    lead_ref, tail_ref, read_terms_ref, write_terms_ref, entry_ref, after_ref, out_ref
):
    states = entry_ref.shape[0]
    entry = entry_ref[...].astype(BF16)
    after = after_ref[...].astype(BF16)
    out_ref[:, :states] = read_terms_ref[...] + dot(lead_ref[...], entry, 1, 1)
    out_ref[:, states:] = write_terms_ref[...] + dot(tail_ref[...], after, 1, 1)


def grads(lead, tail, read_terms, write_terms, entry, after):
    length, lanes = lead.shape
    states = entry.shape[0]
    size = GRADS_STEP
    wide = pl.BlockSpec((size, lanes), lambda c: (c, 0))
    thin = pl.BlockSpec((size, states), lambda c: (c, 0))
    state = pl.BlockSpec((states, lanes), lambda c: (0, 0))
    return pl.pallas_call(
        grads_kernel,
        out_shape=jax.ShapeDtypeStruct((length, 2 * states), F32),
        grid=(length // size,),
        in_specs=[wide, wide, thin, thin, state, state],
        out_specs=pl.BlockSpec((size, 2 * states), lambda c: (c, 0)),
        compiler_params=pltpu.CompilerParams(vmem_limit_bytes=VMEM_BYTES),
        cost_estimate=pl.CostEstimate(
            flops=4 * length * lanes * states, bytes_accessed=4 * length * lanes, transcendentals=0
        ),
        name="grads",
    )(lead, tail, read_terms, write_terms, entry, after)


def outputs_kernel(
    first,
    inputs_ref,
    grad_ref,
    write_ref,
    read_ref,
    entries_ref,
    afters_ref,
    parts_ref,
    rows_ref,
    columns_ref,
    ranges_ref,
    entry_ref,
    after_ref,
    skip_ref,
    *rest,
):
    mixed_ref, grad_in_ref, lanes_of = rest[-3:]
    step = pl.program_id(0)
    heads = skip_ref.shape[1] // WIDTH
    count = ranges_ref.shape[0] // 2
    inner = STEP // BLOCK

    @pl.when(step == 0)
    def _():
        for k in range(3):
            lanes_of[k] = spread_matrix(heads, k)

    for k in range(inner):
        at = slice(k * BLOCK, k * BLOCK + BLOCK)
        block = (first + step) * inner + k
        here = parts_ref[at, :]
        write, read = write_ref[at, :], read_ref[at, :]
        grad = grad_ref[at]
        inputs = inputs_ref[at].astype(F32)
        gains = dot(here, lanes_of[2], 1, 0)
        scaled = (gains * inputs).astype(BF16)
        entry = entries_ref[at].astype(F32) + ranges_ref[pl.ds(block, 1), :] * entry_ref[...]
        after = afters_ref[at].astype(F32) + ranges_ref[pl.ds(count + block, 1), :] * after_ref[...]
        skip = skip_ref[0:1]
        out_rest = dot(here, lanes_of[0], 1, 0) * dot(read, entry.astype(BF16), 1, 0) + skip * inputs
        back_rest = dot(here, lanes_of[1], 1, 0) * dot(write, after.astype(BF16), 1, 0)
        back_rest = back_rest + skip * grad.astype(F32)
        scores = dot(read, write, 1, 1)
        rows = rows_ref[k * heads : k * heads + heads, :]
        columns = columns_ref[at, :]
        lower = lower_block()
        for pair in range(heads // 2):
            lanes = slice(pair * 128, pair * 128 + 128)
            mixing = []
            for j in range(2):
                head = 2 * pair + j
                gap = columns[:, head : head + 1] - rows[head : head + 1, :]
                mixing.append((scores * jnp.exp2(jnp.where(lower, gap, FAR))).astype(BF16))
            mixed = dot(jnp.concatenate(mixing, axis=1), halves(scaled[:, lanes]), 1, 0)
            mixed_ref[at, lanes] = (mixed + out_rest[:, lanes]).astype(BF16)
            back = dot(jnp.concatenate(mixing, axis=0), halves(grad[:, lanes]), 0, 0)
            grad_in_ref[at, lanes] = (gains[:, lanes] * back + back_rest[:, lanes]).astype(BF16)


def outputs(first, steps, earlier, inputs, grad_out, write_keys, read_keys, made, entry, after, skip):
    length, lanes = inputs.shape
    states = write_keys.shape[1]
    entries, afters, parts, rows, columns, ranges = made
    heads = columns.shape[1]

    def tokens(size, width):
        return pl.BlockSpec((size, width), lambda c: (first + c, 0))

    def whole(x):
        return pl.BlockSpec(x.shape, lambda c: (0, 0))

    wide = tokens(STEP, lanes)
    shape = jax.ShapeDtypeStruct((length, lanes), BF16)
    return pl.pallas_call(
        functools.partial(outputs_kernel, first),
        out_shape=(shape, shape),
        grid=(steps,),
        in_specs=[
            wide,
            wide,
            tokens(STEP, states),
            tokens(STEP, states),
            wide,
            wide,
            tokens(STEP, 128),
            tokens(STEP // BLOCK * heads, BLOCK),
            tokens(STEP, heads),
            whole(ranges),
            whole(entry),
            whole(after),
            whole(skip),
            *[pl.BlockSpec(memory_space=pl.ANY) for _ in earlier],
        ],
        out_specs=(wide, wide),
        input_output_aliases={13 + k: k for k in range(len(earlier))},
        scratch_shapes=[pltpu.VMEM((3, 128, lanes), BF16)],
        compiler_params=pltpu.CompilerParams(vmem_limit_bytes=VMEM_BYTES),
        cost_estimate=pl.CostEstimate(
            flops=16 * steps * STEP * lanes * states,
            bytes_accessed=12 * steps * STEP * lanes,
            transcendentals=0,
        ),
        name="outputs",
    )(
        inputs, grad_out, write_keys, read_keys, entries, afters, parts, rows, columns, ranges,
        entry, after, skip, *earlier,
    )


def carried_states(summed, states, beside):
    axes = ("outer", "inner")
    devices = lax.axis_size(axes)
    here = lax.axis_index(axes)
    first = lax.rem(here, 2) == 0
    place = here // 2
    part = states // 2
    other = lax.ppermute(summed, axes, [(d, d ^ 1) for d in range(devices)])
    early = jnp.where(first, summed, other)
    late = jnp.where(first, other, summed)
    early_decay = early[2 * states : 2 * states + 1]
    late_decay = late[2 * states : 2 * states + 1]
    row = jnp.where(first, 0, part)

    def mine(x, start):
        return lax.dynamic_slice_in_dim(x, start + row, part, 0)

    push = mine(late, 0) + late_decay * mine(early, 0)
    pull = mine(early, states) + early_decay * mine(late, states)
    decay = jnp.broadcast_to(early_decay * late_decay, (8, summed.shape[1]))
    forth = jnp.concatenate([push, decay], axis=0)
    back = jnp.concatenate([pull, decay], axis=0)
    got = {}
    for m in range(1, devices // 2):
        sent = jnp.where(place < (place ^ m), forth, back)
        got[m] = lax.ppermute(sent, axes, [(d, d ^ (2 * m)) for d in range(devices)])
    got, made = beside(got)
    entry = jnp.zeros((part, summed.shape[1]), F32)
    after = jnp.zeros((part, summed.shape[1]), F32)
    for m, value in got.items():
        source = place ^ m
        weight = jnp.ones((1, summed.shape[1]), F32)
        for k, between in got.items():
            middle = place ^ k
            inside = ((source < middle) & (middle < place)) | ((place < middle) & (middle < source))
            weight = weight * jnp.where(inside, between[part : part + 1], 1.0)
        term = weight * value[:part]
        entry = entry + jnp.where(source < place, term, 0.0)
        after = after + jnp.where(source > place, term, 0.0)
    own = jnp.concatenate([entry, after], axis=0)
    others = lax.ppermute(own, axes, [(d, d ^ 1) for d in range(devices)])
    top = jnp.where(first, own, others)
    bottom = jnp.where(first, others, own)
    entry = jnp.concatenate([top[:part], bottom[:part]], axis=0)
    after = jnp.concatenate([top[part:], bottom[part:]], axis=0)
    entry = jnp.where(first, entry, early[:states] + early_decay * entry)
    after = jnp.where(first, late[states : 2 * states] + late_decay * after, after)
    return entry, after, made


def head_sum(terms, between):
    rows = terms.shape[0] // 4
    at = lax.axis_index("mp")

    def quarter(k):
        return lax.dynamic_slice_in_dim(terms, k * rows, rows, 0)

    def pick(even_half):
        return jnp.where(at < 2, even_half[0], even_half[1])

    to_far = jnp.where(lax.rem(at, 2) == 0, 3, 0)
    far = lax.ppermute(quarter(to_far), "mp", [(0, 1), (1, 0), (2, 3), (3, 2)])
    crossed = lax.ppermute(quarter(pick((2, 1))), "mp", [(1, 2), (2, 1)])
    done, (far, crossed, terms) = between(far, crossed, terms)
    onward = quarter(pick((3, 0))) + far
    last = lax.ppermute(onward, "mp", [(1, 3), (2, 0)])
    two_away = lax.ppermute(quarter(pick((2, 1))), "mp", [(0, 2), (3, 1)])
    near = lax.ppermute(quarter(pick((1, 2))), "mp", [(0, 1), (3, 2)])
    end = (at == 0) | (at == 3)
    own = quarter(at) + jnp.where(end, far, 0.0)
    return done, own, (crossed, two_away, near, last)


def on_device(inputs, log_decay, write_keys, read_keys, skip_gain, grad_out):
    states = write_keys.shape[1]
    steps = inputs.shape[0] // STEP
    skip = jnp.broadcast_to(jnp.repeat(skip_gain, WIDTH)[None], (8, inputs.shape[1]))
    summed, lead, tail = totals(inputs, grad_out, log_decay, write_keys, read_keys)

    def beside(got):
        made = local(inputs, grad_out, log_decay, write_keys, read_keys)
        return lax.optimization_barrier((got, made))

    entry, after, made = carried_states(summed, states, beside)
    read_terms, write_terms, *made = made
    terms = grads(lead, tail, read_terms, write_terms, entry, after)

    def part(first, count, earlier):
        return outputs(
            first, count, earlier, inputs, grad_out, write_keys, read_keys, made, entry, after, skip
        )

    if lax.axis_size("mp") == 4:
        early = steps // 2
        results, own, parts = head_sum(
            terms, lambda *held: lax.optimization_barrier((part(0, early, ()), held))
        )
        results, parts = lax.optimization_barrier((part(early, steps - early, results), parts))
        for term in parts:
            own = own + term
    else:
        own = lax.psum_scatter(terms, "mp", scatter_dimension=0, tiled=True)
        results = part(0, steps, ())
    return *results, own[:, states:], own[:, :states]


def solution(mesh):
    tokens = ("outer", "inner")
    return jax.shard_map(
        on_device,
        mesh=mesh,
        in_specs=(
            P(tokens, "mp"),
            P("mp", tokens),
            P(tokens, None),
            P(tokens, None),
            P("mp"),
            P(tokens, "mp"),
        ),
        out_specs=(
            P(tokens, "mp"),
            P(tokens, "mp"),
            P(("outer", "inner", "mp"), None),
            P(("outer", "inner", "mp"), None),
        ),
        check_vma=False,
    )
```

```python
import functools

import jax
import jax.numpy as jnp
from jax import lax
from jax.experimental import pallas as pl
from jax.experimental.pallas import tpu as pltpu
from jax.sharding import PartitionSpec as P

WIDTH = 64
BLOCK = 128
STEP = 512
FAR = -1e30
LOG2E = 1.4426950408889634
VMEM_BYTES = 60 * 1024 * 1024
F32 = jnp.float32
BF16 = jnp.bfloat16


def dot(a, b, over_a, over_b):
    return lax.dot_general(a, b, (((over_a,), (over_b,)), ((), ())), preferred_element_type=F32)


def minus_expm1(y):
    series = 1.0 + y * (1.0 / 9.0)
    for k in (8.0, 7.0, 6.0, 5.0, 4.0, 3.0, 2.0):
        series = 1.0 + y * (1.0 / k) * series
    return jnp.where(y > -0.4, -y * series, 1.0 - jnp.exp(y))


def iota(shape, dimension):
    return lax.broadcasted_iota(jnp.int32, shape, dimension)


def spread_matrix(heads, group):
    shape = (128, heads * WIDTH)
    row = iota(shape, 0) - 2 * heads * group
    gap = iota(shape, 1) - WIDTH * jnp.where(row < heads, row, row - heads)
    inside = (row >= 0) & (row < 2 * heads) & (gap >= 0) & (gap < WIDTH)
    return jnp.where(inside, 1.0, 0.0).astype(BF16)


def row_spread_matrix(heads):
    shape = (heads, heads * WIDTH)
    gap = iota(shape, 1) - WIDTH * iota(shape, 0)
    one = jnp.where((gap >= 0) & (gap < WIDTH), 1.0, 0.0)
    return jnp.concatenate([one, one, one], axis=0).astype(BF16)


def three(x):
    high = x.astype(BF16).astype(F32)
    middle = (x - high).astype(BF16).astype(F32)
    return high, middle, x - high - middle


def block_sums(rows):
    shape = (BLOCK, 2 * BLOCK)
    source, target = iota(shape, 0), iota(shape, 1)
    upto = jnp.where(source <= target, 1.0, 0.0)
    beyond = jnp.where(source > target - BLOCK, 1.0, 0.0)
    within = jnp.where(target < BLOCK, upto, beyond).astype(BF16)
    count = rows.shape[0]
    both = dot(jnp.concatenate(three(rows), axis=0).astype(BF16), within, 1, 0)
    both = both[:count] + both[count : 2 * count] + both[2 * count :]
    return both[:, :BLOCK], both[:, BLOCK:]


def stacked(x):
    return jnp.concatenate(
        [x[:, at : at + BLOCK] for at in range(0, x.shape[1], BLOCK)], axis=0
    )


def block_factors(ld_ref):
    ld = ld_ref[...]
    gain = stacked(jnp.sqrt(minus_expm1(2.0 * ld)))
    before, behind = block_sums(stacked(ld))
    return gain, before, behind


def in_columns(groups, heads, block):
    parts = []
    for factor in groups:
        rows = factor[block * heads : block * heads + heads]
        high = rows.astype(BF16).astype(F32)
        parts += [high, rows - high]
    parts.append(jnp.zeros((128 - 2 * heads * len(groups), BLOCK), F32))
    rows = jnp.concatenate(parts, axis=0).astype(BF16)
    eye = jnp.where(iota((BLOCK, BLOCK), 0) == iota((BLOCK, BLOCK), 1), 1.0, 0.0).astype(BF16)
    return dot(eye, rows, 1, 1).astype(BF16)


def starts_and_ends(before, heads, count):
    totals = [before[c * heads : c * heads + heads, BLOCK - 1 :] for c in range(count)]
    start = [jnp.zeros((heads, 1), F32)]
    for total in totals:
        start.append(start[-1] + total)
    end = [jnp.zeros((heads, 1), F32)]
    for total in totals[::-1]:
        end.append(end[-1] + total)
    since = jnp.concatenate(start[:count], axis=0)
    until = jnp.concatenate(end[:count][::-1], axis=0)
    return since, until, start[count]


def totals_kernel(
    inputs_ref, grad_ref, ld_ref, write_ref, read_ref, out_ref, parts, lanes_of
):
    step = pl.program_id(0)
    heads = ld_ref.shape[0]
    states = write_ref.shape[1]
    count = ld_ref.shape[1] // BLOCK

    @pl.when(step == 0)
    def _():
        lanes_of[0] = spread_matrix(heads, 0)
        lanes_of[1] = spread_matrix(heads, 1)
        gain, before, behind = block_factors(ld_ref)
        since, until, whole = starts_and_ends(before, heads, count)
        lead = jnp.exp(since + before)
        tail = gain * jnp.exp(until + behind)
        for c in range(count):
            parts[c * BLOCK : c * BLOCK + BLOCK] = in_columns((lead, tail), heads, c)
        out_ref[...] = jnp.zeros_like(out_ref)
        whole = jnp.concatenate(three(jnp.exp(whole)), axis=0)
        whole = jnp.broadcast_to(whole, (3 * heads, 128)).astype(BF16)
        out_ref[2 * states :] = dot(whole, row_spread_matrix(heads), 0, 0)[0:8]

    at = pl.ds(pl.multiple_of(step * STEP, STEP), STEP)
    here = parts[at, :]
    lead = (dot(here, lanes_of[0], 1, 0) * grad_ref[...].astype(F32)).astype(BF16)
    out_ref[states : 2 * states] += dot(read_ref[...], lead, 0, 0)
    tail = (dot(here, lanes_of[1], 1, 0) * inputs_ref[...].astype(F32)).astype(BF16)
    out_ref[0:states] += dot(write_ref[...], tail, 0, 0)


def totals(inputs, grad_out, log_decay, write_keys, read_keys):
    length, lanes = inputs.shape
    heads = log_decay.shape[0]
    states = write_keys.shape[1]
    wide = pl.BlockSpec((STEP, lanes), lambda c: (c, 0))
    keys = pl.BlockSpec((STEP, states), lambda c: (c, 0))
    return pl.pallas_call(
        totals_kernel,
        out_shape=jax.ShapeDtypeStruct((2 * states + 8, lanes), F32),
        grid=(length // STEP,),
        in_specs=[wide, wide, pl.BlockSpec((heads, length), lambda c: (0, 0)), keys, keys],
        out_specs=pl.BlockSpec((2 * states + 8, lanes), lambda c: (0, 0)),
        scratch_shapes=[
            pltpu.VMEM((length, 128), BF16),
            pltpu.VMEM((2, 128, lanes), BF16),
        ],
        compiler_params=pltpu.CompilerParams(vmem_limit_bytes=VMEM_BYTES),
        cost_estimate=pl.CostEstimate(
            flops=6 * length * lanes * states, bytes_accessed=4 * length * lanes, transcendentals=0
        ),
        name="totals",
    )(inputs, grad_out, log_decay, write_keys, read_keys)


def factors_kernel(ld_ref, near_ref, rows_ref, decays_ref, ranges_ref):
    heads, length = ld_ref.shape
    count = length // BLOCK
    gain, before, behind = block_factors(ld_ref)
    lead = jnp.exp(before)
    tail = gain * jnp.exp(behind)
    rows_ref[...] = before * LOG2E
    lasts = []
    for c in range(count):
        at = slice(c * BLOCK, c * BLOCK + BLOCK)
        near_ref[at] = in_columns((lead, tail, gain), heads, c)
        lasts.append(lead[c * heads : c * heads + heads, BLOCK - 1 :])
    last = jnp.concatenate(lasts, axis=1)
    decays = dot(jnp.concatenate(three(last), axis=0).astype(BF16), row_spread_matrix(heads), 0, 0)
    decays_ref[...] = decays
    ones = jnp.ones((1, heads * WIDTH), F32)
    after, before = [ones], [ones]
    for c in range(count - 1):
        after.append(after[-1] * decays[c : c + 1])
        before.append(before[-1] * decays[count - 1 - c : count - c])
    ranges_ref[:count] = jnp.concatenate(after, axis=0)
    ranges_ref[count:] = jnp.concatenate(before[::-1], axis=0)


def factors(log_decay):
    heads, length = log_decay.shape
    count = length // BLOCK
    lanes = heads * WIDTH
    return pl.pallas_call(
        factors_kernel,
        out_shape=(
            jax.ShapeDtypeStruct((length, 128), BF16),
            jax.ShapeDtypeStruct((count * heads, BLOCK), F32),
            jax.ShapeDtypeStruct((count, lanes), F32),
            jax.ShapeDtypeStruct((2 * count, lanes), F32),
        ),
        compiler_params=pltpu.CompilerParams(vmem_limit_bytes=VMEM_BYTES),
        cost_estimate=pl.CostEstimate(
            flops=heads * length * 6000, bytes_accessed=1000 * length, transcendentals=0
        ),
        name="factors",
    )(log_decay)


def halves(pair):
    first = iota(pair.shape, 1) < WIDTH
    zero = jnp.zeros_like(pair)
    return jnp.concatenate([jnp.where(first, pair, zero), jnp.where(first, zero, pair)], axis=0)


def lower_block():
    return iota((BLOCK, BLOCK), 0) >= iota((BLOCK, BLOCK), 1)


def key_block(scaled, grad, rows):
    heads = rows.shape[0]
    columns = rows.T
    lower = lower_block()
    gathered = jnp.zeros((BLOCK, BLOCK), F32)
    for pair in range(heads // 2):
        lanes = slice(pair * 128, pair * 128 + 128)
        products = dot(grad[:, lanes], halves(scaled[:, lanes]), 1, 1)
        for j in range(2):
            head = 2 * pair + j
            gap = columns[:, head : head + 1] - rows[head : head + 1, :]
            decay = jnp.exp2(jnp.where(lower, gap, FAR))
            gathered += products[:, j * BLOCK : j * BLOCK + BLOCK] * decay
    return gathered


def two_parts(x):
    high = x.astype(BF16)
    return high, (x - high.astype(F32)).astype(BF16)


def local_kernel(
    plan_ref,
    inputs_ref,
    grad_ref,
    write_ref,
    read_ref,
    parts_ref,
    rows_ref,
    decays_ref,
    ranges_ref,
    entries_ref,
    afters_ref,
    read_terms_ref,
    write_terms_ref,
    far_lead_ref,
    far_tail_ref,
    entry,
    leads,
    tails,
    states_in,
    states_out,
    write_terms,
    lanes_of,
):
    step = pl.program_id(0)
    states, lanes = entry.shape
    heads = lanes // WIDTH
    count = decays_ref.shape[0]
    steps = decays_ref.shape[0] * BLOCK // STEP
    inner = STEP // BLOCK

    @pl.when(step == 0)
    def _():
        for k in range(3):
            lanes_of[k] = spread_matrix(heads, k)
        entry[...] = jnp.zeros_like(entry)

    @pl.when(step < steps)
    def _():
        here = parts_ref[...]
        whole = pl.ds(pl.multiple_of(step * STEP, STEP), STEP)
        leads[whole, :] = (dot(here, lanes_of[0], 1, 0) * grad_ref[...].astype(F32)).astype(BF16)
        tails[whole, :] = (dot(here, lanes_of[1], 1, 0) * inputs_ref[...].astype(F32)).astype(BF16)
        entries_ref[...] = entry[...].astype(BF16)
        for k in range(inner):
            block = step * inner + k
            at = pl.ds(pl.multiple_of(block * BLOCK, BLOCK), BLOCK)
            state = entry[...]
            states_in[k * BLOCK : k * BLOCK + BLOCK] = state.astype(BF16)
            entry[...] = state * decays_ref[pl.ds(block, 1), :] + dot(
                write_ref[at, :], tails[at, :], 0, 0
            )

    @pl.when((step == plan_ref[0]) | (step == plan_ref[1]))
    def _():
        scaled = (dot(parts_ref[...], lanes_of[2], 1, 0) * inputs_ref[...].astype(F32)).astype(BF16)
        for k in range(inner):
            inside = slice(k * BLOCK, k * BLOCK + BLOCK)
            block = step * inner + k
            at = pl.ds(pl.multiple_of(block * BLOCK, BLOCK), BLOCK)
            write, read = write_ref[at, :], read_ref[at, :]
            lead, tail = leads[at, :], tails[at, :]
            far_lead_ref[inside] = (lead.astype(F32) * ranges_ref[pl.ds(block, 1), :]).astype(BF16)
            far_tail_ref[inside] = (
                tail.astype(F32) * ranges_ref[pl.ds(count + block, 1), :]
            ).astype(BF16)
            high, low = two_parts(
                key_block(scaled[inside], grad_ref[inside], rows_ref[k * heads : k * heads + heads, :])
            )
            read_terms_ref[inside] = (
                dot(lead, states_in[inside], 1, 1) + dot(high, write, 1, 0) + dot(low, write, 1, 0)
            )
            write_terms[at, :] = dot(high, read, 0, 0) + dot(low, read, 0, 0)

    @pl.when(step == steps)
    def _():
        state = jnp.zeros_like(entry)
        for block in reversed(range(count)):
            at = slice(block * BLOCK, block * BLOCK + BLOCK)
            states_out[at] = state.astype(BF16)
            state = state * decays_ref[block : block + 1] + dot(read_ref[at, :], leads[at], 0, 0)
        for quarter in range(steps):
            last = quarter * STEP + STEP - BLOCK
            afters_ref[quarter * states : quarter * states + states] = states_out[last : last + BLOCK]
        for slot in range(2):
            for k in range(inner):
                place = slot * STEP + k * BLOCK
                at = pl.ds(pl.multiple_of(plan_ref[slot] * STEP + k * BLOCK, BLOCK), BLOCK)
                write_terms_ref[place : place + BLOCK] = write_terms[at, :] + dot(
                    tails[at, :], states_out[at, :], 1, 1
                )


def local(plan, inputs, grad_out, write_keys, read_keys, parts, rows, decays, ranges):
    length, lanes = inputs.shape
    heads = lanes // WIDTH
    states = write_keys.shape[1]
    assert states == BLOCK and 6 * heads <= 128
    steps = length // STEP

    def forth(c, plan):
        return jnp.minimum(c, steps - 1)

    def slot_forth(c, plan):
        return jnp.where(c > plan[0], 1, 0)

    def all_of(c, plan):
        return 0

    def whole(x):
        return pl.BlockSpec(x.shape, lambda c, plan: (0, 0))

    def tokens(at, size, width):
        return pl.BlockSpec((size, width), lambda c, plan: (at(c, plan), 0))

    return pl.pallas_call(
        local_kernel,
        out_shape=(
            jax.ShapeDtypeStruct((steps * states, lanes), BF16),
            jax.ShapeDtypeStruct((steps * states, lanes), BF16),
            jax.ShapeDtypeStruct((2 * STEP, states), F32),
            jax.ShapeDtypeStruct((2 * STEP, states), F32),
            jax.ShapeDtypeStruct((2 * STEP, lanes), BF16),
            jax.ShapeDtypeStruct((2 * STEP, lanes), BF16),
        ),
        grid_spec=pltpu.PrefetchScalarGridSpec(
            num_scalar_prefetch=1,
            grid=(steps + 1,),
            in_specs=[
                tokens(forth, STEP, lanes),
                tokens(forth, STEP, lanes),
                whole(write_keys),
                whole(read_keys),
                tokens(forth, STEP, 128),
                tokens(forth, STEP // BLOCK * heads, BLOCK),
                whole(decays),
                whole(ranges),
            ],
            out_specs=(
                tokens(forth, states, lanes),
                tokens(all_of, steps * states, lanes),
                tokens(slot_forth, STEP, states),
                tokens(all_of, 2 * STEP, states),
                tokens(slot_forth, STEP, lanes),
                tokens(slot_forth, STEP, lanes),
            ),
            scratch_shapes=[
                pltpu.VMEM((states, lanes), F32),
                pltpu.VMEM((length, lanes), BF16),
                pltpu.VMEM((length, lanes), BF16),
                pltpu.VMEM((STEP, lanes), BF16),
                pltpu.VMEM((length, lanes), BF16),
                pltpu.VMEM((length, states), F32),
                pltpu.VMEM((3, 128, lanes), BF16),
            ],
        ),
        compiler_params=pltpu.CompilerParams(vmem_limit_bytes=VMEM_BYTES),
        cost_estimate=pl.CostEstimate(
            flops=24 * length * lanes * states, bytes_accessed=8 * length * lanes, transcendentals=0
        ),
        name="local",
    )(plan, inputs, grad_out, write_keys, read_keys, parts, rows, decays, ranges)


def early_grads_kernel(
    plan_ref,
    lead_ref,
    tail_ref,
    read_terms_ref,
    write_terms_ref,
    own_ref,
    others_ref,
    other_ref,
    entry_ref,
    after_ref,
    far_ref,
    crossed_ref,
    halved,
):
    step = pl.program_id(0)
    states, lanes = entry_ref.shape
    part = states // 2

    @pl.when(step == 0)
    def _():
        first = plan_ref[4] == 1
        own, others = own_ref[...], others_ref[...]
        top, bottom = jnp.where(first, own, others), jnp.where(first, others, own)
        entry = jnp.concatenate([top[:part], bottom[:part]], axis=0)
        after = jnp.concatenate([top[part:], bottom[part:]], axis=0)
        decay = other_ref[2 * states : 2 * states + 1]
        entry = jnp.where(first, entry, other_ref[:states] + decay * entry)
        after = jnp.where(first, other_ref[states : 2 * states] + decay * after, after)
        entry_ref[...] = entry
        after_ref[...] = after
        halved[0] = entry.astype(BF16)
        halved[1] = after.astype(BF16)

    read = read_terms_ref[...] + dot(lead_ref[...], halved[0], 1, 1)
    write = write_terms_ref[...] + dot(tail_ref[...], halved[1], 1, 1)
    for at, out in ((plan_ref[5], far_ref), (1 - plan_ref[5], crossed_ref)):

        @pl.when(step == at)
        def _():
            out[:, :states] = read
            out[:, states:] = write


def early_grads(plan, lead, tail, read_terms, write_terms, own, others, other):
    lanes = lead.shape[1]
    states = read_terms.shape[1]

    def tokens(width):
        return pl.BlockSpec((STEP, width), lambda c, plan: (c, 0))

    def whole(x):
        return pl.BlockSpec(x.shape, lambda c, plan: (0, 0))

    state = jax.ShapeDtypeStruct((states, lanes), F32)
    terms = jax.ShapeDtypeStruct((STEP, 2 * states), F32)
    shapes = (state, state, terms, terms)
    return pl.pallas_call(
        early_grads_kernel,
        out_shape=shapes,
        grid_spec=pltpu.PrefetchScalarGridSpec(
            num_scalar_prefetch=1,
            grid=(2,),
            in_specs=[
                tokens(lanes),
                tokens(lanes),
                tokens(states),
                tokens(states),
                whole(own),
                whole(others),
                whole(other),
            ],
            out_specs=tuple(whole(x) for x in shapes),
            scratch_shapes=[pltpu.VMEM((2, states, lanes), BF16)],
        ),
        compiler_params=pltpu.CompilerParams(vmem_limit_bytes=VMEM_BYTES),
        cost_estimate=pl.CostEstimate(
            flops=8 * STEP * lanes * states, bytes_accessed=8 * STEP * lanes, transcendentals=0
        ),
        name="early_grads",
    )(plan, lead, tail, read_terms, write_terms, own, others, other)


def combine_kernel(place_ref, *refs):
    *got, out_ref = refs
    place = place_ref[0]
    part, lanes = got[0].shape[0] - 8, got[0].shape[1]
    entry = jnp.zeros((part, lanes), F32)
    after = jnp.zeros((part, lanes), F32)
    for m, value in enumerate(got, 1):
        source = place ^ m
        weight = jnp.ones((1, lanes), F32)
        for k, between in enumerate(got, 1):
            middle = place ^ k
            inside = ((source < middle) & (middle < place)) | ((place < middle) & (middle < source))
            weight = weight * jnp.where(inside, between[part : part + 1], 1.0)
        term = weight * value[:part]
        entry = entry + jnp.where(source < place, term, 0.0)
        after = after + jnp.where(source > place, term, 0.0)
    out_ref[:part] = entry
    out_ref[part:] = after


def combine(place, got):
    rows, lanes = got[0].shape
    return pl.pallas_call(
        combine_kernel,
        out_shape=jax.ShapeDtypeStruct((2 * (rows - 8), lanes), F32),
        in_specs=[pl.BlockSpec(memory_space=pltpu.SMEM)]
        + [pl.BlockSpec(memory_space=pltpu.VMEM)] * len(got),
        out_specs=pl.BlockSpec(memory_space=pltpu.VMEM),
        compiler_params=pltpu.CompilerParams(vmem_limit_bytes=VMEM_BYTES),
        cost_estimate=pl.CostEstimate(
            flops=4 * len(got) * rows * lanes,
            bytes_accessed=4 * (len(got) + 2) * rows * lanes,
            transcendentals=0,
        ),
        name="combine",
    )(place.reshape(1), *got)


def outputs_kernel(
    offset,
    with_terms,
    aliased,
    plan_ref,
    inputs_ref,
    grad_ref,
    write_ref,
    read_ref,
    entries_ref,
    afters_ref,
    parts_ref,
    rows_ref,
    decays_ref,
    ranges_ref,
    entry_ref,
    after_ref,
    skip_ref,
    *rest,
):
    mixed_ref, grad_in_ref, *terms, lanes_of, states_in, states_out, skip_row = rest[aliased:]
    step = pl.program_id(0)
    states = write_ref.shape[1]
    heads = skip_ref.shape[1]
    count = ranges_ref.shape[0] // 2
    inner = STEP // BLOCK

    @pl.when(step == 0)
    def _():
        for k in range(3):
            lanes_of[k] = spread_matrix(heads, k)
        gains = jnp.concatenate(three(jnp.broadcast_to(skip_ref[...], (8, heads))), axis=1)
        skip_row[...] = dot(gains.astype(BF16), row_spread_matrix(heads), 1, 0)

    leads, tails, gains = [dot(parts_ref[...], lanes_of[k], 1, 0) for k in range(3)]
    scaled = (gains * inputs_ref[...].astype(F32)).astype(BF16)
    lead = (leads * grad_ref[...].astype(F32)).astype(BF16)
    tail = (tails * inputs_ref[...].astype(F32)).astype(BF16)
    start = plan_ref[offset + step] * inner
    state = entries_ref[...].astype(F32) + ranges_ref[pl.ds(start, 1), :] * entry_ref[...]
    for k in range(inner):
        at = slice(k * BLOCK, k * BLOCK + BLOCK)
        states_in[at] = state.astype(BF16)
        if k < inner - 1:
            state = state * decays_ref[pl.ds(start + k, 1), :] + dot(write_ref[at, :], tail[at], 0, 0)
    end = start + inner - 1
    state = afters_ref[...].astype(F32) + ranges_ref[pl.ds(count + end, 1), :] * after_ref[...]
    for k in reversed(range(inner)):
        at = slice(k * BLOCK, k * BLOCK + BLOCK)
        states_out[at] = state.astype(BF16)
        if k > 0:
            state = state * decays_ref[pl.ds(start + k, 1), :] + dot(read_ref[at, :], lead[at], 0, 0)
    found = []
    for k in range(inner):
        at = slice(k * BLOCK, k * BLOCK + BLOCK)
        write, read = write_ref[at, :], read_ref[at, :]
        grad = grad_ref[at]
        entry, after = states_in[at], states_out[at]
        skip = skip_row[0:1]
        out_rest = leads[at] * dot(read, entry, 1, 0) + skip * inputs_ref[at].astype(F32)
        back_rest = tails[at] * dot(write, after, 1, 0) + skip * grad.astype(F32)
        scores = dot(read, write, 1, 1)
        rows = rows_ref[k * heads : k * heads + heads, :]
        columns = rows.T
        lower = lower_block()
        gathered = jnp.zeros((BLOCK, BLOCK), F32)
        for pair in range(heads // 2):
            lanes = slice(pair * 128, pair * 128 + 128)
            scaled_pair = halves(scaled[at, lanes])
            if with_terms:
                products = dot(grad[:, lanes], scaled_pair, 1, 1)
            mixing = []
            for j in range(2):
                head = 2 * pair + j
                gap = columns[:, head : head + 1] - rows[head : head + 1, :]
                decay = jnp.exp2(jnp.where(lower, gap, FAR))
                mixing.append((scores * decay).astype(BF16))
                if with_terms:
                    gathered += products[:, j * BLOCK : j * BLOCK + BLOCK] * decay
            mixed = dot(jnp.concatenate(mixing, axis=1), scaled_pair, 1, 0)
            mixed_ref[at, lanes] = (mixed + out_rest[:, lanes]).astype(BF16)
            back = dot(jnp.concatenate(mixing, axis=0), halves(grad[:, lanes]), 0, 0)
            grad_in_ref[at, lanes] = (gains[at, lanes] * back + back_rest[:, lanes]).astype(BF16)
        if with_terms:
            high, low = two_parts(gathered)
            found.append(
                (
                    dot(lead[at], entry, 1, 1) + dot(high, write, 1, 0) + dot(low, write, 1, 0),
                    dot(tail[at], after, 1, 1) + dot(high, read, 0, 0) + dot(low, read, 0, 0),
                )
            )
    for k, (for_read, for_write) in enumerate(found):
        terms[0][k * BLOCK : k * BLOCK + BLOCK, :states] = for_read
        terms[0][k * BLOCK : k * BLOCK + BLOCK, states:] = for_write


def outputs(
    plan, offset, steps, with_terms, earlier, inputs, grad_out, write_keys, read_keys, made, entry, after, skip
):
    assert steps == 1 or not with_terms
    length, lanes = inputs.shape
    states = write_keys.shape[1]
    entries, afters, parts, rows, decays, ranges = made
    heads = lanes // WIDTH

    def tokens(size, width):
        return pl.BlockSpec((size, width), lambda c, plan: (plan[offset + c], 0))

    def whole(x):
        return pl.BlockSpec(x.shape, lambda c, plan: (0, 0))

    wide = tokens(STEP, lanes)
    shape = jax.ShapeDtypeStruct((length, lanes), BF16)
    terms = (jax.ShapeDtypeStruct((STEP, 2 * states), F32),) * with_terms
    return pl.pallas_call(
        functools.partial(outputs_kernel, offset, with_terms, len(earlier)),
        out_shape=(shape, shape, *terms),
        grid_spec=pltpu.PrefetchScalarGridSpec(
            num_scalar_prefetch=1,
            grid=(steps,),
            in_specs=[
                wide,
                wide,
                tokens(STEP, states),
                tokens(STEP, states),
                tokens(states, lanes),
                tokens(states, lanes),
                tokens(STEP, 128),
                tokens(STEP // BLOCK * heads, BLOCK),
                whole(decays),
                whole(ranges),
                whole(entry),
                whole(after),
                whole(skip),
                *[pl.BlockSpec(memory_space=pl.ANY) for _ in earlier],
            ],
            out_specs=(wide, wide, *[whole(x) for x in terms]),
            scratch_shapes=[
                pltpu.VMEM((3, 128, lanes), BF16),
                pltpu.VMEM((STEP, lanes), BF16),
                pltpu.VMEM((STEP, lanes), BF16),
                pltpu.VMEM((8, lanes), F32),
            ],
        ),
        input_output_aliases={14 + k: k for k in range(len(earlier))},
        compiler_params=pltpu.CompilerParams(vmem_limit_bytes=VMEM_BYTES),
        cost_estimate=pl.CostEstimate(
            flops=16 * steps * STEP * lanes * states, bytes_accessed=12 * steps * STEP * lanes, transcendentals=0
        ),
        name="outputs_and_terms" if with_terms else "outputs",
    )(
        plan, inputs, grad_out, write_keys, read_keys, entries, afters, parts, rows, decays, ranges,
        entry, after, skip, *earlier,
    )


def carried_states(summed, states, first_window, second_window):
    axes = ("outer", "inner")
    devices = lax.axis_size(axes)
    here = lax.axis_index(axes)
    first = lax.rem(here, 2) == 0
    place = here // 2
    part = states // 2
    other = lax.ppermute(summed, axes, [(d, d ^ 1) for d in range(devices)])
    other, made = first_window(other)
    early_decay = jnp.where(first, summed, other)[2 * states : 2 * states + 1]
    late_decay = jnp.where(first, other, summed)[2 * states : 2 * states + 1]
    row = jnp.where(first, 0, part)

    def mine(x, start):
        return lax.dynamic_slice_in_dim(x, start + row, part, 0)

    early_push = jnp.where(first, mine(summed, 0), mine(other, 0))
    late_push = jnp.where(first, mine(other, 0), mine(summed, 0))
    early_pull = jnp.where(first, mine(summed, states), mine(other, states))
    late_pull = jnp.where(first, mine(other, states), mine(summed, states))
    push = late_push + late_decay * early_push
    pull = early_pull + early_decay * late_pull
    decay = jnp.broadcast_to(early_decay * late_decay, (8, summed.shape[1]))
    got = []
    for m in range(1, devices // 2):
        sent = jnp.concatenate([jnp.where(place < (place ^ m), push, pull), decay], axis=0)
        got.append(lax.ppermute(sent, axes, [(d, d ^ (2 * m)) for d in range(devices)]))
    got, made = second_window(got, made)
    own = combine(place, got)
    others = lax.ppermute(own, axes, [(d, d ^ 1) for d in range(devices)])
    return (own, others, other), made


def on_device(inputs, log_decay, write_keys, read_keys, skip_gain, grad_out):
    states = write_keys.shape[1]
    line = lax.axis_size("mp") == 4
    assert inputs.shape[0] == 4 * STEP

    at = lax.axis_index("mp")
    ends = (at == 0) | (at == 3)

    def of(*values):
        if not line:
            return jnp.int32(values[0])
        return sum(jnp.where(at == k, v, 0) for k, v in enumerate(values)).astype(jnp.int32)

    even = (lax.rem(lax.axis_index(("outer", "inner")), 2) == 0).astype(jnp.int32)
    plan = jnp.stack(
        [
            of(2, 0, 1, 0),
            of(3, 2, 3, 1),
            of(1, 3, 0, 2),
            of(0, 1, 2, 3),
            even,
            of(1, 0, 1, 0),
        ]
    )
    summed = totals(inputs, grad_out, log_decay, write_keys, read_keys)

    def first_window(other):
        ordered, _ = lax.optimization_barrier((log_decay, summed))
        return lax.optimization_barrier((other, factors(ordered)))

    def second_window(got, made):
        parts, rows, decays, ranges = made
        found = local(plan, inputs, grad_out, write_keys, read_keys, parts, rows, decays, ranges)
        return lax.optimization_barrier((got, (found, made)))

    given, made = carried_states(summed, states, first_window, second_window)
    (entries, afters, read_terms, write_terms, lead, tail), made = made
    entry, after, far, crossed = early_grads(plan, lead, tail, read_terms, write_terms, *given)

    def part(offset, steps, with_terms, earlier):
        return outputs(
            plan, offset, steps, with_terms, earlier, inputs, grad_out, write_keys, read_keys,
            (entries, afters, *made), entry, after, skip_gain[None],
        )

    if not line:
        *results, third = part(2, 1, True, ())
        *results, own = part(3, 1, True, results)
        results = part(0, 2, False, results)
        terms = jnp.concatenate([own, third, crossed, far], axis=0)
        own = lax.psum_scatter(terms, "mp", scatter_dimension=0, tiled=True)
        return *results, own[:, states:], own[:, :states]

    far_sum = lax.ppermute(far, "mp", [(0, 1), (1, 0), (2, 3), (3, 2)])
    middle = lax.ppermute(crossed, "mp", [(1, 2), (2, 1)])
    (*results, third), crossed = lax.optimization_barrier((part(2, 1, True, ()), crossed))
    two_away = lax.ppermute(crossed, "mp", [(0, 2), (3, 1)])
    (*results, own), far_sum, third = lax.optimization_barrier(
        (part(3, 1, True, results), far_sum, third)
    )
    last = lax.ppermute(third + far_sum, "mp", [(1, 3), (2, 0)])
    near_terms = lax.ppermute(third, "mp", [(0, 1), (3, 2)])
    results, middle, last, two_away, near_terms = lax.optimization_barrier(
        (part(0, 2, False, results), middle, last, two_away, near_terms)
    )

    def summed_up(lanes):
        came = jnp.where(ends, far_sum[:, lanes], near_terms[:, lanes])
        return own[:, lanes] + came + (middle[:, lanes] + two_away[:, lanes] + last[:, lanes])

    return *results, summed_up(slice(states, None)), summed_up(slice(0, states))


def solution(mesh):
    tokens = ("outer", "inner")
    return jax.shard_map(
        on_device,
        mesh=mesh,
        in_specs=(
            P(tokens, "mp"),
            P("mp", tokens),
            P(tokens, None),
            P(tokens, None),
            P("mp"),
            P(tokens, "mp"),
        ),
        out_specs=(
            P(tokens, "mp"),
            P(tokens, "mp"),
            P(("outer", "inner", "mp"), None),
            P(("outer", "inner", "mp"), None),
        ),
        check_vma=False,
    )
```

```python
import functools

import jax
import jax.numpy as jnp
from jax import lax
from jax.experimental import pallas as pl
from jax.experimental.pallas import tpu as pltpu
from jax.sharding import PartitionSpec as P

WIDTH = 64
BLOCK = 128
STEP = 512
FAR = -1e30
LOG2E = 1.4426950408889634
VMEM_BYTES = 60 * 1024 * 1024
F32 = jnp.float32
BF16 = jnp.bfloat16


def dot(a, b, over_a, over_b):
    return lax.dot_general(a, b, (((over_a,), (over_b,)), ((), ())), preferred_element_type=F32)


def minus_expm1(y):
    series = 1.0 + y * (1.0 / 9.0)
    for k in (8.0, 7.0, 6.0, 5.0, 4.0, 3.0, 2.0):
        series = 1.0 + y * (1.0 / k) * series
    return jnp.where(y > -0.4, -y * series, 1.0 - jnp.exp(y))


def iota(shape, dimension):
    return lax.broadcasted_iota(jnp.int32, shape, dimension)


def spread_matrix(heads, group):
    shape = (128, heads * WIDTH)
    row = iota(shape, 0) - 2 * heads * group
    gap = iota(shape, 1) - WIDTH * jnp.where(row < heads, row, row - heads)
    inside = (row >= 0) & (row < 2 * heads) & (gap >= 0) & (gap < WIDTH)
    return jnp.where(inside, 1.0, 0.0).astype(BF16)


def row_spread_matrix(heads):
    shape = (heads, heads * WIDTH)
    gap = iota(shape, 1) - WIDTH * iota(shape, 0)
    one = jnp.where((gap >= 0) & (gap < WIDTH), 1.0, 0.0)
    return jnp.concatenate([one, one, one], axis=0).astype(BF16)


def three(x):
    high = x.astype(BF16).astype(F32)
    middle = (x - high).astype(BF16).astype(F32)
    return high, middle, x - high - middle


def block_sums(rows):
    shape = (BLOCK, 2 * BLOCK)
    source, target = iota(shape, 0), iota(shape, 1)
    upto = jnp.where(source <= target, 1.0, 0.0)
    beyond = jnp.where(source > target - BLOCK, 1.0, 0.0)
    within = jnp.where(target < BLOCK, upto, beyond).astype(BF16)
    count = rows.shape[0]
    both = dot(jnp.concatenate(three(rows), axis=0).astype(BF16), within, 1, 0)
    both = both[:count] + both[count : 2 * count] + both[2 * count :]
    return both[:, :BLOCK], both[:, BLOCK:]


def stacked(x):
    return jnp.concatenate(
        [x[:, at : at + BLOCK] for at in range(0, x.shape[1], BLOCK)], axis=0
    )


def block_factors(ld_ref):
    ld = ld_ref[...]
    gain = stacked(jnp.sqrt(minus_expm1(2.0 * ld)))
    before, behind = block_sums(stacked(ld))
    return gain, before, behind


def in_columns(groups, heads, block):
    parts = []
    for factor in groups:
        rows = factor[block * heads : block * heads + heads]
        high = rows.astype(BF16).astype(F32)
        parts += [high, rows - high]
    parts.append(jnp.zeros((128 - 2 * heads * len(groups), BLOCK), F32))
    rows = jnp.concatenate(parts, axis=0).astype(BF16)
    eye = jnp.where(iota((BLOCK, BLOCK), 0) == iota((BLOCK, BLOCK), 1), 1.0, 0.0).astype(BF16)
    return dot(eye, rows, 1, 1).astype(BF16)


def starts_and_ends(before, heads, count):
    totals = [before[c * heads : c * heads + heads, BLOCK - 1 :] for c in range(count)]
    start = [jnp.zeros((heads, 1), F32)]
    for total in totals:
        start.append(start[-1] + total)
    end = [jnp.zeros((heads, 1), F32)]
    for total in totals[::-1]:
        end.append(end[-1] + total)
    since = jnp.concatenate(start[:count], axis=0)
    until = jnp.concatenate(end[:count][::-1], axis=0)
    return since, until, start[count]


def totals_kernel(
    inputs_ref, grad_ref, ld_ref, write_ref, read_ref, out_ref, parts, lanes_of
):
    step = pl.program_id(0)
    heads = ld_ref.shape[0]
    states = write_ref.shape[1]
    count = ld_ref.shape[1] // BLOCK

    @pl.when(step == 0)
    def _():
        lanes_of[0] = spread_matrix(heads, 0)
        lanes_of[1] = spread_matrix(heads, 1)
        gain, before, behind = block_factors(ld_ref)
        since, until, whole = starts_and_ends(before, heads, count)
        lead = jnp.exp(since + before)
        tail = gain * jnp.exp(until + behind)
        for c in range(count):
            parts[c * BLOCK : c * BLOCK + BLOCK] = in_columns((lead, tail), heads, c)
        out_ref[...] = jnp.zeros_like(out_ref)
        whole = jnp.concatenate(three(jnp.exp(whole)), axis=0)
        whole = jnp.broadcast_to(whole, (3 * heads, 128)).astype(BF16)
        out_ref[2 * states :] = dot(whole, row_spread_matrix(heads), 0, 0)[0:8]

    at = pl.ds(pl.multiple_of(step * STEP, STEP), STEP)
    here = parts[at, :]
    lead = (dot(here, lanes_of[0], 1, 0) * grad_ref[...].astype(F32)).astype(BF16)
    out_ref[states : 2 * states] += dot(read_ref[...], lead, 0, 0)
    tail = (dot(here, lanes_of[1], 1, 0) * inputs_ref[...].astype(F32)).astype(BF16)
    out_ref[0:states] += dot(write_ref[...], tail, 0, 0)


def totals(inputs, grad_out, log_decay, write_keys, read_keys):
    length, lanes = inputs.shape
    heads = log_decay.shape[0]
    states = write_keys.shape[1]
    wide = pl.BlockSpec((STEP, lanes), lambda c: (c, 0))
    keys = pl.BlockSpec((STEP, states), lambda c: (c, 0))
    return pl.pallas_call(
        totals_kernel,
        out_shape=jax.ShapeDtypeStruct((2 * states + 8, lanes), F32),
        grid=(length // STEP,),
        in_specs=[wide, wide, pl.BlockSpec((heads, length), lambda c: (0, 0)), keys, keys],
        out_specs=pl.BlockSpec((2 * states + 8, lanes), lambda c: (0, 0)),
        scratch_shapes=[
            pltpu.VMEM((length, 128), BF16),
            pltpu.VMEM((2, 128, lanes), BF16),
        ],
        compiler_params=pltpu.CompilerParams(vmem_limit_bytes=VMEM_BYTES),
        cost_estimate=pl.CostEstimate(
            flops=6 * length * lanes * states, bytes_accessed=4 * length * lanes, transcendentals=0
        ),
        name="totals",
    )(inputs, grad_out, log_decay, write_keys, read_keys)


def factors_kernel(ld_ref, near_ref, rows_ref, decays_ref, ranges_ref):
    heads, length = ld_ref.shape
    count = length // BLOCK
    gain, before, behind = block_factors(ld_ref)
    lead = jnp.exp(before)
    tail = gain * jnp.exp(behind)
    rows_ref[...] = before * LOG2E
    lasts = []
    for c in range(count):
        at = slice(c * BLOCK, c * BLOCK + BLOCK)
        near_ref[at] = in_columns((lead, tail, gain), heads, c)
        lasts.append(lead[c * heads : c * heads + heads, BLOCK - 1 :])
    last = jnp.concatenate(lasts, axis=1)
    decays = dot(jnp.concatenate(three(last), axis=0).astype(BF16), row_spread_matrix(heads), 0, 0)
    decays_ref[...] = decays
    ones = jnp.ones((1, heads * WIDTH), F32)
    after, before = [ones], [ones]
    for c in range(count - 1):
        after.append(after[-1] * decays[c : c + 1])
        before.append(before[-1] * decays[count - 1 - c : count - c])
    ranges_ref[:count] = jnp.concatenate(after, axis=0)
    ranges_ref[count:] = jnp.concatenate(before[::-1], axis=0)


def factors(log_decay):
    heads, length = log_decay.shape
    count = length // BLOCK
    lanes = heads * WIDTH
    return pl.pallas_call(
        factors_kernel,
        out_shape=(
            jax.ShapeDtypeStruct((length, 128), BF16),
            jax.ShapeDtypeStruct((count * heads, BLOCK), F32),
            jax.ShapeDtypeStruct((count, lanes), F32),
            jax.ShapeDtypeStruct((2 * count, lanes), F32),
        ),
        compiler_params=pltpu.CompilerParams(vmem_limit_bytes=VMEM_BYTES),
        cost_estimate=pl.CostEstimate(
            flops=heads * length * 6000, bytes_accessed=1000 * length, transcendentals=0
        ),
        name="factors",
    )(log_decay)


def halves(pair):
    first = iota(pair.shape, 1) < WIDTH
    zero = jnp.zeros_like(pair)
    return jnp.concatenate([jnp.where(first, pair, zero), jnp.where(first, zero, pair)], axis=0)


def lower_block():
    return iota((BLOCK, BLOCK), 0) >= iota((BLOCK, BLOCK), 1)


def key_block(scaled, grad, rows):
    heads = rows.shape[0]
    columns = rows.T
    lower = lower_block()
    gathered = jnp.zeros((BLOCK, BLOCK), F32)
    for pair in range(heads // 2):
        lanes = slice(pair * 128, pair * 128 + 128)
        products = dot(grad[:, lanes], halves(scaled[:, lanes]), 1, 1)
        for j in range(2):
            head = 2 * pair + j
            gap = columns[:, head : head + 1] - rows[head : head + 1, :]
            decay = jnp.exp2(jnp.where(lower, gap, FAR))
            gathered += products[:, j * BLOCK : j * BLOCK + BLOCK] * decay
    return gathered


def two_parts(x):
    high = x.astype(BF16)
    return high, (x - high.astype(F32)).astype(BF16)


def local_kernel(
    plan_ref,
    inputs_ref,
    grad_ref,
    write_ref,
    read_ref,
    parts_ref,
    rows_ref,
    decays_ref,
    ranges_ref,
    entries_ref,
    afters_ref,
    read_terms_ref,
    write_terms_ref,
    far_lead_ref,
    far_tail_ref,
    entry,
    leads,
    tails,
    states_in,
    states_out,
    write_terms,
    lanes_of,
):
    step = pl.program_id(0)
    states, lanes = entry.shape
    heads = lanes // WIDTH
    count = decays_ref.shape[0]
    steps = decays_ref.shape[0] * BLOCK // STEP
    inner = STEP // BLOCK

    @pl.when(step == 0)
    def _():
        for k in range(3):
            lanes_of[k] = spread_matrix(heads, k)
        entry[...] = jnp.zeros_like(entry)

    @pl.when(step < steps)
    def _():
        here = parts_ref[...]
        whole = pl.ds(pl.multiple_of(step * STEP, STEP), STEP)
        leads[whole, :] = (dot(here, lanes_of[0], 1, 0) * grad_ref[...].astype(F32)).astype(BF16)
        tails[whole, :] = (dot(here, lanes_of[1], 1, 0) * inputs_ref[...].astype(F32)).astype(BF16)
        entries_ref[...] = entry[...].astype(BF16)
        for k in range(inner):
            block = step * inner + k
            at = pl.ds(pl.multiple_of(block * BLOCK, BLOCK), BLOCK)
            state = entry[...]
            states_in[k * BLOCK : k * BLOCK + BLOCK] = state.astype(BF16)
            entry[...] = state * decays_ref[pl.ds(block, 1), :] + dot(
                write_ref[at, :], tails[at, :], 0, 0
            )

    @pl.when((step == plan_ref[0]) | (step == plan_ref[1]))
    def _():
        scaled = (dot(parts_ref[...], lanes_of[2], 1, 0) * inputs_ref[...].astype(F32)).astype(BF16)
        for k in range(inner):
            inside = slice(k * BLOCK, k * BLOCK + BLOCK)
            block = step * inner + k
            at = pl.ds(pl.multiple_of(block * BLOCK, BLOCK), BLOCK)
            write, read = write_ref[at, :], read_ref[at, :]
            lead, tail = leads[at, :], tails[at, :]
            far_lead_ref[inside] = (lead.astype(F32) * ranges_ref[pl.ds(block, 1), :]).astype(BF16)
            far_tail_ref[inside] = (
                tail.astype(F32) * ranges_ref[pl.ds(count + block, 1), :]
            ).astype(BF16)
            high, low = two_parts(
                key_block(scaled[inside], grad_ref[inside], rows_ref[k * heads : k * heads + heads, :])
            )
            read_terms_ref[inside] = (
                dot(lead, states_in[inside], 1, 1) + dot(high, write, 1, 0) + dot(low, write, 1, 0)
            )
            write_terms[at, :] = dot(high, read, 0, 0) + dot(low, read, 0, 0)

    @pl.when(step == steps)
    def _():
        state = jnp.zeros_like(entry)
        for block in reversed(range(count)):
            at = slice(block * BLOCK, block * BLOCK + BLOCK)
            states_out[at] = state.astype(BF16)
            state = state * decays_ref[block : block + 1] + dot(read_ref[at, :], leads[at], 0, 0)
        for quarter in range(steps):
            last = quarter * STEP + STEP - BLOCK
            afters_ref[quarter * states : quarter * states + states] = states_out[last : last + BLOCK]
        for slot in range(2):
            for k in range(inner):
                place = slot * STEP + k * BLOCK
                at = pl.ds(pl.multiple_of(plan_ref[slot] * STEP + k * BLOCK, BLOCK), BLOCK)
                write_terms_ref[place : place + BLOCK] = write_terms[at, :] + dot(
                    tails[at, :], states_out[at, :], 1, 1
                )


def local(plan, inputs, grad_out, write_keys, read_keys, parts, rows, decays, ranges):
    length, lanes = inputs.shape
    heads = lanes // WIDTH
    states = write_keys.shape[1]
    assert states == BLOCK and 6 * heads <= 128
    steps = length // STEP

    def forth(c, plan):
        return jnp.minimum(c, steps - 1)

    def slot_forth(c, plan):
        return jnp.where(c > plan[0], 1, 0)

    def all_of(c, plan):
        return 0

    def whole(x):
        return pl.BlockSpec(x.shape, lambda c, plan: (0, 0))

    def tokens(at, size, width):
        return pl.BlockSpec((size, width), lambda c, plan: (at(c, plan), 0))

    return pl.pallas_call(
        local_kernel,
        out_shape=(
            jax.ShapeDtypeStruct((steps * states, lanes), BF16),
            jax.ShapeDtypeStruct((steps * states, lanes), BF16),
            jax.ShapeDtypeStruct((2 * STEP, states), F32),
            jax.ShapeDtypeStruct((2 * STEP, states), F32),
            jax.ShapeDtypeStruct((2 * STEP, lanes), BF16),
            jax.ShapeDtypeStruct((2 * STEP, lanes), BF16),
        ),
        grid_spec=pltpu.PrefetchScalarGridSpec(
            num_scalar_prefetch=1,
            grid=(steps + 1,),
            in_specs=[
                tokens(forth, STEP, lanes),
                tokens(forth, STEP, lanes),
                whole(write_keys),
                whole(read_keys),
                tokens(forth, STEP, 128),
                tokens(forth, STEP // BLOCK * heads, BLOCK),
                whole(decays),
                whole(ranges),
            ],
            out_specs=(
                tokens(forth, states, lanes),
                tokens(all_of, steps * states, lanes),
                tokens(slot_forth, STEP, states),
                tokens(all_of, 2 * STEP, states),
                tokens(slot_forth, STEP, lanes),
                tokens(slot_forth, STEP, lanes),
            ),
            scratch_shapes=[
                pltpu.VMEM((states, lanes), F32),
                pltpu.VMEM((length, lanes), BF16),
                pltpu.VMEM((length, lanes), BF16),
                pltpu.VMEM((STEP, lanes), BF16),
                pltpu.VMEM((length, lanes), BF16),
                pltpu.VMEM((length, states), F32),
                pltpu.VMEM((3, 128, lanes), BF16),
            ],
        ),
        compiler_params=pltpu.CompilerParams(vmem_limit_bytes=VMEM_BYTES),
        cost_estimate=pl.CostEstimate(
            flops=24 * length * lanes * states, bytes_accessed=8 * length * lanes, transcendentals=0
        ),
        name="local",
    )(plan, inputs, grad_out, write_keys, read_keys, parts, rows, decays, ranges)


def early_grads_kernel(
    plan_ref,
    lead_ref,
    tail_ref,
    read_terms_ref,
    write_terms_ref,
    own_ref,
    others_ref,
    other_ref,
    entry_ref,
    after_ref,
    far_ref,
    crossed_ref,
    halved,
):
    step = pl.program_id(0)
    states, lanes = entry_ref.shape
    part = states // 2

    @pl.when(step == 0)
    def _():
        first = plan_ref[4] == 1
        own, others = own_ref[...], others_ref[...]
        top, bottom = jnp.where(first, own, others), jnp.where(first, others, own)
        entry = jnp.concatenate([top[:part], bottom[:part]], axis=0)
        after = jnp.concatenate([top[part:], bottom[part:]], axis=0)
        decay = other_ref[2 * states : 2 * states + 1]
        entry = jnp.where(first, entry, other_ref[:states] + decay * entry)
        after = jnp.where(first, other_ref[states : 2 * states] + decay * after, after)
        entry_ref[...] = entry
        after_ref[...] = after
        halved[0] = entry.astype(BF16)
        halved[1] = after.astype(BF16)

    read = read_terms_ref[...] + dot(lead_ref[...], halved[0], 1, 1)
    write = write_terms_ref[...] + dot(tail_ref[...], halved[1], 1, 1)
    for at, out in ((plan_ref[5], far_ref), (1 - plan_ref[5], crossed_ref)):

        @pl.when(step == at)
        def _():
            out[:, :states] = read
            out[:, states:] = write


def early_grads(plan, lead, tail, read_terms, write_terms, own, others, other):
    lanes = lead.shape[1]
    states = read_terms.shape[1]

    def tokens(width):
        return pl.BlockSpec((STEP, width), lambda c, plan: (c, 0))

    def whole(x):
        return pl.BlockSpec(x.shape, lambda c, plan: (0, 0))

    state = jax.ShapeDtypeStruct((states, lanes), F32)
    terms = jax.ShapeDtypeStruct((STEP, 2 * states), F32)
    shapes = (state, state, terms, terms)
    return pl.pallas_call(
        early_grads_kernel,
        out_shape=shapes,
        grid_spec=pltpu.PrefetchScalarGridSpec(
            num_scalar_prefetch=1,
            grid=(2,),
            in_specs=[
                tokens(lanes),
                tokens(lanes),
                tokens(states),
                tokens(states),
                whole(own),
                whole(others),
                whole(other),
            ],
            out_specs=tuple(whole(x) for x in shapes),
            scratch_shapes=[pltpu.VMEM((2, states, lanes), BF16)],
        ),
        compiler_params=pltpu.CompilerParams(vmem_limit_bytes=VMEM_BYTES),
        cost_estimate=pl.CostEstimate(
            flops=8 * STEP * lanes * states, bytes_accessed=8 * STEP * lanes, transcendentals=0
        ),
        name="early_grads",
    )(plan, lead, tail, read_terms, write_terms, own, others, other)


def combine_kernel(place_ref, *refs):
    *got, out_ref = refs
    place = place_ref[0]
    part, lanes = got[0].shape[0] - 8, got[0].shape[1]
    entry = jnp.zeros((part, lanes), F32)
    after = jnp.zeros((part, lanes), F32)
    for m, value in enumerate(got, 1):
        source = place ^ m
        weight = jnp.ones((1, lanes), F32)
        for k, between in enumerate(got, 1):
            middle = place ^ k
            inside = ((source < middle) & (middle < place)) | ((place < middle) & (middle < source))
            weight = weight * jnp.where(inside, between[part : part + 1], 1.0)
        term = weight * value[:part]
        entry = entry + jnp.where(source < place, term, 0.0)
        after = after + jnp.where(source > place, term, 0.0)
    out_ref[:part] = entry
    out_ref[part:] = after


def combine(place, got):
    rows, lanes = got[0].shape
    return pl.pallas_call(
        combine_kernel,
        out_shape=jax.ShapeDtypeStruct((2 * (rows - 8), lanes), F32),
        in_specs=[pl.BlockSpec(memory_space=pltpu.SMEM)]
        + [pl.BlockSpec(memory_space=pltpu.VMEM)] * len(got),
        out_specs=pl.BlockSpec(memory_space=pltpu.VMEM),
        compiler_params=pltpu.CompilerParams(vmem_limit_bytes=VMEM_BYTES),
        cost_estimate=pl.CostEstimate(
            flops=4 * len(got) * rows * lanes,
            bytes_accessed=4 * (len(got) + 2) * rows * lanes,
            transcendentals=0,
        ),
        name="combine",
    )(place.reshape(1), *got)


def outputs_kernel(
    offset,
    with_terms,
    aliased,
    plan_ref,
    inputs_ref,
    grad_ref,
    write_ref,
    read_ref,
    entries_ref,
    afters_ref,
    parts_ref,
    rows_ref,
    decays_ref,
    ranges_ref,
    entry_ref,
    after_ref,
    skip_ref,
    *rest,
):
    mixed_ref, grad_in_ref, *terms, lanes_of, states_in, states_out, skip_row = rest[aliased:]
    step = pl.program_id(0)
    states = write_ref.shape[1]
    heads = skip_ref.shape[1]
    count = ranges_ref.shape[0] // 2
    inner = STEP // BLOCK

    @pl.when(step == 0)
    def _():
        for k in range(3):
            lanes_of[k] = spread_matrix(heads, k)
        gains = jnp.concatenate(three(jnp.broadcast_to(skip_ref[...], (8, heads))), axis=1)
        skip_row[...] = dot(gains.astype(BF16), row_spread_matrix(heads), 1, 0)

    leads, tails, gains = [dot(parts_ref[...], lanes_of[k], 1, 0) for k in range(3)]
    scaled = (gains * inputs_ref[...].astype(F32)).astype(BF16)
    lead = (leads * grad_ref[...].astype(F32)).astype(BF16)
    tail = (tails * inputs_ref[...].astype(F32)).astype(BF16)
    start = plan_ref[offset + step] * inner
    state = entries_ref[...].astype(F32) + ranges_ref[pl.ds(start, 1), :] * entry_ref[...]
    for k in range(inner):
        at = slice(k * BLOCK, k * BLOCK + BLOCK)
        states_in[at] = state.astype(BF16)
        if k < inner - 1:
            state = state * decays_ref[pl.ds(start + k, 1), :] + dot(write_ref[at, :], tail[at], 0, 0)
    end = start + inner - 1
    state = afters_ref[...].astype(F32) + ranges_ref[pl.ds(count + end, 1), :] * after_ref[...]
    for k in reversed(range(inner)):
        at = slice(k * BLOCK, k * BLOCK + BLOCK)
        states_out[at] = state.astype(BF16)
        if k > 0:
            state = state * decays_ref[pl.ds(start + k, 1), :] + dot(read_ref[at, :], lead[at], 0, 0)
    found = []
    for k in range(inner):
        at = slice(k * BLOCK, k * BLOCK + BLOCK)
        write, read = write_ref[at, :], read_ref[at, :]
        grad = grad_ref[at]
        entry, after = states_in[at], states_out[at]
        skip = skip_row[0:1]
        out_rest = leads[at] * dot(read, entry, 1, 0) + skip * inputs_ref[at].astype(F32)
        back_rest = tails[at] * dot(write, after, 1, 0) + skip * grad.astype(F32)
        scores = dot(read, write, 1, 1)
        rows = rows_ref[k * heads : k * heads + heads, :]
        columns = rows.T
        lower = lower_block()
        gathered = jnp.zeros((BLOCK, BLOCK), F32)
        for pair in range(heads // 2):
            lanes = slice(pair * 128, pair * 128 + 128)
            scaled_pair = halves(scaled[at, lanes])
            if with_terms:
                products = dot(grad[:, lanes], scaled_pair, 1, 1)
            mixing = []
            for j in range(2):
                head = 2 * pair + j
                gap = columns[:, head : head + 1] - rows[head : head + 1, :]
                decay = jnp.exp2(jnp.where(lower, gap, FAR))
                mixing.append((scores * decay).astype(BF16))
                if with_terms:
                    gathered += products[:, j * BLOCK : j * BLOCK + BLOCK] * decay
            mixed = dot(jnp.concatenate(mixing, axis=1), scaled_pair, 1, 0)
            mixed_ref[at, lanes] = (mixed + out_rest[:, lanes]).astype(BF16)
            back = dot(jnp.concatenate(mixing, axis=0), halves(grad[:, lanes]), 0, 0)
            grad_in_ref[at, lanes] = (gains[at, lanes] * back + back_rest[:, lanes]).astype(BF16)
        if with_terms:
            high, low = two_parts(gathered)
            found.append(
                (
                    dot(lead[at], entry, 1, 1) + dot(high, write, 1, 0) + dot(low, write, 1, 0),
                    dot(tail[at], after, 1, 1) + dot(high, read, 0, 0) + dot(low, read, 0, 0),
                )
            )
    for n, out in enumerate(terms):

        @pl.when(step == n)
        def _():
            for k, (for_read, for_write) in enumerate(found):
                out[k * BLOCK : k * BLOCK + BLOCK, :states] = for_read
                out[k * BLOCK : k * BLOCK + BLOCK, states:] = for_write


def outputs(
    plan, offset, steps, with_terms, earlier, inputs, grad_out, write_keys, read_keys, made, entry, after, skip
):
    length, lanes = inputs.shape
    states = write_keys.shape[1]
    entries, afters, parts, rows, decays, ranges = made
    heads = lanes // WIDTH

    def tokens(size, width):
        return pl.BlockSpec((size, width), lambda c, plan: (plan[offset + c], 0))

    def whole(x):
        return pl.BlockSpec(x.shape, lambda c, plan: (0, 0))

    wide = tokens(STEP, lanes)
    shape = jax.ShapeDtypeStruct((length, lanes), BF16)
    terms = (jax.ShapeDtypeStruct((STEP, 2 * states), F32),) * (steps * with_terms)
    return pl.pallas_call(
        functools.partial(outputs_kernel, offset, with_terms, len(earlier)),
        out_shape=(shape, shape, *terms),
        grid_spec=pltpu.PrefetchScalarGridSpec(
            num_scalar_prefetch=1,
            grid=(steps,),
            in_specs=[
                wide,
                wide,
                tokens(STEP, states),
                tokens(STEP, states),
                tokens(states, lanes),
                tokens(states, lanes),
                tokens(STEP, 128),
                tokens(STEP // BLOCK * heads, BLOCK),
                whole(decays),
                whole(ranges),
                whole(entry),
                whole(after),
                whole(skip),
                *[pl.BlockSpec(memory_space=pl.ANY) for _ in earlier],
            ],
            out_specs=(wide, wide, *[whole(x) for x in terms]),
            scratch_shapes=[
                pltpu.VMEM((3, 128, lanes), BF16),
                pltpu.VMEM((STEP, lanes), BF16),
                pltpu.VMEM((STEP, lanes), BF16),
                pltpu.VMEM((8, lanes), F32),
            ],
        ),
        input_output_aliases={14 + k: k for k in range(len(earlier))},
        compiler_params=pltpu.CompilerParams(vmem_limit_bytes=VMEM_BYTES),
        cost_estimate=pl.CostEstimate(
            flops=16 * steps * STEP * lanes * states, bytes_accessed=12 * steps * STEP * lanes, transcendentals=0
        ),
        name="outputs_and_terms" if with_terms else "outputs",
    )(
        plan, inputs, grad_out, write_keys, read_keys, entries, afters, parts, rows, decays, ranges,
        entry, after, skip, *earlier,
    )


def carried_states(summed, states, first_window, second_window):
    axes = ("outer", "inner")
    devices = lax.axis_size(axes)
    here = lax.axis_index(axes)
    first = lax.rem(here, 2) == 0
    place = here // 2
    part = states // 2
    other = lax.ppermute(summed, axes, [(d, d ^ 1) for d in range(devices)])
    other, made = first_window(other)
    early_decay = jnp.where(first, summed, other)[2 * states : 2 * states + 1]
    late_decay = jnp.where(first, other, summed)[2 * states : 2 * states + 1]
    row = jnp.where(first, 0, part)

    def mine(x, start):
        return lax.dynamic_slice_in_dim(x, start + row, part, 0)

    early_push = jnp.where(first, mine(summed, 0), mine(other, 0))
    late_push = jnp.where(first, mine(other, 0), mine(summed, 0))
    early_pull = jnp.where(first, mine(summed, states), mine(other, states))
    late_pull = jnp.where(first, mine(other, states), mine(summed, states))
    push = late_push + late_decay * early_push
    pull = early_pull + early_decay * late_pull
    decay = jnp.broadcast_to(early_decay * late_decay, (8, summed.shape[1]))
    got = []
    for m in range(1, devices // 2):
        sent = jnp.concatenate([jnp.where(place < (place ^ m), push, pull), decay], axis=0)
        got.append(lax.ppermute(sent, axes, [(d, d ^ (2 * m)) for d in range(devices)]))
    got, made = second_window(got, made)
    own = combine(place, got)
    others = lax.ppermute(own, axes, [(d, d ^ 1) for d in range(devices)])
    return (own, others, other), made


def on_device(inputs, log_decay, write_keys, read_keys, skip_gain, grad_out):
    states = write_keys.shape[1]
    line = lax.axis_size("mp") == 4
    assert inputs.shape[0] == 4 * STEP

    at = lax.axis_index("mp")
    ends = (at == 0) | (at == 3)

    def of(*values):
        if not line:
            return jnp.int32(values[0])
        return sum(jnp.where(at == k, v, 0) for k, v in enumerate(values)).astype(jnp.int32)

    even = (lax.rem(lax.axis_index(("outer", "inner")), 2) == 0).astype(jnp.int32)
    plan = jnp.stack(
        [
            of(2, 0, 1, 0),
            of(3, 2, 3, 1),
            of(1, 3, 0, 2),
            of(0, 1, 2, 3),
            even,
            of(1, 0, 1, 0),
        ]
    )
    summed = totals(inputs, grad_out, log_decay, write_keys, read_keys)

    def first_window(other):
        ordered, _ = lax.optimization_barrier((log_decay, summed))
        return lax.optimization_barrier((other, factors(ordered)))

    def second_window(got, made):
        parts, rows, decays, ranges = made
        found = local(plan, inputs, grad_out, write_keys, read_keys, parts, rows, decays, ranges)
        return lax.optimization_barrier((got, (found, made)))

    given, made = carried_states(summed, states, first_window, second_window)
    (entries, afters, read_terms, write_terms, lead, tail), made = made
    entry, after, far, crossed = early_grads(plan, lead, tail, read_terms, write_terms, *given)

    def part(offset, steps, with_terms, earlier):
        return outputs(
            plan, offset, steps, with_terms, earlier, inputs, grad_out, write_keys, read_keys,
            (entries, afters, *made), entry, after, skip_gain[None],
        )

    if not line:
        *results, third, own = part(2, 2, True, ())
        results = part(0, 2, False, results)
        terms = jnp.concatenate([own, third, crossed, far], axis=0)
        own = lax.psum_scatter(terms, "mp", scatter_dimension=0, tiled=True)
        return *results, own[:, states:], own[:, :states]

    two_away = lax.ppermute(crossed, "mp", [(0, 2), (3, 1)])
    far_sum = lax.ppermute(far, "mp", [(0, 1), (1, 0), (2, 3), (3, 2)])
    middle = lax.ppermute(crossed, "mp", [(1, 2), (2, 1)])
    (*results, third, own), far_sum, two_away, middle = lax.optimization_barrier(
        (part(2, 2, True, ()), far_sum, two_away, middle)
    )
    came = jnp.where(ends, 0.0, far_sum)
    last = lax.ppermute(third + came, "mp", [(0, 1), (1, 3), (3, 2), (2, 0)])
    own = own + (far_sum - came) + middle + two_away
    results, own, last = lax.optimization_barrier((part(0, 2, False, results), own, last))
    total = own + last
    return *results, total[:, states:], total[:, :states]


def solution(mesh):
    tokens = ("outer", "inner")
    return jax.shard_map(
        on_device,
        mesh=mesh,
        in_specs=(
            P(tokens, "mp"),
            P("mp", tokens),
            P(tokens, None),
            P(tokens, None),
            P("mp"),
            P(tokens, "mp"),
        ),
        out_specs=(
            P(tokens, "mp"),
            P(tokens, "mp"),
            P(("outer", "inner", "mp"), None),
            P(("outer", "inner", "mp"), None),
        ),
        check_vma=False,
    )
```

```python
import functools

import jax
import jax.numpy as jnp
from jax import lax
from jax.experimental import pallas as pl
from jax.experimental.pallas import tpu as pltpu
from jax.sharding import PartitionSpec as P

WIDTH = 64
BLOCK = 128
STEP = 512
FAR = -1e30
LOG2E = 1.4426950408889634
VMEM_BYTES = 60 * 1024 * 1024
F32 = jnp.float32
BF16 = jnp.bfloat16


def dot(a, b, over_a, over_b):
    return lax.dot_general(a, b, (((over_a,), (over_b,)), ((), ())), preferred_element_type=F32)


def minus_expm1(y):
    series = 1.0 + y * (1.0 / 9.0)
    for k in (8.0, 7.0, 6.0, 5.0, 4.0, 3.0, 2.0):
        series = 1.0 + y * (1.0 / k) * series
    return jnp.where(y > -0.4, -y * series, 1.0 - jnp.exp(y))


def iota(shape, dimension):
    return lax.broadcasted_iota(jnp.int32, shape, dimension)


def spread_matrix(heads, group):
    shape = (128, heads * WIDTH)
    row = iota(shape, 0) - 2 * heads * group
    gap = iota(shape, 1) - WIDTH * jnp.where(row < heads, row, row - heads)
    inside = (row >= 0) & (row < 2 * heads) & (gap >= 0) & (gap < WIDTH)
    return jnp.where(inside, 1.0, 0.0).astype(BF16)


def row_spread_matrix(heads):
    shape = (heads, heads * WIDTH)
    gap = iota(shape, 1) - WIDTH * iota(shape, 0)
    one = jnp.where((gap >= 0) & (gap < WIDTH), 1.0, 0.0)
    return jnp.concatenate([one, one, one], axis=0).astype(BF16)


def three(x):
    high = x.astype(BF16).astype(F32)
    middle = (x - high).astype(BF16).astype(F32)
    return high, middle, x - high - middle


def block_sums(rows):
    shape = (BLOCK, 2 * BLOCK)
    source, target = iota(shape, 0), iota(shape, 1)
    upto = jnp.where(source <= target, 1.0, 0.0)
    beyond = jnp.where(source > target - BLOCK, 1.0, 0.0)
    within = jnp.where(target < BLOCK, upto, beyond).astype(BF16)
    count = rows.shape[0]
    both = dot(jnp.concatenate(three(rows), axis=0).astype(BF16), within, 1, 0)
    both = both[:count] + both[count : 2 * count] + both[2 * count :]
    return both[:, :BLOCK], both[:, BLOCK:]


def stacked(x):
    return jnp.concatenate(
        [x[:, at : at + BLOCK] for at in range(0, x.shape[1], BLOCK)], axis=0
    )


def block_factors(ld_ref):
    ld = ld_ref[...]
    gain = stacked(jnp.sqrt(minus_expm1(2.0 * ld)))
    before, behind = block_sums(stacked(ld))
    return gain, before, behind


def in_columns(groups, heads, block):
    parts = []
    for factor in groups:
        rows = factor[block * heads : block * heads + heads]
        high = rows.astype(BF16).astype(F32)
        parts += [high, rows - high]
    parts.append(jnp.zeros((128 - 2 * heads * len(groups), BLOCK), F32))
    rows = jnp.concatenate(parts, axis=0).astype(BF16)
    eye = jnp.where(iota((BLOCK, BLOCK), 0) == iota((BLOCK, BLOCK), 1), 1.0, 0.0).astype(BF16)
    return dot(eye, rows, 1, 1).astype(BF16)


def starts_and_ends(before, heads, count):
    totals = [before[c * heads : c * heads + heads, BLOCK - 1 :] for c in range(count)]
    start = [jnp.zeros((heads, 1), F32)]
    for total in totals:
        start.append(start[-1] + total)
    end = [jnp.zeros((heads, 1), F32)]
    for total in totals[::-1]:
        end.append(end[-1] + total)
    since = jnp.concatenate(start[:count], axis=0)
    until = jnp.concatenate(end[:count][::-1], axis=0)
    return since, until, start[count]


def totals_kernel(
    inputs_ref, grad_ref, ld_ref, write_ref, read_ref, out_ref, parts, lanes_of
):
    step = pl.program_id(0)
    heads = ld_ref.shape[0]
    states = write_ref.shape[1]
    count = ld_ref.shape[1] // BLOCK

    @pl.when(step == 0)
    def _():
        lanes_of[0] = spread_matrix(heads, 0)
        lanes_of[1] = spread_matrix(heads, 1)
        gain, before, behind = block_factors(ld_ref)
        since, until, whole = starts_and_ends(before, heads, count)
        lead = jnp.exp(since + before)
        tail = gain * jnp.exp(until + behind)
        for c in range(count):
            parts[c * BLOCK : c * BLOCK + BLOCK] = in_columns((lead, tail), heads, c)
        out_ref[...] = jnp.zeros_like(out_ref)
        whole = jnp.concatenate(three(jnp.exp(whole)), axis=0)
        whole = jnp.broadcast_to(whole, (3 * heads, 128)).astype(BF16)
        out_ref[2 * states :] = dot(whole, row_spread_matrix(heads), 0, 0)[0:8]

    at = pl.ds(pl.multiple_of(step * STEP, STEP), STEP)
    here = parts[at, :]
    lead = (dot(here, lanes_of[0], 1, 0) * grad_ref[...].astype(F32)).astype(BF16)
    out_ref[states : 2 * states] += dot(read_ref[...], lead, 0, 0)
    tail = (dot(here, lanes_of[1], 1, 0) * inputs_ref[...].astype(F32)).astype(BF16)
    out_ref[0:states] += dot(write_ref[...], tail, 0, 0)


def totals(inputs, grad_out, log_decay, write_keys, read_keys):
    length, lanes = inputs.shape
    heads = log_decay.shape[0]
    states = write_keys.shape[1]
    wide = pl.BlockSpec((STEP, lanes), lambda c: (c, 0))
    keys = pl.BlockSpec((STEP, states), lambda c: (c, 0))
    return pl.pallas_call(
        totals_kernel,
        out_shape=jax.ShapeDtypeStruct((2 * states + 8, lanes), F32),
        grid=(length // STEP,),
        in_specs=[wide, wide, pl.BlockSpec((heads, length), lambda c: (0, 0)), keys, keys],
        out_specs=pl.BlockSpec((2 * states + 8, lanes), lambda c: (0, 0)),
        scratch_shapes=[
            pltpu.VMEM((length, 128), BF16),
            pltpu.VMEM((2, 128, lanes), BF16),
        ],
        compiler_params=pltpu.CompilerParams(vmem_limit_bytes=48 * 1024 * 1024),
        cost_estimate=pl.CostEstimate(
            flops=6 * length * lanes * states, bytes_accessed=4 * length * lanes, transcendentals=0
        ),
        name="totals",
    )(inputs, grad_out, log_decay, write_keys, read_keys)


def factors_kernel(ld_ref, near_ref, rows_ref, decays_ref, ranges_ref):
    heads, length = ld_ref.shape
    count = length // BLOCK
    gain, before, behind = block_factors(ld_ref)
    lead = jnp.exp(before)
    tail = gain * jnp.exp(behind)
    rows_ref[...] = before * LOG2E
    lasts = []
    for c in range(count):
        at = slice(c * BLOCK, c * BLOCK + BLOCK)
        near_ref[at] = in_columns((lead, tail, gain), heads, c)
        lasts.append(lead[c * heads : c * heads + heads, BLOCK - 1 :])
    last = jnp.concatenate(lasts, axis=1)
    decays = dot(jnp.concatenate(three(last), axis=0).astype(BF16), row_spread_matrix(heads), 0, 0)
    decays_ref[...] = decays
    ones = jnp.ones((1, heads * WIDTH), F32)
    after, before = [ones], [ones]
    for c in range(count - 1):
        after.append(after[-1] * decays[c : c + 1])
        before.append(before[-1] * decays[count - 1 - c : count - c])
    ranges_ref[:count] = jnp.concatenate(after, axis=0)
    ranges_ref[count:] = jnp.concatenate(before[::-1], axis=0)


def factors(log_decay):
    heads, length = log_decay.shape
    count = length // BLOCK
    lanes = heads * WIDTH
    return pl.pallas_call(
        factors_kernel,
        out_shape=(
            jax.ShapeDtypeStruct((length, 128), BF16),
            jax.ShapeDtypeStruct((count * heads, BLOCK), F32),
            jax.ShapeDtypeStruct((count, lanes), F32),
            jax.ShapeDtypeStruct((2 * count, lanes), F32),
        ),
        compiler_params=pltpu.CompilerParams(vmem_limit_bytes=48 * 1024 * 1024),
        cost_estimate=pl.CostEstimate(
            flops=heads * length * 6000, bytes_accessed=1000 * length, transcendentals=0
        ),
        name="factors",
    )(log_decay)


def halves(pair):
    first = iota(pair.shape, 1) < WIDTH
    zero = jnp.zeros_like(pair)
    return jnp.concatenate([jnp.where(first, pair, zero), jnp.where(first, zero, pair)], axis=0)


def lower_block():
    return iota((BLOCK, BLOCK), 0) >= iota((BLOCK, BLOCK), 1)


def key_block(scaled, grad, rows):
    heads = rows.shape[0]
    columns = rows.T
    lower = lower_block()
    gathered = jnp.zeros((BLOCK, BLOCK), F32)
    for pair in range(heads // 2):
        lanes = slice(pair * 128, pair * 128 + 128)
        products = dot(grad[:, lanes], halves(scaled[:, lanes]), 1, 1)
        for j in range(2):
            head = 2 * pair + j
            gap = columns[:, head : head + 1] - rows[head : head + 1, :]
            decay = jnp.exp2(jnp.where(lower, gap, FAR))
            gathered += products[:, j * BLOCK : j * BLOCK + BLOCK] * decay
    return gathered


def two_parts(x):
    high = x.astype(BF16)
    return high, (x - high.astype(F32)).astype(BF16)


def local_kernel(
    plan_ref,
    inputs_ref,
    grad_ref,
    write_ref,
    read_ref,
    parts_ref,
    rows_ref,
    decays_ref,
    ranges_ref,
    entries_ref,
    afters_ref,
    read_terms_ref,
    write_terms_ref,
    far_lead_ref,
    far_tail_ref,
    entry,
    leads,
    tails,
    states_in,
    states_out,
    write_terms,
    lanes_of,
):
    step = pl.program_id(0)
    states, lanes = entry.shape
    heads = lanes // WIDTH
    count = decays_ref.shape[0]
    steps = decays_ref.shape[0] * BLOCK // STEP
    inner = STEP // BLOCK

    @pl.when(step == 0)
    def _():
        for k in range(3):
            lanes_of[k] = spread_matrix(heads, k)
        entry[...] = jnp.zeros_like(entry)

    @pl.when(step < steps)
    def _():
        here = parts_ref[...]
        whole = pl.ds(pl.multiple_of(step * STEP, STEP), STEP)
        leads[whole, :] = (dot(here, lanes_of[0], 1, 0) * grad_ref[...].astype(F32)).astype(BF16)
        tails[whole, :] = (dot(here, lanes_of[1], 1, 0) * inputs_ref[...].astype(F32)).astype(BF16)
        entries_ref[...] = entry[...].astype(BF16)
        for k in range(inner):
            block = step * inner + k
            at = pl.ds(pl.multiple_of(block * BLOCK, BLOCK), BLOCK)
            state = entry[...]
            states_in[k * BLOCK : k * BLOCK + BLOCK] = state.astype(BF16)
            entry[...] = state * decays_ref[pl.ds(block, 1), :] + dot(
                write_ref[at, :], tails[at, :], 0, 0
            )

    @pl.when((step == plan_ref[0]) | (step == plan_ref[1]))
    def _():
        scaled = (dot(parts_ref[...], lanes_of[2], 1, 0) * inputs_ref[...].astype(F32)).astype(BF16)
        for k in range(inner):
            inside = slice(k * BLOCK, k * BLOCK + BLOCK)
            block = step * inner + k
            at = pl.ds(pl.multiple_of(block * BLOCK, BLOCK), BLOCK)
            write, read = write_ref[at, :], read_ref[at, :]
            lead, tail = leads[at, :], tails[at, :]
            far_lead_ref[inside] = (lead.astype(F32) * ranges_ref[pl.ds(block, 1), :]).astype(BF16)
            far_tail_ref[inside] = (
                tail.astype(F32) * ranges_ref[pl.ds(count + block, 1), :]
            ).astype(BF16)
            high, low = two_parts(
                key_block(scaled[inside], grad_ref[inside], rows_ref[k * heads : k * heads + heads, :])
            )
            read_terms_ref[inside] = (
                dot(lead, states_in[inside], 1, 1) + dot(high, write, 1, 0) + dot(low, write, 1, 0)
            )
            write_terms[at, :] = dot(high, read, 0, 0) + dot(low, read, 0, 0)

    @pl.when(step == steps)
    def _():
        state = jnp.zeros_like(entry)
        for block in reversed(range(count)):
            at = slice(block * BLOCK, block * BLOCK + BLOCK)
            states_out[at] = state.astype(BF16)
            state = state * decays_ref[block : block + 1] + dot(read_ref[at, :], leads[at], 0, 0)
        for quarter in range(steps):
            last = quarter * STEP + STEP - BLOCK
            afters_ref[quarter * states : quarter * states + states] = states_out[last : last + BLOCK]
        for slot in range(2):
            for k in range(inner):
                place = slot * STEP + k * BLOCK
                at = pl.ds(pl.multiple_of(plan_ref[slot] * STEP + k * BLOCK, BLOCK), BLOCK)
                write_terms_ref[place : place + BLOCK] = write_terms[at, :] + dot(
                    tails[at, :], states_out[at, :], 1, 1
                )


def local(plan, inputs, grad_out, write_keys, read_keys, parts, rows, decays, ranges):
    length, lanes = inputs.shape
    heads = lanes // WIDTH
    states = write_keys.shape[1]
    assert states == BLOCK and 6 * heads <= 128
    steps = length // STEP

    def forth(c, plan):
        return jnp.minimum(c, steps - 1)

    def slot_forth(c, plan):
        return jnp.where(c > plan[0], 1, 0)

    def all_of(c, plan):
        return 0

    def whole(x):
        return pl.BlockSpec(x.shape, lambda c, plan: (0, 0))

    def tokens(at, size, width):
        return pl.BlockSpec((size, width), lambda c, plan: (at(c, plan), 0))

    return pl.pallas_call(
        local_kernel,
        out_shape=(
            jax.ShapeDtypeStruct((steps * states, lanes), BF16),
            jax.ShapeDtypeStruct((steps * states, lanes), BF16),
            jax.ShapeDtypeStruct((2 * STEP, states), F32),
            jax.ShapeDtypeStruct((2 * STEP, states), F32),
            jax.ShapeDtypeStruct((2 * STEP, lanes), BF16),
            jax.ShapeDtypeStruct((2 * STEP, lanes), BF16),
        ),
        grid_spec=pltpu.PrefetchScalarGridSpec(
            num_scalar_prefetch=1,
            grid=(steps + 1,),
            in_specs=[
                tokens(forth, STEP, lanes),
                tokens(forth, STEP, lanes),
                whole(write_keys),
                whole(read_keys),
                tokens(forth, STEP, 128),
                tokens(forth, STEP // BLOCK * heads, BLOCK),
                whole(decays),
                whole(ranges),
            ],
            out_specs=(
                tokens(forth, states, lanes),
                tokens(all_of, steps * states, lanes),
                tokens(slot_forth, STEP, states),
                tokens(all_of, 2 * STEP, states),
                tokens(slot_forth, STEP, lanes),
                tokens(slot_forth, STEP, lanes),
            ),
            scratch_shapes=[
                pltpu.VMEM((states, lanes), F32),
                pltpu.VMEM((length, lanes), BF16),
                pltpu.VMEM((length, lanes), BF16),
                pltpu.VMEM((STEP, lanes), BF16),
                pltpu.VMEM((length, lanes), BF16),
                pltpu.VMEM((length, states), F32),
                pltpu.VMEM((3, 128, lanes), BF16),
            ],
        ),
        compiler_params=pltpu.CompilerParams(vmem_limit_bytes=44 * 1024 * 1024),
        cost_estimate=pl.CostEstimate(
            flops=24 * length * lanes * states, bytes_accessed=8 * length * lanes, transcendentals=0
        ),
        name="local",
    )(plan, inputs, grad_out, write_keys, read_keys, parts, rows, decays, ranges)


def early_grads_kernel(
    plan_ref,
    lead_ref,
    tail_ref,
    read_terms_ref,
    write_terms_ref,
    own_ref,
    others_ref,
    other_ref,
    entry_ref,
    after_ref,
    far_ref,
    crossed_ref,
    halved,
):
    step = pl.program_id(0)
    states, lanes = entry_ref.shape
    part = states // 2

    @pl.when(step == 0)
    def _():
        first = plan_ref[4] == 1
        own, others = own_ref[...], others_ref[...]
        top, bottom = jnp.where(first, own, others), jnp.where(first, others, own)
        entry = jnp.concatenate([top[:part], bottom[:part]], axis=0)
        after = jnp.concatenate([top[part:], bottom[part:]], axis=0)
        decay = other_ref[2 * states : 2 * states + 1]
        entry = jnp.where(first, entry, other_ref[:states] + decay * entry)
        after = jnp.where(first, other_ref[states : 2 * states] + decay * after, after)
        entry_ref[...] = entry
        after_ref[...] = after
        halved[0] = entry.astype(BF16)
        halved[1] = after.astype(BF16)

    read = read_terms_ref[...] + dot(lead_ref[...], halved[0], 1, 1)
    write = write_terms_ref[...] + dot(tail_ref[...], halved[1], 1, 1)
    for at, out in ((plan_ref[5], far_ref), (1 - plan_ref[5], crossed_ref)):

        @pl.when(step == at)
        def _():
            out[:, :states] = read
            out[:, states:] = write


def early_grads(plan, lead, tail, read_terms, write_terms, own, others, other):
    lanes = lead.shape[1]
    states = read_terms.shape[1]

    def tokens(width):
        return pl.BlockSpec((STEP, width), lambda c, plan: (c, 0))

    def whole(x):
        return pl.BlockSpec(x.shape, lambda c, plan: (0, 0))

    state = jax.ShapeDtypeStruct((states, lanes), F32)
    terms = jax.ShapeDtypeStruct((STEP, 2 * states), F32)
    shapes = (state, state, terms, terms)
    return pl.pallas_call(
        early_grads_kernel,
        out_shape=shapes,
        grid_spec=pltpu.PrefetchScalarGridSpec(
            num_scalar_prefetch=1,
            grid=(2,),
            in_specs=[
                tokens(lanes),
                tokens(lanes),
                tokens(states),
                tokens(states),
                whole(own),
                whole(others),
                whole(other),
            ],
            out_specs=tuple(whole(x) for x in shapes),
            scratch_shapes=[pltpu.VMEM((2, states, lanes), BF16)],
        ),
        compiler_params=pltpu.CompilerParams(vmem_limit_bytes=24 * 1024 * 1024),
        cost_estimate=pl.CostEstimate(
            flops=8 * STEP * lanes * states, bytes_accessed=8 * STEP * lanes, transcendentals=0
        ),
        name="early_grads",
    )(plan, lead, tail, read_terms, write_terms, own, others, other)


def combine_kernel(place_ref, *refs):
    *got, out_ref = refs
    place = place_ref[0]
    part, lanes = got[0].shape[0] - 8, got[0].shape[1]
    entry = jnp.zeros((part, lanes), F32)
    after = jnp.zeros((part, lanes), F32)
    for m, value in enumerate(got, 1):
        source = place ^ m
        weight = jnp.ones((1, lanes), F32)
        for k, between in enumerate(got, 1):
            middle = place ^ k
            inside = ((source < middle) & (middle < place)) | ((place < middle) & (middle < source))
            weight = weight * jnp.where(inside, between[part : part + 1], 1.0)
        term = weight * value[:part]
        entry = entry + jnp.where(source < place, term, 0.0)
        after = after + jnp.where(source > place, term, 0.0)
    out_ref[:part] = entry
    out_ref[part:] = after


def combine(place, got):
    rows, lanes = got[0].shape
    return pl.pallas_call(
        combine_kernel,
        out_shape=jax.ShapeDtypeStruct((2 * (rows - 8), lanes), F32),
        in_specs=[pl.BlockSpec(memory_space=pltpu.SMEM)]
        + [pl.BlockSpec(memory_space=pltpu.VMEM)] * len(got),
        out_specs=pl.BlockSpec(memory_space=pltpu.VMEM),
        compiler_params=pltpu.CompilerParams(vmem_limit_bytes=16 * 1024 * 1024),
        cost_estimate=pl.CostEstimate(
            flops=4 * len(got) * rows * lanes,
            bytes_accessed=4 * (len(got) + 2) * rows * lanes,
            transcendentals=0,
        ),
        name="combine",
    )(place.reshape(1), *got)


def outputs_kernel(
    offset,
    with_terms,
    aliased,
    plan_ref,
    inputs_ref,
    grad_ref,
    write_ref,
    read_ref,
    entries_ref,
    afters_ref,
    parts_ref,
    rows_ref,
    decays_ref,
    ranges_ref,
    entry_ref,
    after_ref,
    skip_ref,
    *rest,
):
    mixed_ref, grad_in_ref, *terms, lanes_of, states_in, states_out, skip_row = rest[aliased:]
    step = pl.program_id(0)
    states = write_ref.shape[1]
    heads = skip_ref.shape[1]
    count = ranges_ref.shape[0] // 2
    inner = STEP // BLOCK

    @pl.when(step == 0)
    def _():
        for k in range(3):
            lanes_of[k] = spread_matrix(heads, k)
        gains = jnp.concatenate(three(jnp.broadcast_to(skip_ref[...], (8, heads))), axis=1)
        skip_row[...] = dot(gains.astype(BF16), row_spread_matrix(heads), 1, 0)

    leads, tails, gains = [dot(parts_ref[...], lanes_of[k], 1, 0) for k in range(3)]
    scaled = (gains * inputs_ref[...].astype(F32)).astype(BF16)
    lead = (leads * grad_ref[...].astype(F32)).astype(BF16)
    tail = (tails * inputs_ref[...].astype(F32)).astype(BF16)
    start = plan_ref[offset + step] * inner
    state = entries_ref[...].astype(F32) + ranges_ref[pl.ds(start, 1), :] * entry_ref[...]
    for k in range(inner):
        at = slice(k * BLOCK, k * BLOCK + BLOCK)
        states_in[at] = state.astype(BF16)
        if k < inner - 1:
            state = state * decays_ref[pl.ds(start + k, 1), :] + dot(write_ref[at, :], tail[at], 0, 0)
    end = start + inner - 1
    state = afters_ref[...].astype(F32) + ranges_ref[pl.ds(count + end, 1), :] * after_ref[...]
    for k in reversed(range(inner)):
        at = slice(k * BLOCK, k * BLOCK + BLOCK)
        states_out[at] = state.astype(BF16)
        if k > 0:
            state = state * decays_ref[pl.ds(start + k, 1), :] + dot(read_ref[at, :], lead[at], 0, 0)
    found = []
    for k in range(inner):
        at = slice(k * BLOCK, k * BLOCK + BLOCK)
        write, read = write_ref[at, :], read_ref[at, :]
        grad = grad_ref[at]
        entry, after = states_in[at], states_out[at]
        skip = skip_row[0:1]
        out_rest = leads[at] * dot(read, entry, 1, 0) + skip * inputs_ref[at].astype(F32)
        back_rest = tails[at] * dot(write, after, 1, 0) + skip * grad.astype(F32)
        scores = dot(read, write, 1, 1)
        rows = rows_ref[k * heads : k * heads + heads, :]
        columns = rows.T
        lower = lower_block()
        gathered = jnp.zeros((BLOCK, BLOCK), F32)
        for pair in range(heads // 2):
            lanes = slice(pair * 128, pair * 128 + 128)
            scaled_pair = halves(scaled[at, lanes])
            if with_terms:
                products = dot(grad[:, lanes], scaled_pair, 1, 1)
            mixing = []
            for j in range(2):
                head = 2 * pair + j
                gap = columns[:, head : head + 1] - rows[head : head + 1, :]
                decay = jnp.exp2(jnp.where(lower, gap, FAR))
                mixing.append((scores * decay).astype(BF16))
                if with_terms:
                    gathered += products[:, j * BLOCK : j * BLOCK + BLOCK] * decay
            mixed = dot(jnp.concatenate(mixing, axis=1), scaled_pair, 1, 0)
            mixed_ref[at, lanes] = (mixed + out_rest[:, lanes]).astype(BF16)
            back = dot(jnp.concatenate(mixing, axis=0), halves(grad[:, lanes]), 0, 0)
            grad_in_ref[at, lanes] = (gains[at, lanes] * back + back_rest[:, lanes]).astype(BF16)
        if with_terms:
            high, low = two_parts(gathered)
            found.append(
                (
                    dot(lead[at], entry, 1, 1) + dot(high, write, 1, 0) + dot(low, write, 1, 0),
                    dot(tail[at], after, 1, 1) + dot(high, read, 0, 0) + dot(low, read, 0, 0),
                )
            )
    for n, out in enumerate(terms):

        @pl.when(step == n)
        def _():
            for k, (for_read, for_write) in enumerate(found):
                out[k * BLOCK : k * BLOCK + BLOCK, :states] = for_read
                out[k * BLOCK : k * BLOCK + BLOCK, states:] = for_write


def outputs(
    plan, offset, steps, with_terms, earlier, inputs, grad_out, write_keys, read_keys, made, entry, after, skip
):
    length, lanes = inputs.shape
    states = write_keys.shape[1]
    entries, afters, parts, rows, decays, ranges = made
    heads = lanes // WIDTH

    def tokens(size, width):
        return pl.BlockSpec((size, width), lambda c, plan: (plan[offset + c], 0))

    def whole(x):
        return pl.BlockSpec(x.shape, lambda c, plan: (0, 0))

    wide = tokens(STEP, lanes)
    shape = jax.ShapeDtypeStruct((length, lanes), BF16)
    terms = (jax.ShapeDtypeStruct((STEP, 2 * states), F32),) * (steps * with_terms)
    return pl.pallas_call(
        functools.partial(outputs_kernel, offset, with_terms, len(earlier)),
        out_shape=(shape, shape, *terms),
        grid_spec=pltpu.PrefetchScalarGridSpec(
            num_scalar_prefetch=1,
            grid=(steps,),
            in_specs=[
                wide,
                wide,
                tokens(STEP, states),
                tokens(STEP, states),
                tokens(states, lanes),
                tokens(states, lanes),
                tokens(STEP, 128),
                tokens(STEP // BLOCK * heads, BLOCK),
                whole(decays),
                whole(ranges),
                whole(entry),
                whole(after),
                whole(skip),
                *[pl.BlockSpec(memory_space=pl.ANY) for _ in earlier],
            ],
            out_specs=(wide, wide, *[whole(x) for x in terms]),
            scratch_shapes=[
                pltpu.VMEM((3, 128, lanes), BF16),
                pltpu.VMEM((STEP, lanes), BF16),
                pltpu.VMEM((STEP, lanes), BF16),
                pltpu.VMEM((8, lanes), F32),
            ],
        ),
        input_output_aliases={14 + k: k for k in range(len(earlier))},
        compiler_params=pltpu.CompilerParams(vmem_limit_bytes=VMEM_BYTES),
        cost_estimate=pl.CostEstimate(
            flops=16 * steps * STEP * lanes * states, bytes_accessed=12 * steps * STEP * lanes, transcendentals=0
        ),
        name="outputs_and_terms" if with_terms else "outputs",
    )(
        plan, inputs, grad_out, write_keys, read_keys, entries, afters, parts, rows, decays, ranges,
        entry, after, skip, *earlier,
    )


def carried_states(summed, states, first_window, second_window):
    axes = ("outer", "inner")
    devices = lax.axis_size(axes)
    here = lax.axis_index(axes)
    first = lax.rem(here, 2) == 0
    place = here // 2
    part = states // 2
    other = lax.ppermute(summed, axes, [(d, d ^ 1) for d in range(devices)])
    other, made = first_window(other)
    early_decay = jnp.where(first, summed, other)[2 * states : 2 * states + 1]
    late_decay = jnp.where(first, other, summed)[2 * states : 2 * states + 1]
    row = jnp.where(first, 0, part)

    def mine(x, start):
        return lax.dynamic_slice_in_dim(x, start + row, part, 0)

    early_push = jnp.where(first, mine(summed, 0), mine(other, 0))
    late_push = jnp.where(first, mine(other, 0), mine(summed, 0))
    early_pull = jnp.where(first, mine(summed, states), mine(other, states))
    late_pull = jnp.where(first, mine(other, states), mine(summed, states))
    push = late_push + late_decay * early_push
    pull = early_pull + early_decay * late_pull
    decay = jnp.broadcast_to(early_decay * late_decay, (8, summed.shape[1]))
    got = []
    for m in range(1, devices // 2):
        sent = jnp.concatenate([jnp.where(place < (place ^ m), push, pull), decay], axis=0)
        got.append(lax.ppermute(sent, axes, [(d, d ^ (2 * m)) for d in range(devices)]))
    got, made = second_window(got, made)
    own = combine(place, got)
    others = lax.ppermute(own, axes, [(d, d ^ 1) for d in range(devices)])
    return (own, others, other), made


def on_device(inputs, log_decay, write_keys, read_keys, skip_gain, grad_out):
    states = write_keys.shape[1]
    line = lax.axis_size("mp") == 4
    assert inputs.shape[0] == 4 * STEP

    at = lax.axis_index("mp")
    ends = (at == 0) | (at == 3)

    def of(*values):
        if not line:
            return jnp.int32(values[0])
        return sum(jnp.where(at == k, v, 0) for k, v in enumerate(values)).astype(jnp.int32)

    even = (lax.rem(lax.axis_index(("outer", "inner")), 2) == 0).astype(jnp.int32)
    plan = jnp.stack(
        [
            of(2, 0, 1, 0),
            of(3, 2, 3, 1),
            of(1, 3, 0, 2),
            of(0, 1, 2, 3),
            even,
            of(1, 0, 1, 0),
        ]
    )
    summed = totals(inputs, grad_out, log_decay, write_keys, read_keys)

    def first_window(other):
        ordered, _ = lax.optimization_barrier((log_decay, summed))
        return lax.optimization_barrier((other, factors(ordered)))

    def second_window(got, made):
        parts, rows, decays, ranges = made
        found = local(plan, inputs, grad_out, write_keys, read_keys, parts, rows, decays, ranges)
        return lax.optimization_barrier((got, (found, made)))

    given, made = carried_states(summed, states, first_window, second_window)
    (entries, afters, read_terms, write_terms, lead, tail), made = made
    entry, after, far, crossed = early_grads(plan, lead, tail, read_terms, write_terms, *given)

    def part(offset, steps, with_terms, earlier):
        return outputs(
            plan, offset, steps, with_terms, earlier, inputs, grad_out, write_keys, read_keys,
            (entries, afters, *made), entry, after, skip_gain[None],
        )

    if not line:
        *results, third, own = part(2, 2, True, ())
        results = part(0, 2, False, results)
        terms = jnp.concatenate([own, third, crossed, far], axis=0)
        own = lax.psum_scatter(terms, "mp", scatter_dimension=0, tiled=True)
        return *results, own[:, states:], own[:, :states]

    two_away = lax.ppermute(crossed, "mp", [(0, 2), (3, 1)])
    far_sum = lax.ppermute(far, "mp", [(0, 1), (1, 0), (2, 3), (3, 2)])
    middle = lax.ppermute(crossed, "mp", [(1, 2), (2, 1)])
    (*results, third, own), far_sum, two_away, middle = lax.optimization_barrier(
        (part(2, 2, True, ()), far_sum, two_away, middle)
    )
    came = jnp.where(ends, 0.0, far_sum)
    last = lax.ppermute(third + came, "mp", [(0, 1), (1, 3), (3, 2), (2, 0)])
    own = own + (far_sum - came) + middle + two_away
    results, own, last = lax.optimization_barrier((part(0, 2, False, results), own, last))
    total = own + last
    return *results, total[:, states:], total[:, :states]


def solution(mesh):
    tokens = ("outer", "inner")
    return jax.shard_map(
        on_device,
        mesh=mesh,
        in_specs=(
            P(tokens, "mp"),
            P("mp", tokens),
            P(tokens, None),
            P(tokens, None),
            P("mp"),
            P(tokens, "mp"),
        ),
        out_specs=(
            P(tokens, "mp"),
            P(tokens, "mp"),
            P(("outer", "inner", "mp"), None),
            P(("outer", "inner", "mp"), None),
        ),
        check_vma=False,
    )
```

```python
import functools

import jax
import jax.numpy as jnp
from jax import lax
from jax.experimental import pallas as pl
from jax.experimental.pallas import tpu as pltpu
from jax.sharding import PartitionSpec as P

WIDTH = 64
BLOCK = 128
STEP = 512
FAR = -1e30
LOG2E = 1.4426950408889634
VMEM_BYTES = 60 * 1024 * 1024
F32 = jnp.float32
BF16 = jnp.bfloat16


def dot(a, b, over_a, over_b):
    return lax.dot_general(a, b, (((over_a,), (over_b,)), ((), ())), preferred_element_type=F32)


def minus_expm1(y):
    series = 1.0 + y * (1.0 / 9.0)
    for k in (8.0, 7.0, 6.0, 5.0, 4.0, 3.0, 2.0):
        series = 1.0 + y * (1.0 / k) * series
    return jnp.where(y > -0.4, -y * series, 1.0 - jnp.exp(y))


def iota(shape, dimension):
    return lax.broadcasted_iota(jnp.int32, shape, dimension)


def spread_matrix(heads, group):
    shape = (128, heads * WIDTH)
    row = iota(shape, 0) - 2 * heads * group
    gap = iota(shape, 1) - WIDTH * jnp.where(row < heads, row, row - heads)
    inside = (row >= 0) & (row < 2 * heads) & (gap >= 0) & (gap < WIDTH)
    return jnp.where(inside, 1.0, 0.0).astype(BF16)


def row_spread_matrix(heads):
    shape = (heads, heads * WIDTH)
    gap = iota(shape, 1) - WIDTH * iota(shape, 0)
    one = jnp.where((gap >= 0) & (gap < WIDTH), 1.0, 0.0)
    return jnp.concatenate([one, one, one], axis=0).astype(BF16)


def three(x):
    high = x.astype(BF16).astype(F32)
    middle = (x - high).astype(BF16).astype(F32)
    return high, middle, x - high - middle


def block_sums(rows):
    shape = (BLOCK, 2 * BLOCK)
    source, target = iota(shape, 0), iota(shape, 1)
    upto = jnp.where(source <= target, 1.0, 0.0)
    beyond = jnp.where(source > target - BLOCK, 1.0, 0.0)
    within = jnp.where(target < BLOCK, upto, beyond).astype(BF16)
    count = rows.shape[0]
    both = dot(jnp.concatenate(three(rows), axis=0).astype(BF16), within, 1, 0)
    both = both[:count] + both[count : 2 * count] + both[2 * count :]
    return both[:, :BLOCK], both[:, BLOCK:]


def stacked(x):
    return jnp.concatenate(
        [x[:, at : at + BLOCK] for at in range(0, x.shape[1], BLOCK)], axis=0
    )


def block_factors(ld_ref):
    ld = ld_ref[...]
    gain = stacked(jnp.sqrt(minus_expm1(2.0 * ld)))
    before, behind = block_sums(stacked(ld))
    return gain, before, behind


def in_columns(groups, heads, block):
    parts = []
    for factor in groups:
        rows = factor[block * heads : block * heads + heads]
        high = rows.astype(BF16).astype(F32)
        parts += [high, rows - high]
    parts.append(jnp.zeros((128 - 2 * heads * len(groups), BLOCK), F32))
    rows = jnp.concatenate(parts, axis=0).astype(BF16)
    eye = jnp.where(iota((BLOCK, BLOCK), 0) == iota((BLOCK, BLOCK), 1), 1.0, 0.0).astype(BF16)
    return dot(eye, rows, 1, 1).astype(BF16)


def starts_and_ends(before, heads, count):
    totals = [before[c * heads : c * heads + heads, BLOCK - 1 :] for c in range(count)]
    start = [jnp.zeros((heads, 1), F32)]
    for total in totals:
        start.append(start[-1] + total)
    end = [jnp.zeros((heads, 1), F32)]
    for total in totals[::-1]:
        end.append(end[-1] + total)
    since = jnp.concatenate(start[:count], axis=0)
    until = jnp.concatenate(end[:count][::-1], axis=0)
    return since, until, start[count]


def totals_kernel(
    inputs_ref, grad_ref, ld_ref, write_ref, read_ref, out_ref, parts, lanes_of
):
    step = pl.program_id(0)
    heads = ld_ref.shape[0]
    states = write_ref.shape[1]
    count = ld_ref.shape[1] // BLOCK

    @pl.when(step == 0)
    def _():
        lanes_of[0] = spread_matrix(heads, 0)
        lanes_of[1] = spread_matrix(heads, 1)
        gain, before, behind = block_factors(ld_ref)
        since, until, whole = starts_and_ends(before, heads, count)
        lead = jnp.exp(since + before)
        tail = gain * jnp.exp(until + behind)
        for c in range(count):
            parts[c * BLOCK : c * BLOCK + BLOCK] = in_columns((lead, tail), heads, c)
        out_ref[...] = jnp.zeros_like(out_ref)
        whole = jnp.concatenate(three(jnp.exp(whole)), axis=0)
        whole = jnp.broadcast_to(whole, (3 * heads, 128)).astype(BF16)
        out_ref[2 * states :] = dot(whole, row_spread_matrix(heads), 0, 0)[0:8]

    at = pl.ds(pl.multiple_of(step * STEP, STEP), STEP)
    here = parts[at, :]
    lead = (dot(here, lanes_of[0], 1, 0) * grad_ref[...].astype(F32)).astype(BF16)
    out_ref[states : 2 * states] += dot(read_ref[...], lead, 0, 0)
    tail = (dot(here, lanes_of[1], 1, 0) * inputs_ref[...].astype(F32)).astype(BF16)
    out_ref[0:states] += dot(write_ref[...], tail, 0, 0)


def totals(inputs, grad_out, log_decay, write_keys, read_keys):
    length, lanes = inputs.shape
    heads = log_decay.shape[0]
    states = write_keys.shape[1]
    wide = pl.BlockSpec((STEP, lanes), lambda c: (c, 0))
    keys = pl.BlockSpec((STEP, states), lambda c: (c, 0))
    return pl.pallas_call(
        totals_kernel,
        out_shape=jax.ShapeDtypeStruct((2 * states + 8, lanes), F32),
        grid=(length // STEP,),
        in_specs=[wide, wide, pl.BlockSpec((heads, length), lambda c: (0, 0)), keys, keys],
        out_specs=pl.BlockSpec((2 * states + 8, lanes), lambda c: (0, 0)),
        scratch_shapes=[
            pltpu.VMEM((length, 128), BF16),
            pltpu.VMEM((2, 128, lanes), BF16),
        ],
        compiler_params=pltpu.CompilerParams(vmem_limit_bytes=48 * 1024 * 1024),
        cost_estimate=pl.CostEstimate(
            flops=6 * length * lanes * states, bytes_accessed=4 * length * lanes, transcendentals=0
        ),
        name="totals",
    )(inputs, grad_out, log_decay, write_keys, read_keys)


def factors_kernel(ld_ref, near_ref, rows_ref, decays_ref, ranges_ref):
    heads, length = ld_ref.shape
    count = length // BLOCK
    gain, before, behind = block_factors(ld_ref)
    lead = jnp.exp(before)
    tail = gain * jnp.exp(behind)
    rows_ref[...] = before * LOG2E
    lasts = []
    for c in range(count):
        at = slice(c * BLOCK, c * BLOCK + BLOCK)
        near_ref[at] = in_columns((lead, tail, gain), heads, c)
        lasts.append(lead[c * heads : c * heads + heads, BLOCK - 1 :])
    last = jnp.concatenate(lasts, axis=1)
    decays = dot(jnp.concatenate(three(last), axis=0).astype(BF16), row_spread_matrix(heads), 0, 0)
    decays_ref[...] = decays
    ones = jnp.ones((1, heads * WIDTH), F32)
    after, before = [ones], [ones]
    for c in range(count - 1):
        after.append(after[-1] * decays[c : c + 1])
        before.append(before[-1] * decays[count - 1 - c : count - c])
    ranges_ref[:count] = jnp.concatenate(after, axis=0)
    ranges_ref[count:] = jnp.concatenate(before[::-1], axis=0)


def factors(log_decay):
    heads, length = log_decay.shape
    count = length // BLOCK
    lanes = heads * WIDTH
    return pl.pallas_call(
        factors_kernel,
        out_shape=(
            jax.ShapeDtypeStruct((length, 128), BF16),
            jax.ShapeDtypeStruct((count * heads, BLOCK), F32),
            jax.ShapeDtypeStruct((count, lanes), F32),
            jax.ShapeDtypeStruct((2 * count, lanes), F32),
        ),
        compiler_params=pltpu.CompilerParams(vmem_limit_bytes=48 * 1024 * 1024),
        cost_estimate=pl.CostEstimate(
            flops=heads * length * 6000, bytes_accessed=1000 * length, transcendentals=0
        ),
        name="factors",
    )(log_decay)


def halves(pair):
    first = iota(pair.shape, 1) < WIDTH
    zero = jnp.zeros_like(pair)
    return jnp.concatenate([jnp.where(first, pair, zero), jnp.where(first, zero, pair)], axis=0)


def lower_block():
    return iota((BLOCK, BLOCK), 0) >= iota((BLOCK, BLOCK), 1)


def key_block(scaled, grad, rows):
    heads = rows.shape[0]
    columns = rows.T
    lower = lower_block()
    gathered = jnp.zeros((BLOCK, BLOCK), F32)
    for pair in range(heads // 2):
        lanes = slice(pair * 128, pair * 128 + 128)
        products = dot(grad[:, lanes], halves(scaled[:, lanes]), 1, 1)
        for j in range(2):
            head = 2 * pair + j
            gap = columns[:, head : head + 1] - rows[head : head + 1, :]
            decay = jnp.exp2(jnp.where(lower, gap, FAR))
            gathered += products[:, j * BLOCK : j * BLOCK + BLOCK] * decay
    return gathered


def two_parts(x):
    high = x.astype(BF16)
    return high, (x - high.astype(F32)).astype(BF16)


def local_kernel(
    plan_ref,
    inputs_ref,
    grad_ref,
    write_ref,
    read_ref,
    parts_ref,
    rows_ref,
    decays_ref,
    ranges_ref,
    entries_ref,
    afters_ref,
    read_terms_ref,
    write_terms_ref,
    far_lead_ref,
    far_tail_ref,
    entry,
    leads,
    tails,
    states_in,
    states_out,
    write_terms,
    lanes_of,
):
    step = pl.program_id(0)
    states, lanes = entry.shape
    heads = lanes // WIDTH
    count = decays_ref.shape[0]
    steps = decays_ref.shape[0] * BLOCK // STEP
    inner = STEP // BLOCK

    @pl.when(step == 0)
    def _():
        for k in range(3):
            lanes_of[k] = spread_matrix(heads, k)
        entry[...] = jnp.zeros_like(entry)

    @pl.when(step < steps)
    def _():
        here = parts_ref[...]
        whole = pl.ds(pl.multiple_of(step * STEP, STEP), STEP)
        leads[whole, :] = (dot(here, lanes_of[0], 1, 0) * grad_ref[...].astype(F32)).astype(BF16)
        tails[whole, :] = (dot(here, lanes_of[1], 1, 0) * inputs_ref[...].astype(F32)).astype(BF16)
        entries_ref[...] = entry[...].astype(BF16)
        for k in range(inner):
            block = step * inner + k
            at = pl.ds(pl.multiple_of(block * BLOCK, BLOCK), BLOCK)
            state = entry[...]
            states_in[k * BLOCK : k * BLOCK + BLOCK] = state.astype(BF16)
            entry[...] = state * decays_ref[pl.ds(block, 1), :] + dot(
                write_ref[at, :], tails[at, :], 0, 0
            )

    @pl.when((step == plan_ref[0]) | (step == plan_ref[1]))
    def _():
        scaled = (dot(parts_ref[...], lanes_of[2], 1, 0) * inputs_ref[...].astype(F32)).astype(BF16)
        for k in range(inner):
            inside = slice(k * BLOCK, k * BLOCK + BLOCK)
            block = step * inner + k
            at = pl.ds(pl.multiple_of(block * BLOCK, BLOCK), BLOCK)
            write, read = write_ref[at, :], read_ref[at, :]
            lead, tail = leads[at, :], tails[at, :]
            far_lead_ref[inside] = (lead.astype(F32) * ranges_ref[pl.ds(block, 1), :]).astype(BF16)
            far_tail_ref[inside] = (
                tail.astype(F32) * ranges_ref[pl.ds(count + block, 1), :]
            ).astype(BF16)
            high, low = two_parts(
                key_block(scaled[inside], grad_ref[inside], rows_ref[k * heads : k * heads + heads, :])
            )
            read_terms_ref[inside] = (
                dot(lead, states_in[inside], 1, 1) + dot(high, write, 1, 0) + dot(low, write, 1, 0)
            )
            write_terms[at, :] = dot(high, read, 0, 0) + dot(low, read, 0, 0)

    @pl.when(step == steps)
    def _():
        state = jnp.zeros_like(entry)
        for block in reversed(range(count)):
            at = slice(block * BLOCK, block * BLOCK + BLOCK)
            states_out[at] = state.astype(BF16)
            state = state * decays_ref[block : block + 1] + dot(read_ref[at, :], leads[at], 0, 0)
        for quarter in range(steps):
            last = quarter * STEP + STEP - BLOCK
            afters_ref[quarter * states : quarter * states + states] = states_out[last : last + BLOCK]
        for slot in range(2):
            for k in range(inner):
                place = slot * STEP + k * BLOCK
                at = pl.ds(pl.multiple_of(plan_ref[slot] * STEP + k * BLOCK, BLOCK), BLOCK)
                write_terms_ref[place : place + BLOCK] = write_terms[at, :] + dot(
                    tails[at, :], states_out[at, :], 1, 1
                )


def local(plan, inputs, grad_out, write_keys, read_keys, parts, rows, decays, ranges):
    length, lanes = inputs.shape
    heads = lanes // WIDTH
    states = write_keys.shape[1]
    assert states == BLOCK and 6 * heads <= 128
    steps = length // STEP

    def forth(c, plan):
        return jnp.minimum(c, steps - 1)

    def slot_forth(c, plan):
        return jnp.where(c > plan[0], 1, 0)

    def all_of(c, plan):
        return 0

    def whole(x):
        return pl.BlockSpec(x.shape, lambda c, plan: (0, 0))

    def tokens(at, size, width):
        return pl.BlockSpec((size, width), lambda c, plan: (at(c, plan), 0))

    return pl.pallas_call(
        local_kernel,
        out_shape=(
            jax.ShapeDtypeStruct((steps * states, lanes), BF16),
            jax.ShapeDtypeStruct((steps * states, lanes), BF16),
            jax.ShapeDtypeStruct((2 * STEP, states), F32),
            jax.ShapeDtypeStruct((2 * STEP, states), F32),
            jax.ShapeDtypeStruct((2 * STEP, lanes), BF16),
            jax.ShapeDtypeStruct((2 * STEP, lanes), BF16),
        ),
        grid_spec=pltpu.PrefetchScalarGridSpec(
            num_scalar_prefetch=1,
            grid=(steps + 1,),
            in_specs=[
                tokens(forth, STEP, lanes),
                tokens(forth, STEP, lanes),
                whole(write_keys),
                whole(read_keys),
                tokens(forth, STEP, 128),
                tokens(forth, STEP // BLOCK * heads, BLOCK),
                whole(decays),
                whole(ranges),
            ],
            out_specs=(
                tokens(forth, states, lanes),
                tokens(all_of, steps * states, lanes),
                tokens(slot_forth, STEP, states),
                tokens(all_of, 2 * STEP, states),
                tokens(slot_forth, STEP, lanes),
                tokens(slot_forth, STEP, lanes),
            ),
            scratch_shapes=[
                pltpu.VMEM((states, lanes), F32),
                pltpu.VMEM((length, lanes), BF16),
                pltpu.VMEM((length, lanes), BF16),
                pltpu.VMEM((STEP, lanes), BF16),
                pltpu.VMEM((length, lanes), BF16),
                pltpu.VMEM((length, states), F32),
                pltpu.VMEM((3, 128, lanes), BF16),
            ],
        ),
        compiler_params=pltpu.CompilerParams(vmem_limit_bytes=44 * 1024 * 1024),
        cost_estimate=pl.CostEstimate(
            flops=24 * length * lanes * states, bytes_accessed=8 * length * lanes, transcendentals=0
        ),
        name="local",
    )(plan, inputs, grad_out, write_keys, read_keys, parts, rows, decays, ranges)


def early_grads_kernel(
    plan_ref,
    lead_ref,
    tail_ref,
    read_terms_ref,
    write_terms_ref,
    own_ref,
    others_ref,
    other_ref,
    ends_ref,
    far_ref,
    crossed_ref,
    halved,
):
    step = pl.program_id(0)
    states = ends_ref.shape[0] // 2
    part = states // 2

    @pl.when(step == 0)
    def _():
        first = plan_ref[4] == 1
        own, others = own_ref[...], others_ref[...]
        top, bottom = jnp.where(first, own, others), jnp.where(first, others, own)
        entry = jnp.concatenate([top[:part], bottom[:part]], axis=0)
        after = jnp.concatenate([top[part:], bottom[part:]], axis=0)
        decay = other_ref[2 * states : 2 * states + 1]
        entry = jnp.where(first, entry, other_ref[:states] + decay * entry)
        after = jnp.where(first, other_ref[states : 2 * states] + decay * after, after)
        ends_ref[:states] = entry
        ends_ref[states:] = after
        halved[0] = entry.astype(BF16)
        halved[1] = after.astype(BF16)

    read = read_terms_ref[...] + dot(lead_ref[...], halved[0], 1, 1)
    write = write_terms_ref[...] + dot(tail_ref[...], halved[1], 1, 1)
    for at, out in ((plan_ref[5], far_ref), (1 - plan_ref[5], crossed_ref)):

        @pl.when(step == at)
        def _():
            out[:, :states] = read
            out[:, states:] = write


def early_grads(plan, lead, tail, read_terms, write_terms, own, others, other):
    lanes = lead.shape[1]
    states = read_terms.shape[1]

    def tokens(width):
        return pl.BlockSpec((STEP, width), lambda c, plan: (c, 0))

    def whole(x):
        return pl.BlockSpec(x.shape, lambda c, plan: (0, 0))

    ends = jax.ShapeDtypeStruct((2 * states, lanes), F32)
    terms = jax.ShapeDtypeStruct((STEP, 2 * states), F32)
    shapes = (ends, terms, terms)
    return pl.pallas_call(
        early_grads_kernel,
        out_shape=shapes,
        grid_spec=pltpu.PrefetchScalarGridSpec(
            num_scalar_prefetch=1,
            grid=(2,),
            in_specs=[
                tokens(lanes),
                tokens(lanes),
                tokens(states),
                tokens(states),
                whole(own),
                whole(others),
                whole(other),
            ],
            out_specs=tuple(whole(x) for x in shapes),
            scratch_shapes=[pltpu.VMEM((2, states, lanes), BF16)],
        ),
        compiler_params=pltpu.CompilerParams(vmem_limit_bytes=24 * 1024 * 1024),
        cost_estimate=pl.CostEstimate(
            flops=8 * STEP * lanes * states, bytes_accessed=8 * STEP * lanes, transcendentals=0
        ),
        name="early_grads",
    )(plan, lead, tail, read_terms, write_terms, own, others, other)


def combine_kernel(place_ref, *refs):
    *got, out_ref = refs
    place = place_ref[0]
    part, lanes = got[0].shape[0] - 8, got[0].shape[1]
    entry = jnp.zeros((part, lanes), F32)
    after = jnp.zeros((part, lanes), F32)
    for m, value in enumerate(got, 1):
        source = place ^ m
        weight = jnp.ones((1, lanes), F32)
        for k, between in enumerate(got, 1):
            middle = place ^ k
            inside = ((source < middle) & (middle < place)) | ((place < middle) & (middle < source))
            weight = weight * jnp.where(inside, between[part : part + 1], 1.0)
        term = weight * value[:part]
        entry = entry + jnp.where(source < place, term, 0.0)
        after = after + jnp.where(source > place, term, 0.0)
    out_ref[:part] = entry
    out_ref[part:] = after


def combine(place, got):
    rows, lanes = got[0].shape
    return pl.pallas_call(
        combine_kernel,
        out_shape=jax.ShapeDtypeStruct((2 * (rows - 8), lanes), F32),
        in_specs=[pl.BlockSpec(memory_space=pltpu.SMEM)]
        + [pl.BlockSpec(memory_space=pltpu.VMEM)] * len(got),
        out_specs=pl.BlockSpec(memory_space=pltpu.VMEM),
        compiler_params=pltpu.CompilerParams(vmem_limit_bytes=16 * 1024 * 1024),
        cost_estimate=pl.CostEstimate(
            flops=4 * len(got) * rows * lanes,
            bytes_accessed=4 * (len(got) + 2) * rows * lanes,
            transcendentals=0,
        ),
        name="combine",
    )(place.reshape(1), *got)


def outputs_kernel(
    offset,
    with_terms,
    aliased,
    plan_ref,
    inputs_ref,
    grad_ref,
    write_ref,
    read_ref,
    entries_ref,
    afters_ref,
    parts_ref,
    rows_ref,
    decays_ref,
    ranges_ref,
    ends_ref,
    skip_ref,
    *rest,
):
    mixed_ref, grad_in_ref, *terms, lanes_of, states_in, states_out, skip_row = rest[aliased:]
    step = pl.program_id(0)
    states = write_ref.shape[1]
    heads = skip_ref.shape[1]
    count = ranges_ref.shape[0] // 2
    inner = STEP // BLOCK

    @pl.when(step == 0)
    def _():
        for k in range(3):
            lanes_of[k] = spread_matrix(heads, k)
        gains = jnp.concatenate(three(jnp.broadcast_to(skip_ref[...], (8, heads))), axis=1)
        skip_row[...] = dot(gains.astype(BF16), row_spread_matrix(heads), 1, 0)

    leads, tails, gains = [dot(parts_ref[...], lanes_of[k], 1, 0) for k in range(3)]
    scaled = (gains * inputs_ref[...].astype(F32)).astype(BF16)
    lead = (leads * grad_ref[...].astype(F32)).astype(BF16)
    tail = (tails * inputs_ref[...].astype(F32)).astype(BF16)
    start = plan_ref[offset + step] * inner
    state = entries_ref[...].astype(F32) + ranges_ref[pl.ds(start, 1), :] * ends_ref[:states]
    for k in range(inner):
        at = slice(k * BLOCK, k * BLOCK + BLOCK)
        states_in[at] = state.astype(BF16)
        if k < inner - 1:
            state = state * decays_ref[pl.ds(start + k, 1), :] + dot(write_ref[at, :], tail[at], 0, 0)
    end = start + inner - 1
    state = afters_ref[...].astype(F32) + ranges_ref[pl.ds(count + end, 1), :] * ends_ref[states:]
    for k in reversed(range(inner)):
        at = slice(k * BLOCK, k * BLOCK + BLOCK)
        states_out[at] = state.astype(BF16)
        if k > 0:
            state = state * decays_ref[pl.ds(start + k, 1), :] + dot(read_ref[at, :], lead[at], 0, 0)
    found = []
    for k in range(inner):
        at = slice(k * BLOCK, k * BLOCK + BLOCK)
        write, read = write_ref[at, :], read_ref[at, :]
        grad = grad_ref[at]
        entry, after = states_in[at], states_out[at]
        skip = skip_row[0:1]
        out_rest = leads[at] * dot(read, entry, 1, 0) + skip * inputs_ref[at].astype(F32)
        back_rest = tails[at] * dot(write, after, 1, 0) + skip * grad.astype(F32)
        scores = dot(read, write, 1, 1)
        rows = rows_ref[k * heads : k * heads + heads, :]
        columns = rows.T
        lower = lower_block()
        gathered = jnp.zeros((BLOCK, BLOCK), F32)
        for pair in range(heads // 2):
            lanes = slice(pair * 128, pair * 128 + 128)
            scaled_pair = halves(scaled[at, lanes])
            if with_terms:
                products = dot(grad[:, lanes], scaled_pair, 1, 1)
            mixing = []
            for j in range(2):
                head = 2 * pair + j
                gap = columns[:, head : head + 1] - rows[head : head + 1, :]
                decay = jnp.exp2(jnp.where(lower, gap, FAR))
                mixing.append((scores * decay).astype(BF16))
                if with_terms:
                    gathered += products[:, j * BLOCK : j * BLOCK + BLOCK] * decay
            mixed = dot(jnp.concatenate(mixing, axis=1), scaled_pair, 1, 0)
            mixed_ref[at, lanes] = (mixed + out_rest[:, lanes]).astype(BF16)
            back = dot(jnp.concatenate(mixing, axis=0), halves(grad[:, lanes]), 0, 0)
            grad_in_ref[at, lanes] = (gains[at, lanes] * back + back_rest[:, lanes]).astype(BF16)
        if with_terms:
            high, low = two_parts(gathered)
            found.append(
                (
                    dot(lead[at], entry, 1, 1) + dot(high, write, 1, 0) + dot(low, write, 1, 0),
                    dot(tail[at], after, 1, 1) + dot(high, read, 0, 0) + dot(low, read, 0, 0),
                )
            )
    for n, out in enumerate(terms):

        @pl.when(step == n)
        def _():
            for k, (for_read, for_write) in enumerate(found):
                out[k * BLOCK : k * BLOCK + BLOCK, :states] = for_read
                out[k * BLOCK : k * BLOCK + BLOCK, states:] = for_write


def outputs(
    plan, offset, steps, with_terms, earlier, inputs, grad_out, write_keys, read_keys, made, ends, skip
):
    length, lanes = inputs.shape
    states = write_keys.shape[1]
    entries, afters, parts, rows, decays, ranges = made
    heads = lanes // WIDTH

    def tokens(size, width):
        return pl.BlockSpec((size, width), lambda c, plan: (plan[offset + c], 0))

    def whole(x):
        return pl.BlockSpec(x.shape, lambda c, plan: (0, 0))

    wide = tokens(STEP, lanes)
    shape = jax.ShapeDtypeStruct((length, lanes), BF16)
    terms = (jax.ShapeDtypeStruct((STEP, 2 * states), F32),) * (steps * with_terms)
    return pl.pallas_call(
        functools.partial(outputs_kernel, offset, with_terms, len(earlier)),
        out_shape=(shape, shape, *terms),
        grid_spec=pltpu.PrefetchScalarGridSpec(
            num_scalar_prefetch=1,
            grid=(steps,),
            in_specs=[
                wide,
                wide,
                tokens(STEP, states),
                tokens(STEP, states),
                tokens(states, lanes),
                tokens(states, lanes),
                tokens(STEP, 128),
                tokens(STEP // BLOCK * heads, BLOCK),
                whole(decays),
                whole(ranges),
                whole(ends),
                whole(skip),
                *[pl.BlockSpec(memory_space=pl.ANY) for _ in earlier],
            ],
            out_specs=(wide, wide, *[whole(x) for x in terms]),
            scratch_shapes=[
                pltpu.VMEM((3, 128, lanes), BF16),
                pltpu.VMEM((STEP, lanes), BF16),
                pltpu.VMEM((STEP, lanes), BF16),
                pltpu.VMEM((8, lanes), F32),
            ],
        ),
        input_output_aliases={13 + k: k for k in range(len(earlier))},
        compiler_params=pltpu.CompilerParams(vmem_limit_bytes=VMEM_BYTES),
        cost_estimate=pl.CostEstimate(
            flops=16 * steps * STEP * lanes * states, bytes_accessed=12 * steps * STEP * lanes, transcendentals=0
        ),
        name="outputs_and_terms" if with_terms else "outputs",
    )(
        plan, inputs, grad_out, write_keys, read_keys, entries, afters, parts, rows, decays, ranges,
        ends, skip, *earlier,
    )


def carried_states(summed, states, first_window, second_window):
    axes = ("outer", "inner")
    devices = lax.axis_size(axes)
    here = lax.axis_index(axes)
    first = lax.rem(here, 2) == 0
    place = here // 2
    part = states // 2
    other = lax.ppermute(summed, axes, [(d, d ^ 1) for d in range(devices)])
    other, made = first_window(other)
    early_decay = jnp.where(first, summed, other)[2 * states : 2 * states + 1]
    late_decay = jnp.where(first, other, summed)[2 * states : 2 * states + 1]
    row = jnp.where(first, 0, part)

    def mine(x, start):
        return lax.dynamic_slice_in_dim(x, start + row, part, 0)

    early_push = jnp.where(first, mine(summed, 0), mine(other, 0))
    late_push = jnp.where(first, mine(other, 0), mine(summed, 0))
    early_pull = jnp.where(first, mine(summed, states), mine(other, states))
    late_pull = jnp.where(first, mine(other, states), mine(summed, states))
    push = late_push + late_decay * early_push
    pull = early_pull + early_decay * late_pull
    decay = jnp.broadcast_to(early_decay * late_decay, (8, summed.shape[1]))
    got = []
    for m in range(1, devices // 2):
        sent = jnp.concatenate([jnp.where(place < (place ^ m), push, pull), decay], axis=0)
        got.append(lax.ppermute(sent, axes, [(d, d ^ (2 * m)) for d in range(devices)]))
    got, made = second_window(got, made)
    own = combine(place, got)
    others = lax.ppermute(own, axes, [(d, d ^ 1) for d in range(devices)])
    return (own, others, other), made


def on_device(inputs, log_decay, write_keys, read_keys, skip_gain, grad_out):
    states = write_keys.shape[1]
    line = lax.axis_size("mp") == 4
    assert inputs.shape[0] == 4 * STEP

    at = lax.axis_index("mp")
    ends = (at == 0) | (at == 3)

    def of(*values):
        if not line:
            return jnp.int32(values[0])
        return sum(jnp.where(at == k, v, 0) for k, v in enumerate(values)).astype(jnp.int32)

    even = (lax.rem(lax.axis_index(("outer", "inner")), 2) == 0).astype(jnp.int32)
    plan = jnp.stack(
        [
            of(2, 0, 1, 0),
            of(3, 2, 3, 1),
            of(1, 3, 0, 2),
            of(0, 1, 2, 3),
            even,
            of(1, 0, 1, 0),
        ]
    )
    summed = totals(inputs, grad_out, log_decay, write_keys, read_keys)

    def first_window(other):
        ordered, _ = lax.optimization_barrier((log_decay, summed))
        return lax.optimization_barrier((other, factors(ordered)))

    def second_window(got, made):
        parts, rows, decays, ranges = made
        found = local(plan, inputs, grad_out, write_keys, read_keys, parts, rows, decays, ranges)
        return lax.optimization_barrier((got, (found, made)))

    given, made = carried_states(summed, states, first_window, second_window)
    (entries, afters, read_terms, write_terms, lead, tail), made = made
    states_at_ends, far, crossed = early_grads(plan, lead, tail, read_terms, write_terms, *given)

    def part(offset, steps, with_terms, earlier):
        return outputs(
            plan, offset, steps, with_terms, earlier, inputs, grad_out, write_keys, read_keys,
            (entries, afters, *made), states_at_ends, skip_gain[None],
        )

    if not line:
        *results, third, own = part(2, 2, True, ())
        results = part(0, 2, False, results)
        terms = jnp.concatenate([own, third, crossed, far], axis=0)
        own = lax.psum_scatter(terms, "mp", scatter_dimension=0, tiled=True)
        return *results, own[:, states:], own[:, :states]

    two_away = lax.ppermute(crossed, "mp", [(0, 2), (3, 1)])
    far_sum = lax.ppermute(far, "mp", [(0, 1), (1, 0), (2, 3), (3, 2)])
    middle = lax.ppermute(crossed, "mp", [(1, 2), (2, 1)])
    (*results, third, own), far_sum, two_away, middle = lax.optimization_barrier(
        (part(2, 2, True, ()), far_sum, two_away, middle)
    )
    came = jnp.where(ends, 0.0, far_sum)
    last = lax.ppermute(third + came, "mp", [(0, 1), (1, 3), (3, 2), (2, 0)])
    own = own + (far_sum - came) + middle + two_away
    results, own, last = lax.optimization_barrier((part(0, 2, False, results), own, last))
    total = own + last
    return *results, total[:, states:], total[:, :states]


def solution(mesh):
    tokens = ("outer", "inner")
    return jax.shard_map(
        on_device,
        mesh=mesh,
        in_specs=(
            P(tokens, "mp"),
            P("mp", tokens),
            P(tokens, None),
            P(tokens, None),
            P("mp"),
            P(tokens, "mp"),
        ),
        out_specs=(
            P(tokens, "mp"),
            P(tokens, "mp"),
            P(("outer", "inner", "mp"), None),
            P(("outer", "inner", "mp"), None),
        ),
        check_vma=False,
    )
```

```python
import functools

import jax
import jax.numpy as jnp
from jax import lax
from jax.experimental import pallas as pl
from jax.experimental.pallas import tpu as pltpu
from jax.sharding import PartitionSpec as P

WIDTH = 64
BLOCK = 128
STEP = 512
FAR = -1e30
LOG2E = 1.4426950408889634
VMEM_BYTES = 60 * 1024 * 1024
F32 = jnp.float32
BF16 = jnp.bfloat16


def dot(a, b, over_a, over_b):
    return lax.dot_general(a, b, (((over_a,), (over_b,)), ((), ())), preferred_element_type=F32)


def minus_expm1(y):
    series = 1.0 + y * (1.0 / 9.0)
    for k in (8.0, 7.0, 6.0, 5.0, 4.0, 3.0, 2.0):
        series = 1.0 + y * (1.0 / k) * series
    return jnp.where(y > -0.4, -y * series, 1.0 - jnp.exp(y))


def iota(shape, dimension):
    return lax.broadcasted_iota(jnp.int32, shape, dimension)


def spread_matrix(heads, group):
    shape = (128, heads * WIDTH)
    row = iota(shape, 0) - 2 * heads * group
    gap = iota(shape, 1) - WIDTH * jnp.where(row < heads, row, row - heads)
    inside = (row >= 0) & (row < 2 * heads) & (gap >= 0) & (gap < WIDTH)
    return jnp.where(inside, 1.0, 0.0).astype(BF16)


def row_spread_matrix(heads):
    shape = (heads, heads * WIDTH)
    gap = iota(shape, 1) - WIDTH * iota(shape, 0)
    one = jnp.where((gap >= 0) & (gap < WIDTH), 1.0, 0.0)
    return jnp.concatenate([one, one, one], axis=0).astype(BF16)


def three(x):
    high = x.astype(BF16).astype(F32)
    middle = (x - high).astype(BF16).astype(F32)
    return high, middle, x - high - middle


def block_sums(rows):
    shape = (BLOCK, 2 * BLOCK)
    source, target = iota(shape, 0), iota(shape, 1)
    upto = jnp.where(source <= target, 1.0, 0.0)
    beyond = jnp.where(source > target - BLOCK, 1.0, 0.0)
    within = jnp.where(target < BLOCK, upto, beyond).astype(BF16)
    count = rows.shape[0]
    both = dot(jnp.concatenate(three(rows), axis=0).astype(BF16), within, 1, 0)
    both = both[:count] + both[count : 2 * count] + both[2 * count :]
    return both[:, :BLOCK], both[:, BLOCK:]


def stacked(x):
    return jnp.concatenate(
        [x[:, at : at + BLOCK] for at in range(0, x.shape[1], BLOCK)], axis=0
    )


def block_factors(ld_ref):
    ld = ld_ref[...]
    gain = stacked(jnp.sqrt(minus_expm1(2.0 * ld)))
    before, behind = block_sums(stacked(ld))
    return gain, before, behind


def in_columns(groups, heads, block):
    parts = []
    for factor in groups:
        rows = factor[block * heads : block * heads + heads]
        high = rows.astype(BF16).astype(F32)
        parts += [high, rows - high]
    parts.append(jnp.zeros((128 - 2 * heads * len(groups), BLOCK), F32))
    rows = jnp.concatenate(parts, axis=0).astype(BF16)
    eye = jnp.where(iota((BLOCK, BLOCK), 0) == iota((BLOCK, BLOCK), 1), 1.0, 0.0).astype(BF16)
    return dot(eye, rows, 1, 1).astype(BF16)


def starts_and_ends(before, heads, count):
    totals = [before[c * heads : c * heads + heads, BLOCK - 1 :] for c in range(count)]
    start = [jnp.zeros((heads, 1), F32)]
    for total in totals:
        start.append(start[-1] + total)
    end = [jnp.zeros((heads, 1), F32)]
    for total in totals[::-1]:
        end.append(end[-1] + total)
    since = jnp.concatenate(start[:count], axis=0)
    until = jnp.concatenate(end[:count][::-1], axis=0)
    return since, until, start[count]


def totals_kernel(
    inputs_ref, grad_ref, ld_ref, write_ref, read_ref, out_ref, parts, lanes_of
):
    step = pl.program_id(0)
    heads = ld_ref.shape[0]
    states = write_ref.shape[1]
    count = ld_ref.shape[1] // BLOCK

    @pl.when(step == 0)
    def _():
        lanes_of[0] = spread_matrix(heads, 0)
        lanes_of[1] = spread_matrix(heads, 1)
        gain, before, behind = block_factors(ld_ref)
        since, until, whole = starts_and_ends(before, heads, count)
        lead = jnp.exp(since + before)
        tail = gain * jnp.exp(until + behind)
        for c in range(count):
            parts[c * BLOCK : c * BLOCK + BLOCK] = in_columns((lead, tail), heads, c)
        out_ref[...] = jnp.zeros_like(out_ref)
        whole = jnp.concatenate(three(jnp.exp(whole)), axis=0)
        whole = jnp.broadcast_to(whole, (3 * heads, 128)).astype(BF16)
        out_ref[2 * states :] = dot(whole, row_spread_matrix(heads), 0, 0)[0:8]

    at = pl.ds(pl.multiple_of(step * STEP, STEP), STEP)
    here = parts[at, :]
    lead = (dot(here, lanes_of[0], 1, 0) * grad_ref[...].astype(F32)).astype(BF16)
    out_ref[states : 2 * states] += dot(read_ref[...], lead, 0, 0)
    tail = (dot(here, lanes_of[1], 1, 0) * inputs_ref[...].astype(F32)).astype(BF16)
    out_ref[0:states] += dot(write_ref[...], tail, 0, 0)


def totals(inputs, grad_out, log_decay, write_keys, read_keys):
    length, lanes = inputs.shape
    heads = log_decay.shape[0]
    states = write_keys.shape[1]
    wide = pl.BlockSpec((STEP, lanes), lambda c: (c, 0))
    keys = pl.BlockSpec((STEP, states), lambda c: (c, 0))
    return pl.pallas_call(
        totals_kernel,
        out_shape=jax.ShapeDtypeStruct((2 * states + 8, lanes), F32),
        grid=(length // STEP,),
        in_specs=[wide, wide, pl.BlockSpec((heads, length), lambda c: (0, 0)), keys, keys],
        out_specs=pl.BlockSpec((2 * states + 8, lanes), lambda c: (0, 0)),
        scratch_shapes=[
            pltpu.VMEM((length, 128), BF16),
            pltpu.VMEM((2, 128, lanes), BF16),
        ],
        compiler_params=pltpu.CompilerParams(vmem_limit_bytes=48 * 1024 * 1024),
        cost_estimate=pl.CostEstimate(
            flops=6 * length * lanes * states, bytes_accessed=4 * length * lanes, transcendentals=0
        ),
        name="totals",
    )(inputs, grad_out, log_decay, write_keys, read_keys)


def factors_kernel(ld_ref, near_ref, rows_ref, decays_ref, ranges_ref):
    heads, length = ld_ref.shape
    count = length // BLOCK
    gain, before, behind = block_factors(ld_ref)
    lead = jnp.exp(before)
    tail = gain * jnp.exp(behind)
    rows_ref[...] = before * LOG2E
    lasts = []
    for c in range(count):
        at = slice(c * BLOCK, c * BLOCK + BLOCK)
        near_ref[at] = in_columns((lead, tail, gain), heads, c)
        lasts.append(lead[c * heads : c * heads + heads, BLOCK - 1 :])
    last = jnp.concatenate(lasts, axis=1)
    decays = dot(jnp.concatenate(three(last), axis=0).astype(BF16), row_spread_matrix(heads), 0, 0)
    decays_ref[...] = decays
    ones = jnp.ones((1, heads * WIDTH), F32)
    after, before = [ones], [ones]
    for c in range(count - 1):
        after.append(after[-1] * decays[c : c + 1])
        before.append(before[-1] * decays[count - 1 - c : count - c])
    ranges_ref[:count] = jnp.concatenate(after, axis=0)
    ranges_ref[count:] = jnp.concatenate(before[::-1], axis=0)


def factors(log_decay):
    heads, length = log_decay.shape
    count = length // BLOCK
    lanes = heads * WIDTH
    return pl.pallas_call(
        factors_kernel,
        out_shape=(
            jax.ShapeDtypeStruct((length, 128), BF16),
            jax.ShapeDtypeStruct((count * heads, BLOCK), F32),
            jax.ShapeDtypeStruct((count, lanes), F32),
            jax.ShapeDtypeStruct((2 * count, lanes), F32),
        ),
        compiler_params=pltpu.CompilerParams(vmem_limit_bytes=48 * 1024 * 1024),
        cost_estimate=pl.CostEstimate(
            flops=heads * length * 6000, bytes_accessed=1000 * length, transcendentals=0
        ),
        name="factors",
    )(log_decay)


def halves(pair):
    first = iota(pair.shape, 1) < WIDTH
    zero = jnp.zeros_like(pair)
    return jnp.concatenate([jnp.where(first, pair, zero), jnp.where(first, zero, pair)], axis=0)


def lower_block():
    return iota((BLOCK, BLOCK), 0) >= iota((BLOCK, BLOCK), 1)


def key_block(scaled, grad, rows):
    heads = rows.shape[0]
    columns = rows.T
    lower = lower_block()
    gathered = jnp.zeros((BLOCK, BLOCK), F32)
    for pair in range(heads // 2):
        lanes = slice(pair * 128, pair * 128 + 128)
        products = dot(grad[:, lanes], halves(scaled[:, lanes]), 1, 1)
        for j in range(2):
            head = 2 * pair + j
            gap = columns[:, head : head + 1] - rows[head : head + 1, :]
            decay = jnp.exp2(jnp.where(lower, gap, FAR))
            gathered += products[:, j * BLOCK : j * BLOCK + BLOCK] * decay
    return gathered


def two_parts(x):
    high = x.astype(BF16)
    return high, (x - high.astype(F32)).astype(BF16)


def local_kernel(
    plan_ref,
    inputs_ref,
    grad_ref,
    write_ref,
    read_ref,
    parts_ref,
    rows_ref,
    decays_ref,
    ranges_ref,
    entries_ref,
    afters_ref,
    read_terms_ref,
    write_terms_ref,
    far_lead_ref,
    far_tail_ref,
    entry,
    leads,
    tails,
    states_in,
    states_out,
    write_terms,
    lanes_of,
):
    step = pl.program_id(0)
    states, lanes = entry.shape
    heads = lanes // WIDTH
    count = decays_ref.shape[0]
    steps = decays_ref.shape[0] * BLOCK // STEP
    inner = STEP // BLOCK

    @pl.when(step == 0)
    def _():
        for k in range(3):
            lanes_of[k] = spread_matrix(heads, k)
        entry[...] = jnp.zeros_like(entry)

    @pl.when(step < steps)
    def _():
        here = parts_ref[...]
        whole = pl.ds(pl.multiple_of(step * STEP, STEP), STEP)
        leads[whole, :] = (dot(here, lanes_of[0], 1, 0) * grad_ref[...].astype(F32)).astype(BF16)
        tails[whole, :] = (dot(here, lanes_of[1], 1, 0) * inputs_ref[...].astype(F32)).astype(BF16)
        entries_ref[...] = entry[...].astype(BF16)
        for k in range(inner):
            block = step * inner + k
            at = pl.ds(pl.multiple_of(block * BLOCK, BLOCK), BLOCK)
            state = entry[...]
            states_in[k * BLOCK : k * BLOCK + BLOCK] = state.astype(BF16)
            entry[...] = state * decays_ref[pl.ds(block, 1), :] + dot(
                write_ref[at, :], tails[at, :], 0, 0
            )

    @pl.when((step == plan_ref[0]) | (step == plan_ref[1]))
    def _():
        scaled = (dot(parts_ref[...], lanes_of[2], 1, 0) * inputs_ref[...].astype(F32)).astype(BF16)
        for k in range(inner):
            inside = slice(k * BLOCK, k * BLOCK + BLOCK)
            block = step * inner + k
            at = pl.ds(pl.multiple_of(block * BLOCK, BLOCK), BLOCK)
            write, read = write_ref[at, :], read_ref[at, :]
            lead, tail = leads[at, :], tails[at, :]
            far_lead_ref[inside] = (lead.astype(F32) * ranges_ref[pl.ds(block, 1), :]).astype(BF16)
            far_tail_ref[inside] = (
                tail.astype(F32) * ranges_ref[pl.ds(count + block, 1), :]
            ).astype(BF16)
            high, low = two_parts(
                key_block(scaled[inside], grad_ref[inside], rows_ref[k * heads : k * heads + heads, :])
            )
            read_terms_ref[inside] = (
                dot(lead, states_in[inside], 1, 1) + dot(high, write, 1, 0) + dot(low, write, 1, 0)
            )
            write_terms[at, :] = dot(high, read, 0, 0) + dot(low, read, 0, 0)

    @pl.when(step == steps)
    def _():
        state = jnp.zeros_like(entry)
        for block in reversed(range(count)):
            at = slice(block * BLOCK, block * BLOCK + BLOCK)
            states_out[at] = state.astype(BF16)
            state = state * decays_ref[block : block + 1] + dot(read_ref[at, :], leads[at], 0, 0)
        for quarter in range(steps):
            last = quarter * STEP + STEP - BLOCK
            afters_ref[quarter * states : quarter * states + states] = states_out[last : last + BLOCK]
        for slot in range(2):
            for k in range(inner):
                place = slot * STEP + k * BLOCK
                at = pl.ds(pl.multiple_of(plan_ref[slot] * STEP + k * BLOCK, BLOCK), BLOCK)
                write_terms_ref[place : place + BLOCK] = write_terms[at, :] + dot(
                    tails[at, :], states_out[at, :], 1, 1
                )


def local(plan, inputs, grad_out, write_keys, read_keys, parts, rows, decays, ranges):
    length, lanes = inputs.shape
    heads = lanes // WIDTH
    states = write_keys.shape[1]
    assert states == BLOCK and 6 * heads <= 128
    steps = length // STEP

    def forth(c, plan):
        return jnp.minimum(c, steps - 1)

    def slot_forth(c, plan):
        return jnp.where(c > plan[0], 1, 0)

    def all_of(c, plan):
        return 0

    def whole(x):
        return pl.BlockSpec(x.shape, lambda c, plan: (0, 0))

    def tokens(at, size, width):
        return pl.BlockSpec((size, width), lambda c, plan: (at(c, plan), 0))

    return pl.pallas_call(
        local_kernel,
        out_shape=(
            jax.ShapeDtypeStruct((steps * states, lanes), BF16),
            jax.ShapeDtypeStruct((steps * states, lanes), BF16),
            jax.ShapeDtypeStruct((2 * STEP, states), F32),
            jax.ShapeDtypeStruct((2 * STEP, states), F32),
            jax.ShapeDtypeStruct((2 * STEP, lanes), BF16),
            jax.ShapeDtypeStruct((2 * STEP, lanes), BF16),
        ),
        grid_spec=pltpu.PrefetchScalarGridSpec(
            num_scalar_prefetch=1,
            grid=(steps + 1,),
            in_specs=[
                tokens(forth, STEP, lanes),
                tokens(forth, STEP, lanes),
                whole(write_keys),
                whole(read_keys),
                tokens(forth, STEP, 128),
                tokens(forth, STEP // BLOCK * heads, BLOCK),
                whole(decays),
                whole(ranges),
            ],
            out_specs=(
                tokens(forth, states, lanes),
                tokens(all_of, steps * states, lanes),
                tokens(slot_forth, STEP, states),
                tokens(all_of, 2 * STEP, states),
                tokens(slot_forth, STEP, lanes),
                tokens(slot_forth, STEP, lanes),
            ),
            scratch_shapes=[
                pltpu.VMEM((states, lanes), F32),
                pltpu.VMEM((length, lanes), BF16),
                pltpu.VMEM((length, lanes), BF16),
                pltpu.VMEM((STEP, lanes), BF16),
                pltpu.VMEM((length, lanes), BF16),
                pltpu.VMEM((length, states), F32),
                pltpu.VMEM((3, 128, lanes), BF16),
            ],
        ),
        compiler_params=pltpu.CompilerParams(vmem_limit_bytes=40 * 1024 * 1024),
        cost_estimate=pl.CostEstimate(
            flops=24 * length * lanes * states, bytes_accessed=8 * length * lanes, transcendentals=0
        ),
        name="local",
    )(plan, inputs, grad_out, write_keys, read_keys, parts, rows, decays, ranges)


def early_grads_kernel(
    plan_ref,
    lead_ref,
    tail_ref,
    read_terms_ref,
    write_terms_ref,
    own_ref,
    others_ref,
    other_ref,
    ends_ref,
    far_ref,
    crossed_ref,
    halved,
):
    step = pl.program_id(0)
    states = ends_ref.shape[0] // 2
    part = states // 2

    @pl.when(step == 0)
    def _():
        first = plan_ref[4] == 1
        own, others = own_ref[...], others_ref[...]
        top, bottom = jnp.where(first, own, others), jnp.where(first, others, own)
        entry = jnp.concatenate([top[:part], bottom[:part]], axis=0)
        after = jnp.concatenate([top[part:], bottom[part:]], axis=0)
        decay = other_ref[2 * states : 2 * states + 1]
        entry = jnp.where(first, entry, other_ref[:states] + decay * entry)
        after = jnp.where(first, other_ref[states : 2 * states] + decay * after, after)
        ends_ref[:states] = entry
        ends_ref[states:] = after
        halved[0] = entry.astype(BF16)
        halved[1] = after.astype(BF16)

    read = read_terms_ref[...] + dot(lead_ref[...], halved[0], 1, 1)
    write = write_terms_ref[...] + dot(tail_ref[...], halved[1], 1, 1)
    for at, out in ((plan_ref[5], far_ref), (1 - plan_ref[5], crossed_ref)):

        @pl.when(step == at)
        def _():
            out[:, :states] = read
            out[:, states:] = write


def early_grads(plan, lead, tail, read_terms, write_terms, own, others, other):
    lanes = lead.shape[1]
    states = read_terms.shape[1]

    def tokens(width):
        return pl.BlockSpec((STEP, width), lambda c, plan: (c, 0))

    def whole(x):
        return pl.BlockSpec(x.shape, lambda c, plan: (0, 0))

    ends = jax.ShapeDtypeStruct((2 * states, lanes), F32)
    terms = jax.ShapeDtypeStruct((STEP, 2 * states), F32)
    shapes = (ends, terms, terms)
    return pl.pallas_call(
        early_grads_kernel,
        out_shape=shapes,
        grid_spec=pltpu.PrefetchScalarGridSpec(
            num_scalar_prefetch=1,
            grid=(2,),
            in_specs=[
                tokens(lanes),
                tokens(lanes),
                tokens(states),
                tokens(states),
                whole(own),
                whole(others),
                whole(other),
            ],
            out_specs=tuple(whole(x) for x in shapes),
            scratch_shapes=[pltpu.VMEM((2, states, lanes), BF16)],
        ),
        compiler_params=pltpu.CompilerParams(vmem_limit_bytes=24 * 1024 * 1024),
        cost_estimate=pl.CostEstimate(
            flops=8 * STEP * lanes * states, bytes_accessed=8 * STEP * lanes, transcendentals=0
        ),
        name="early_grads",
    )(plan, lead, tail, read_terms, write_terms, own, others, other)


def combine_kernel(place_ref, *refs):
    *got, out_ref = refs
    place = place_ref[0]
    part, lanes = got[0].shape[0] - 8, got[0].shape[1]
    entry = jnp.zeros((part, lanes), F32)
    after = jnp.zeros((part, lanes), F32)
    for m, value in enumerate(got, 1):
        source = place ^ m
        weight = jnp.ones((1, lanes), F32)
        for k, between in enumerate(got, 1):
            middle = place ^ k
            inside = ((source < middle) & (middle < place)) | ((place < middle) & (middle < source))
            weight = weight * jnp.where(inside, between[part : part + 1], 1.0)
        term = weight * value[:part]
        entry = entry + jnp.where(source < place, term, 0.0)
        after = after + jnp.where(source > place, term, 0.0)
    out_ref[:part] = entry
    out_ref[part:] = after


def combine(place, got):
    rows, lanes = got[0].shape
    return pl.pallas_call(
        combine_kernel,
        out_shape=jax.ShapeDtypeStruct((2 * (rows - 8), lanes), F32),
        in_specs=[pl.BlockSpec(memory_space=pltpu.SMEM)]
        + [pl.BlockSpec(memory_space=pltpu.VMEM)] * len(got),
        out_specs=pl.BlockSpec(memory_space=pltpu.VMEM),
        compiler_params=pltpu.CompilerParams(vmem_limit_bytes=16 * 1024 * 1024),
        cost_estimate=pl.CostEstimate(
            flops=4 * len(got) * rows * lanes,
            bytes_accessed=4 * (len(got) + 2) * rows * lanes,
            transcendentals=0,
        ),
        name="combine",
    )(place.reshape(1), *got)


def outputs_kernel(
    offset,
    with_terms,
    aliased,
    plan_ref,
    inputs_ref,
    grad_ref,
    write_ref,
    read_ref,
    entries_ref,
    afters_ref,
    parts_ref,
    rows_ref,
    decays_ref,
    ranges_ref,
    ends_ref,
    skip_ref,
    *rest,
):
    mixed_ref, grad_in_ref, *terms, lanes_of, states_in, states_out, skip_row = rest[aliased:]
    step = pl.program_id(0)
    states = write_ref.shape[1]
    heads = skip_ref.shape[1]
    count = ranges_ref.shape[0] // 2
    inner = STEP // BLOCK

    @pl.when(step == 0)
    def _():
        for k in range(3):
            lanes_of[k] = spread_matrix(heads, k)
        gains = jnp.concatenate(three(jnp.broadcast_to(skip_ref[...], (8, heads))), axis=1)
        skip_row[...] = dot(gains.astype(BF16), row_spread_matrix(heads), 1, 0)

    leads, tails, gains = [dot(parts_ref[...], lanes_of[k], 1, 0) for k in range(3)]
    scaled = (gains * inputs_ref[...].astype(F32)).astype(BF16)
    lead = (leads * grad_ref[...].astype(F32)).astype(BF16)
    tail = (tails * inputs_ref[...].astype(F32)).astype(BF16)
    start = plan_ref[offset + step] * inner
    state = entries_ref[...].astype(F32) + ranges_ref[pl.ds(start, 1), :] * ends_ref[:states]
    for k in range(inner):
        at = slice(k * BLOCK, k * BLOCK + BLOCK)
        states_in[at] = state.astype(BF16)
        if k < inner - 1:
            state = state * decays_ref[pl.ds(start + k, 1), :] + dot(write_ref[at, :], tail[at], 0, 0)
    end = start + inner - 1
    state = afters_ref[...].astype(F32) + ranges_ref[pl.ds(count + end, 1), :] * ends_ref[states:]
    for k in reversed(range(inner)):
        at = slice(k * BLOCK, k * BLOCK + BLOCK)
        states_out[at] = state.astype(BF16)
        if k > 0:
            state = state * decays_ref[pl.ds(start + k, 1), :] + dot(read_ref[at, :], lead[at], 0, 0)
    found = []
    for k in range(inner):
        at = slice(k * BLOCK, k * BLOCK + BLOCK)
        write, read = write_ref[at, :], read_ref[at, :]
        grad = grad_ref[at]
        entry, after = states_in[at], states_out[at]
        skip = skip_row[0:1]
        out_rest = leads[at] * dot(read, entry, 1, 0) + skip * inputs_ref[at].astype(F32)
        back_rest = tails[at] * dot(write, after, 1, 0) + skip * grad.astype(F32)
        scores = dot(read, write, 1, 1)
        rows = rows_ref[k * heads : k * heads + heads, :]
        columns = rows.T
        lower = lower_block()
        gathered = jnp.zeros((BLOCK, BLOCK), F32)
        for pair in range(heads // 2):
            lanes = slice(pair * 128, pair * 128 + 128)
            scaled_pair = halves(scaled[at, lanes])
            if with_terms:
                products = dot(grad[:, lanes], scaled_pair, 1, 1)
            mixing = []
            for j in range(2):
                head = 2 * pair + j
                gap = columns[:, head : head + 1] - rows[head : head + 1, :]
                decay = jnp.exp2(jnp.where(lower, gap, FAR))
                mixing.append((scores * decay).astype(BF16))
                if with_terms:
                    gathered += products[:, j * BLOCK : j * BLOCK + BLOCK] * decay
            mixed = dot(jnp.concatenate(mixing, axis=1), scaled_pair, 1, 0)
            mixed_ref[at, lanes] = (mixed + out_rest[:, lanes]).astype(BF16)
            back = dot(jnp.concatenate(mixing, axis=0), halves(grad[:, lanes]), 0, 0)
            grad_in_ref[at, lanes] = (gains[at, lanes] * back + back_rest[:, lanes]).astype(BF16)
        if with_terms:
            high, low = two_parts(gathered)
            found.append(
                (
                    dot(lead[at], entry, 1, 1) + dot(high, write, 1, 0) + dot(low, write, 1, 0),
                    dot(tail[at], after, 1, 1) + dot(high, read, 0, 0) + dot(low, read, 0, 0),
                )
            )
    for n, out in enumerate(terms):

        @pl.when(step == n)
        def _():
            for k, (for_read, for_write) in enumerate(found):
                out[k * BLOCK : k * BLOCK + BLOCK, :states] = for_read
                out[k * BLOCK : k * BLOCK + BLOCK, states:] = for_write


def outputs(
    plan, offset, steps, with_terms, earlier, inputs, grad_out, write_keys, read_keys, made, ends, skip
):
    length, lanes = inputs.shape
    states = write_keys.shape[1]
    entries, afters, parts, rows, decays, ranges = made
    heads = lanes // WIDTH

    def tokens(size, width):
        return pl.BlockSpec((size, width), lambda c, plan: (plan[offset + c], 0))

    def whole(x):
        return pl.BlockSpec(x.shape, lambda c, plan: (0, 0))

    wide = tokens(STEP, lanes)
    shape = jax.ShapeDtypeStruct((length, lanes), BF16)
    terms = (jax.ShapeDtypeStruct((STEP, 2 * states), F32),) * (steps * with_terms)
    return pl.pallas_call(
        functools.partial(outputs_kernel, offset, with_terms, len(earlier)),
        out_shape=(shape, shape, *terms),
        grid_spec=pltpu.PrefetchScalarGridSpec(
            num_scalar_prefetch=1,
            grid=(steps,),
            in_specs=[
                wide,
                wide,
                tokens(STEP, states),
                tokens(STEP, states),
                tokens(states, lanes),
                tokens(states, lanes),
                tokens(STEP, 128),
                tokens(STEP // BLOCK * heads, BLOCK),
                whole(decays),
                whole(ranges),
                whole(ends),
                whole(skip),
                *[pl.BlockSpec(memory_space=pl.ANY) for _ in earlier],
            ],
            out_specs=(wide, wide, *[whole(x) for x in terms]),
            scratch_shapes=[
                pltpu.VMEM((3, 128, lanes), BF16),
                pltpu.VMEM((STEP, lanes), BF16),
                pltpu.VMEM((STEP, lanes), BF16),
                pltpu.VMEM((8, lanes), F32),
            ],
        ),
        input_output_aliases={13 + k: k for k in range(len(earlier))},
        compiler_params=pltpu.CompilerParams(vmem_limit_bytes=VMEM_BYTES),
        cost_estimate=pl.CostEstimate(
            flops=16 * steps * STEP * lanes * states, bytes_accessed=12 * steps * STEP * lanes, transcendentals=0
        ),
        name="outputs_and_terms" if with_terms else "outputs",
    )(
        plan, inputs, grad_out, write_keys, read_keys, entries, afters, parts, rows, decays, ranges,
        ends, skip, *earlier,
    )


def carried_states(summed, states, first_window, second_window):
    axes = ("outer", "inner")
    devices = lax.axis_size(axes)
    here = lax.axis_index(axes)
    first = lax.rem(here, 2) == 0
    place = here // 2
    part = states // 2
    other = lax.ppermute(summed, axes, [(d, d ^ 1) for d in range(devices)])
    other, made = first_window(other)
    early_decay = jnp.where(first, summed, other)[2 * states : 2 * states + 1]
    late_decay = jnp.where(first, other, summed)[2 * states : 2 * states + 1]
    row = jnp.where(first, 0, part)

    def mine(x, start):
        return lax.dynamic_slice_in_dim(x, start + row, part, 0)

    early_push = jnp.where(first, mine(summed, 0), mine(other, 0))
    late_push = jnp.where(first, mine(other, 0), mine(summed, 0))
    early_pull = jnp.where(first, mine(summed, states), mine(other, states))
    late_pull = jnp.where(first, mine(other, states), mine(summed, states))
    push = late_push + late_decay * early_push
    pull = early_pull + early_decay * late_pull
    decay = jnp.broadcast_to(early_decay * late_decay, (8, summed.shape[1]))
    got = []
    for m in range(1, devices // 2):
        sent = jnp.concatenate([jnp.where(place < (place ^ m), push, pull), decay], axis=0)
        got.append(lax.ppermute(sent, axes, [(d, d ^ (2 * m)) for d in range(devices)]))
    got, made = second_window(got, made)
    own = combine(place, got)
    others = lax.ppermute(own, axes, [(d, d ^ 1) for d in range(devices)])
    return (own, others, other), made


def on_device(inputs, log_decay, write_keys, read_keys, skip_gain, grad_out):
    states = write_keys.shape[1]
    line = lax.axis_size("mp") == 4
    assert inputs.shape[0] == 4 * STEP

    at = lax.axis_index("mp")
    ends = (at == 0) | (at == 3)

    def of(*values):
        if not line:
            return jnp.int32(values[0])
        return sum(jnp.where(at == k, v, 0) for k, v in enumerate(values)).astype(jnp.int32)

    even = (lax.rem(lax.axis_index(("outer", "inner")), 2) == 0).astype(jnp.int32)
    plan = jnp.stack(
        [
            of(2, 0, 1, 0),
            of(3, 2, 3, 1),
            of(1, 3, 0, 2),
            of(0, 1, 2, 3),
            even,
            of(1, 0, 1, 0),
        ]
    )
    summed = totals(inputs, grad_out, log_decay, write_keys, read_keys)

    def first_window(other):
        ordered, _ = lax.optimization_barrier((log_decay, summed))
        return lax.optimization_barrier((other, factors(ordered)))

    def second_window(got, made):
        parts, rows, decays, ranges = made
        found = local(plan, inputs, grad_out, write_keys, read_keys, parts, rows, decays, ranges)
        return lax.optimization_barrier((got, (found, made)))

    given, made = carried_states(summed, states, first_window, second_window)
    (entries, afters, read_terms, write_terms, lead, tail), made = made
    states_at_ends, far, crossed = early_grads(plan, lead, tail, read_terms, write_terms, *given)

    def part(offset, steps, with_terms, earlier):
        return outputs(
            plan, offset, steps, with_terms, earlier, inputs, grad_out, write_keys, read_keys,
            (entries, afters, *made), states_at_ends, skip_gain[None],
        )

    if not line:
        *results, third, own = part(2, 2, True, ())
        results = part(0, 2, False, results)
        terms = jnp.concatenate([own, third, crossed, far], axis=0)
        own = lax.psum_scatter(terms, "mp", scatter_dimension=0, tiled=True)
        return *results, own[:, states:], own[:, :states]

    two_away = lax.ppermute(crossed, "mp", [(0, 2), (3, 1)])
    far_sum = lax.ppermute(far, "mp", [(0, 1), (1, 0), (2, 3), (3, 2)])
    middle = lax.ppermute(crossed, "mp", [(1, 2), (2, 1)])
    (*results, third, own), far_sum, two_away, middle = lax.optimization_barrier(
        (part(2, 2, True, ()), far_sum, two_away, middle)
    )
    came = jnp.where(ends, 0.0, far_sum)
    last = lax.ppermute(third + came, "mp", [(0, 1), (1, 3), (3, 2), (2, 0)])
    own = own + (far_sum - came) + middle + two_away
    results, own, last = lax.optimization_barrier((part(0, 2, False, results), own, last))
    total = own + last
    return *results, total[:, states:], total[:, :states]


def solution(mesh):
    tokens = ("outer", "inner")
    return jax.shard_map(
        on_device,
        mesh=mesh,
        in_specs=(
            P(tokens, "mp"),
            P("mp", tokens),
            P(tokens, None),
            P(tokens, None),
            P("mp"),
            P(tokens, "mp"),
        ),
        out_specs=(
            P(tokens, "mp"),
            P(tokens, "mp"),
            P(("outer", "inner", "mp"), None),
            P(("outer", "inner", "mp"), None),
        ),
        check_vma=False,
    )
```
